32 devices in a mesh: sp: 4 (over y, x), fsdp: 8 (over z, core).
Axes of the slice: x: 2, y: 2, z: 4, core: 2. Of those that a mesh axis runs over, the one named last changes fastest.
Arguments:
- layer_input: bfloat16 [8, 1024, 2048], P('fsdp', 'sp'), may hold values from -6 to 6
- positions: int32 [8, 1024], P('fsdp'), may hold values from 0 to 1023, as said below
- cotangent: bfloat16 [8, 1024, 2048], P('fsdp', 'sp'), may hold values from -6 to 6
- w_qkv: bfloat16 [2048, 1536], P('fsdp'), may hold values from -0.125 to 0.125
- w_out: bfloat16 [1024, 2048], P('fsdp'), may hold values from -1 to 1
- w_gate: bfloat16 [2048, 4096], P('fsdp'), may hold values from -0.125 to 0.125
- w_up: bfloat16 [2048, 4096], P('fsdp'), may hold values from -0.125 to 0.125
- w_down: bfloat16 [4096, 2048], P('fsdp'), may hold values from -0.09375 to 0.09375
- gain_attn: bfloat16 [2048], P('fsdp'), may hold values from 0.099609375 to 1.8984375
- gain_ffn: bfloat16 [2048], P('fsdp'), may hold values from 0.099609375 to 1.8984375
- gain_query: bfloat16 [64], replicated, may hold values from 1 to 2
- gain_key: bfloat16 [64], replicated, may hold values from 1 to 2
Outputs:
- out: bfloat16 [8, 1024, 2048], P('fsdp', 'sp')
- grad_input: float32 [8, 1024, 2048], P('fsdp', 'sp')
- grad_qkv: float32 [2048, 1536], P(('sp', 'fsdp'))
- grad_out: float32 [1024, 2048], P(('sp', 'fsdp'))
- grad_gate: float32 [2048, 4096], P(('sp', 'fsdp'))
- grad_up: float32 [2048, 4096], P(('sp', 'fsdp'))
- grad_down: float32 [4096, 2048], P(('sp', 'fsdp'))
- grad_gain_attn: float32 [2048], P(('sp', 'fsdp'))
- grad_gain_ffn: float32 [2048], P(('sp', 'fsdp'))
- grad_gain_query: float32 [64], replicated
- grad_gain_key: float32 [64], replicated
The draws below stay inside these ranges and needn't reach their ends.
Inputs may be any that keep to these rules, and one draw needn't show every extreme that they name: `positions`: in each sequence the first position is 0, and every later position is either 0 (a new document starts) or the previous position plus 1. The first sequence is a single document.
All inputs are finite; a program needn't handle non-finite values.
Results may differ from the reference program's by a relative error of at most 0.015.
The reference program's roundings to bfloat16 on the way count: a program that leaves them out, or rounds other values in their place, can miss the bound.
Values may be sent and summed in bfloat16 or wider, within the bound.
A program may use at most 320 MiB of HBM per device.

```python
import math
import jax
import jax.numpy as jnp
from jax import lax

D = 2048
FF = 4096
QUERY_HEAD_COUNT = 16
KEY_VALUE_HEADS = 4
HEAD_DIMENSION = 64
LENGTH = 1024
SEQS = 8
QKV = 1536
N_SP = 4


def draw_positions(key, part):
    starts = jax.random.randint(key, (SEQS, LENGTH), 0, LENGTH // 4) == 0
    index = jnp.broadcast_to(jnp.arange(LENGTH, dtype=jnp.int32)[None, :], (SEQS, LENGTH))
    row_index = jnp.broadcast_to(jnp.arange(SEQS, dtype=jnp.int32)[:, None], (SEQS, LENGTH))
    starts = starts & (row_index != 0)
    marks = jnp.where(starts | (index == 0), index, 0)
    latest = lax.cummax(marks, axis=1)
    return (index - latest).astype(jnp.int32)


def spiked(entries, rng, source, target, shards_of, factor):
    def block_of(axis_at):
        return (jnp.arange(entries.shape[axis_at]) // (entries.shape[axis_at] // shards_of)).reshape((-1,) + (1,) * (entries.ndim - 1 - axis_at))

    near = jax.random.permutation(rng, shards_of)[block_of(target)]
    second = (block_of(target) + shards_of // 2) % shards_of
    return jnp.where((block_of(source) == near) | (block_of(source) == second), factor * entries, entries)


def shard_levels(own_key, dims, split, low, top_value):
    loudness = 1.0
    for axis_at, blocks in split:
        draws = jax.random.uniform(jax.random.fold_in(jax.random.fold_in(own_key, 6), axis_at), (blocks,), jnp.float32, low / len(split), top_value / len(split))
        loudness = loudness * jnp.repeat(jnp.exp(draws), dims[axis_at] // blocks).reshape((-1,) + (1,) * (len(dims) - 1 - axis_at))
    return loudness


def bell_draw(key, dims, scale, bound, pieces=(), kind=jnp.bfloat16):
    entries = jax.random.normal(key, dims, jnp.float32) * scale
    if len(pieces) > 0:
        entries = shard_levels(key, dims, pieces, -0.22, 0.18) * entries
    return jnp.clip(entries, min=-bound, max=bound).astype(kind)


def noise_with(stream_key, extent, width, bound, shards, heavy, held_as=jnp.bfloat16):
    array = width * jax.random.normal(stream_key, extent, jnp.float32)
    if shards:
        array = array * shard_levels(stream_key, extent, shards, -0.22, 0.18)
    return jnp.clip(spiked(array, jax.random.fold_in(stream_key, 3), *heavy), -bound, bound).astype(held_as)


def setup_inputs(seed: int = 0) -> dict:
    key_of = jax.random.split(jax.random.key(seed), 13)
    return {
        "layer_input": noise_with(key_of[0], (SEQS, LENGTH, D), 1.0, 6.0, ((0, 8), (1, 4)), (0, 2, 8, 2.0)),
        "positions": draw_positions(jax.random.fold_in(key_of[12], 71), 0),
        "cotangent": bell_draw(key_of[2], (SEQS, LENGTH, D), 1.0, 6.0, ((0, 8), (1, 4))),
        "w_qkv": bell_draw(key_of[3], (D, QKV), D ** -0.5, 0.125, ((0, 8),)),
        "w_out": bell_draw(key_of[4], (QUERY_HEAD_COUNT * HEAD_DIMENSION, D), (QUERY_HEAD_COUNT * HEAD_DIMENSION // 32) ** -0.5, 1.0, ((0, 8),)),
        "w_gate": bell_draw(key_of[5], (D, FF), D ** -0.5, 0.125, ((0, 8),)),
        "w_up": bell_draw(key_of[6], (D, FF), D ** -0.5, 0.125, ((0, 8),)),
        "w_down": bell_draw(key_of[7], (FF, D), FF ** -0.5, 0.09375, ((0, 8),)),
        "gain_attn": jnp.clip(1.0 + 0.18 * jax.random.normal(key_of[8], (D,), jnp.float32), 0.099609375, 1.8984375).astype(jnp.bfloat16),
        "gain_ffn": jnp.clip(1.0 + 0.18 * jax.random.normal(key_of[9], (D,), jnp.float32), 0.099609375, 1.8984375).astype(jnp.bfloat16),
        "gain_query": jnp.clip(jnp.exp(jax.random.uniform(key_of[10], (HEAD_DIMENSION,), jnp.float32, math.log(1.0), math.log(2.0))), 1.0, 2.0).astype(jnp.bfloat16),
        "gain_key": jnp.clip(jnp.exp(jax.random.uniform(key_of[11], (HEAD_DIMENSION,), jnp.float32, math.log(1.0), math.log(2.0))), 1.0, 2.0).astype(jnp.bfloat16),
    }


@jax.custom_vjp
def low(v):
    return lax.optimization_barrier(v.astype(jnp.bfloat16)).astype(jnp.float32)

@jax.custom_vjp
def low_back(v):
    return v

def low_keep(v):
    return (low(v), None)

def low_pass(kept, grad):
    return (grad,)

def back_keep(v):
    return (v, None)

def back_low(kept, grad):
    return (low(grad),)
low.defvjp(low_keep, low_pass)
low_back.defvjp(back_keep, back_low)
epsilon = 1e-06
highest = lax.Precision.HIGHEST

def rms_scale(values, weight_gain):
    return values * lax.rsqrt(lax.optimization_barrier(jnp.mean(values * values, axis=-1, keepdims=True)) + epsilon) * weight_gain

def rope_tables(position_ids, head_size):
    half_dim = head_size // 2
    frequency = 10000.0 ** (-2.0 * jnp.arange(half_dim, dtype=jnp.float32) / head_size)
    angles = position_ids.astype(jnp.float32)[:, None, None] * frequency
    return (jnp.cos(angles), jnp.sin(angles))

def rotate(values, cosine, sine_part):
    half_dim = values.shape[-1] // 2
    front_part = values[..., :half_dim]
    back_part = values[..., half_dim:]
    return jnp.concatenate([front_part * cosine - back_part * sine_part, back_part * cosine + front_part * sine_part], axis=-1)

def head_prep(raw_heads, head_gain, cosine, sine_part):
    return rotate(rms_scale(raw_heads, head_gain), cosine, sine_part)

def layer_forward(inputs, position_ids, w_qkv, w_out, w_gate, w_up, w_down, gain_attn, gain_ffn, gain_query, gain_key):
    sequence_length = inputs.shape[0]
    head_copies = max(1, N_SP // KEY_VALUE_HEADS)
    normed = low(rms_scale(inputs, gain_attn))
    projected_rows = low_back(jnp.dot(normed, w_qkv, precision=highest))
    query_raw = projected_rows[:, :QUERY_HEAD_COUNT * HEAD_DIMENSION].reshape(sequence_length, QUERY_HEAD_COUNT, HEAD_DIMENSION)
    key_unrotated = projected_rows[:, QUERY_HEAD_COUNT * HEAD_DIMENSION:(QUERY_HEAD_COUNT + KEY_VALUE_HEADS) * HEAD_DIMENSION].reshape(sequence_length, KEY_VALUE_HEADS, HEAD_DIMENSION)
    value_unprojected = projected_rows[:, (QUERY_HEAD_COUNT + KEY_VALUE_HEADS) * HEAD_DIMENSION:].reshape(sequence_length, KEY_VALUE_HEADS, HEAD_DIMENSION)
    cosine, sine_part = rope_tables(position_ids, HEAD_DIMENSION)
    query_rows = low(low_back(head_prep(query_raw, gain_query, cosine, sine_part)))
    keys = low(low_back(jnp.repeat(head_prep(key_unrotated, gain_key, cosine, sine_part), head_copies, axis=1)))
    values = low(low_back(jnp.repeat(value_unprojected, head_copies, axis=1)))
    query_group_width = QUERY_HEAD_COUNT // (KEY_VALUE_HEADS * head_copies)
    grouped_queries = query_rows.reshape(sequence_length, KEY_VALUE_HEADS * head_copies, query_group_width, HEAD_DIMENSION)
    scores = low_back(jnp.einsum('qkgd,tkd->kgqt', grouped_queries, keys, precision=highest) * HEAD_DIMENSION ** (-0.5))
    index = jnp.arange(sequence_length, dtype=jnp.int32)
    allowed = (index[None, :] <= index[:, None]) & (index[:, None] - index[None, :] <= position_ids[:, None])
    masked = jnp.where(allowed, scores, -1e+30)
    largest = lax.optimization_barrier(jnp.max(masked, axis=-1, keepdims=True))
    exponent = jnp.exp(masked - largest)
    probabilities = low(exponent / lax.optimization_barrier(jnp.sum(exponent, axis=-1, keepdims=True)))
    mixture = jnp.einsum('kgqt,tkd->qkgd', probabilities, values, precision=highest)
    mixture = low(low_back(mixture.reshape(sequence_length, QUERY_HEAD_COUNT * HEAD_DIMENSION)))
    middle = inputs + low_back(jnp.dot(mixture, w_out, precision=highest))
    ffn_in = low(rms_scale(middle, gain_ffn))
    gate_value = low_back(jnp.dot(ffn_in, w_gate, precision=highest))
    up_value = low_back(jnp.dot(ffn_in, w_up, precision=highest))
    hidden = low(jax.nn.silu(gate_value) * up_value)
    return middle + jnp.dot(hidden, w_down, precision=highest)

def reference(layer_input, positions, cotangent, w_qkv, w_out, w_gate, w_up, w_down, gain_attn, gain_ffn, gain_query, gain_key):
    weights = tuple((weight.astype(jnp.float32) for weight in (w_qkv, w_out, w_gate, w_up, w_down, gain_attn, gain_ffn, gain_query, gain_key)))

    def one_sequence(totals, packed):
        inputs, position_ids, grad_seq = packed

        def forward_fn(inputs_f, *params):
            return layer_forward(inputs_f, position_ids, *params)
        result, pullback = jax.vjp(forward_fn, inputs.astype(jnp.float32), *weights)
        gradients = pullback(grad_seq.astype(jnp.float32))
        new_totals = tuple((total + grad_part for total, grad_part in zip(totals, gradients[1:])))
        return (new_totals, (result.astype(jnp.bfloat16), gradients[0]))
    zeros_init = tuple((jnp.zeros(weight.shape, jnp.float32) for weight in weights))
    totals, (output, grad_input) = lax.scan(one_sequence, zeros_init, (layer_input, positions, cotangent))
    return (output, grad_input, totals[0], totals[1], totals[2], totals[3], totals[4], totals[5], totals[6], totals[7], totals[8])
```

```python
import jax
import jax.numpy as jnp
from jax import lax
from jax.sharding import PartitionSpec as P

QUERY_HEADS = 16
KV_HEADS = 4
HD = 64
EPS = 1e-06
f32 = jnp.float32
bf16 = jnp.bfloat16


def rms_scale(values, gain):
    return values * lax.rsqrt(jnp.mean(values * values, axis=-1, keepdims=True) + EPS) * gain


def rope_tables(position_ids):
    half = HD // 2
    frequency = 10000.0 ** (-2.0 * jnp.arange(half, dtype=f32) / HD)
    angles = position_ids.astype(f32)[:, None, None] * frequency
    return jnp.cos(angles), jnp.sin(angles)


def rotate(values, cosine, sine):
    half = HD // 2
    front, back = values[..., :half], values[..., half:]
    return jnp.concatenate([front * cosine - back * sine, back * cosine + front * sine], axis=-1)


def over_rows(a, b):
    return lax.dot_general(a, b, (((0,), (0,)), ((), ())), preferred_element_type=f32)


def times_transposed(a, b):
    return lax.dot_general(a, b, (((1,), (1,)), ((), ())), preferred_element_type=f32)


def masked_scores(q, k, position_ids):
    length = q.shape[0]
    scores = jnp.einsum("qgd,td->gqt", q, k, preferred_element_type=f32) * HD ** (-0.5)
    qi = jnp.arange(length, dtype=jnp.int32)[:, None]
    ki = jnp.arange(length, dtype=jnp.int32)[None, :]
    allowed = (ki <= qi) & (qi - ki <= position_ids[:, None])
    return jnp.where(allowed, scores, -1e30), allowed


def attend(q, k, v, position_ids):
    masked, _ = masked_scores(q, k, position_ids)
    largest = jnp.max(masked, axis=-1, keepdims=True)
    exponent = jnp.exp(masked - largest)
    total = jnp.sum(exponent, axis=-1, keepdims=True)
    probs = (exponent / total).astype(bf16)
    mixture = jnp.einsum("gqt,td->qgd", probs, v, preferred_element_type=f32)
    return mixture.astype(bf16), (largest + jnp.log(total))[..., 0]


def attend_back(q, k, v, position_ids, grad_mixture, log_total):
    masked, allowed = masked_scores(q, k, position_ids)
    probs = jnp.exp(masked - log_total[..., None])
    grad_v = jnp.einsum("gqt,qgd->td", probs.astype(bf16), grad_mixture, preferred_element_type=f32)
    grad_p = jnp.einsum("qgd,td->gqt", grad_mixture, v, preferred_element_type=f32)
    inner = jnp.sum(grad_p * probs, axis=-1, keepdims=True)
    grad_s = jnp.where(allowed, probs * (grad_p - inner), 0.0).astype(bf16)
    scale = HD ** (-0.5)
    grad_q = jnp.einsum("gqt,td->qgd", grad_s, k, preferred_element_type=f32) * scale
    grad_k = jnp.einsum("gqt,qgd->td", grad_s, q, preferred_element_type=f32) * scale
    return grad_q.astype(bf16), grad_k.astype(bf16), grad_v.astype(bf16)


def swap(value, mask, count):
    return lax.ppermute(value, "sp", [(i, i ^ mask) for i in range(count)])


def gather_chunks(chunk, s, count):
    if count != 4:
        return lax.all_gather(chunk, "sp", axis=0)
    half = chunk.shape[0] // 2
    over_x = swap(chunk, 1, count)
    over_y = swap(chunk, 2, count)
    first = swap(over_x[:half], 2, count)
    second = swap(over_y[half:], 1, count)
    stack = jnp.zeros((count,) + chunk.shape, chunk.dtype)
    for mask, part in ((0, chunk), (1, over_x), (2, over_y)):
        stack = lax.dynamic_update_slice_in_dim(stack, part[None], s ^ mask, 0)
    across = jnp.concatenate([first, second], axis=0)
    return lax.dynamic_update_slice_in_dim(stack, across[None], s ^ 3, 0)


def scatter_sum(partial, s, count):
    rows = partial.shape[0] // count
    if count != 4:
        return lax.psum_scatter(partial.astype(bf16), "sp", scatter_dimension=0, tiled=True).astype(f32)
    half = rows // 2

    def part(mask):
        return lax.dynamic_slice_in_dim(partial, (s ^ mask) * rows, rows, 0)

    across = part(3).astype(bf16)
    from_y = swap(across[:half], 2, count)
    from_x = swap(across[half:], 1, count)
    to_x, to_y = part(1), part(2)
    to_x = jnp.concatenate([to_x[:half] + from_y.astype(f32), to_x[half:]], axis=0).astype(bf16)
    to_y = jnp.concatenate([to_y[:half], to_y[half:] + from_x.astype(f32)], axis=0).astype(bf16)
    return part(0) + swap(to_x, 1, count).astype(f32) + swap(to_y, 2, count).astype(f32)


def local(x_own, positions, ct_own, w_qkv, w_out, w_gate, w_up, w_down, gain_attn, gain_ffn, gain_query, gain_key):
    S, F = lax.axis_size("sp"), lax.axis_size("fsdp")
    s = lax.axis_index("sp")
    _, T, D = x_own.shape
    L = positions.shape[1]
    pos = positions[0]
    copies = max(1, S // KV_HEADS)
    QW = QUERY_HEADS * HD
    KW = KV_HEADS * HD
    heads = QUERY_HEADS // S
    qw = heads * HD
    FF = w_gate.shape[1]
    FFs = FF // S
    rows_d = D // (S * F)
    x_own = x_own[0]
    ct_own = ct_own[0]

    def cut(w, start, size, axis):
        return lax.dynamic_slice_in_dim(w, start, size, axis)

    def regroup(w):
        size = w.shape[0] // S
        perm = [(i * F + j, j * S + i) for i in range(S) for j in range(F)]
        return lax.ppermute(cut(w, s * size, size, 0), ("sp", "fsdp"), perm)

    def gather_z(w):
        return lax.all_gather(w, "fsdp", axis=0, tiled=True)

    gains = jnp.pad(jnp.stack([gain_attn, gain_ffn], axis=1), ((0, 0), (0, 126)))
    kv = s // copies
    attn_part = jnp.concatenate(
        [
            cut(w_qkv, s * qw, qw, 1),
            cut(w_qkv, QW + kv * HD, HD, 1),
            cut(w_qkv, QW + KW + kv * HD, HD, 1),
            gains,
        ],
        axis=1,
    )
    attn_full = gather_z(attn_part)
    hw = qw + 2 * HD
    wqkv_s = attn_full[:, :hw]
    g_attn = attn_full[:, hw].astype(f32)
    g_ffn = attn_full[:, hw + 1].astype(f32)
    wout_s = gather_z(regroup(w_out))
    gu_part = jnp.concatenate([cut(w_gate, s * FFs, FFs, 1), cut(w_up, s * FFs, FFs, 1)], axis=1)
    w_gu = gather_z(gu_part)
    w_dn = gather_z(regroup(w_down))

    x_bf = gather_chunks(x_own, s, S).reshape(L, D)
    x_all = x_bf.astype(f32)
    normed = rms_scale(x_all, g_attn).astype(bf16)
    projected = jnp.dot(normed, wqkv_s, preferred_element_type=f32)
    cosine, sine = rope_tables(pos)

    def prep(raw, gain):
        return rotate(rms_scale(raw, gain), cosine, sine)

    q_rot, q_pull = jax.vjp(prep, projected[:, :qw].reshape(L, heads, HD), gain_query.astype(f32))
    k_rot, k_pull = jax.vjp(prep, projected[:, qw : qw + HD].reshape(L, 1, HD), gain_key.astype(f32))
    q = q_rot.astype(bf16)
    k = k_rot.astype(bf16)[:, 0]
    v = projected[:, qw + HD :].astype(bf16)
    mixture, log_total = attend(q, k, v, pos)
    mix_s = mixture.reshape(L, qw)
    mix_all = jnp.swapaxes(gather_chunks(mix_s, s, S), 0, 1).reshape(L, QW)
    wout_full = gather_chunks(wout_s, s, S).reshape(QW, D)
    middle = x_all + jnp.dot(mix_all, wout_full, preferred_element_type=f32)
    ffn_in = rms_scale(middle, g_ffn).astype(bf16)
    gu = jnp.dot(ffn_in, w_gu, preferred_element_type=f32)

    def gated(g, u):
        return jax.nn.silu(g) * u

    hidden_val, hidden_pull = jax.vjp(gated, gu[:, :FFs], gu[:, FFs:])
    hidden = hidden_val.astype(bf16)
    ct_all = gather_chunks(ct_own, s, S).reshape(L, D)
    grad_down = over_rows(hidden, ct_all).astype(bf16)
    grad_down = lax.psum_scatter(grad_down, "fsdp", scatter_dimension=0, tiled=True).astype(f32)

    grad_hidden = times_transposed(ct_all, w_dn)
    d_gate, d_up = hidden_pull(grad_hidden)
    d_gu = jnp.concatenate([d_gate.astype(bf16), d_up.astype(bf16)], axis=1)

    def share_rows(grad):
        width = grad.shape[1]
        grad = grad.astype(bf16).reshape(S, F, rows_d, width)
        grad = jnp.swapaxes(grad, 0, 1).reshape(D, width)
        mine = lax.psum_scatter(grad, "fsdp", scatter_dimension=0, tiled=True)
        mine = mine.reshape(S, rows_d, width)
        return lax.all_to_all(mine, "sp", split_axis=0, concat_axis=0)

    grad_gu = share_rows(over_rows(ffn_in, d_gu))
    grad_gate = jnp.swapaxes(grad_gu[:, :, :FFs], 0, 1).reshape(rows_d, FF).astype(f32)
    grad_up = jnp.swapaxes(grad_gu[:, :, FFs:], 0, 1).reshape(rows_d, FF).astype(f32)

    grad_ffn_in = scatter_sum(times_transposed(d_gu, w_gu), s, S)
    out_sum = scatter_sum(jnp.dot(hidden, w_dn, preferred_element_type=f32), s, S)
    middle_own = cut(middle, s * T, T, 0)
    out = (middle_own + out_sum).astype(bf16)
    _, ffn_pull = jax.vjp(rms_scale, middle_own, g_ffn)
    grad_middle, grad_g_ffn = ffn_pull(grad_ffn_in)
    grad_middle = ct_own.astype(f32) + grad_middle
    d_attn = grad_middle.astype(bf16)

    d_mix_tok = times_transposed(d_attn, wout_full).astype(bf16).reshape(T, S, qw)
    d_mix = lax.all_to_all(jnp.swapaxes(d_mix_tok, 0, 1), "sp", split_axis=0, concat_axis=0)
    d_mix = d_mix.reshape(L, heads, HD)
    d_attn_all = gather_chunks(d_attn, s, S).reshape(L, D)
    grad_out = over_rows(mix_s, d_attn_all).astype(bf16)
    grad_out = lax.psum_scatter(grad_out, "fsdp", scatter_dimension=0, tiled=True).astype(f32)

    dq, dk, dv = attend_back(q, k, v, pos, d_mix, log_total)
    dk, dv = dk.astype(f32), dv.astype(f32)
    if copies > 1:
        groups = [[i * copies + j for j in range(copies)] for i in range(KV_HEADS)]
        dk, dv = lax.psum((dk, dv), "sp", axis_index_groups=groups)
        first = (s % copies == 0).astype(f32)
        dk, dv = dk * first, dv * first
    d_q_raw, grad_g_query = q_pull(dq.astype(f32))
    d_k_raw, grad_g_key = k_pull(dk[:, None])
    d_proj = jnp.concatenate([d_q_raw.reshape(L, qw), d_k_raw[:, 0], dv], axis=1).astype(bf16)

    grad_qkv = share_rows(over_rows(normed, d_proj))
    grad_q = jnp.swapaxes(grad_qkv[:, :, :qw], 0, 1).reshape(rows_d, QW)
    grad_k = jnp.swapaxes(grad_qkv[::copies, :, qw : qw + HD], 0, 1).reshape(rows_d, KW)
    grad_v = jnp.swapaxes(grad_qkv[::copies, :, qw + HD :], 0, 1).reshape(rows_d, KW)
    grad_qkv = jnp.concatenate([grad_q, grad_k, grad_v], axis=1).astype(f32)

    d_proj_own = lax.all_to_all(d_proj.reshape(S, T, hw), "sp", split_axis=0, concat_axis=0)
    wqkv_all = gather_chunks(wqkv_s, s, S)
    grad_normed = jnp.einsum("stc,sdc->td", d_proj_own, wqkv_all, preferred_element_type=f32)
    _, attn_pull = jax.vjp(rms_scale, x_own.astype(f32), g_attn)
    grad_x, grad_g_attn = attn_pull(grad_normed)
    grad_input = grad_middle + grad_x

    tiny = jnp.concatenate([grad_g_attn, grad_g_ffn, grad_g_query, grad_g_key])
    tiny = lax.psum(tiny, ("sp", "fsdp"))
    mine = (s * F + lax.axis_index("fsdp")) * rows_d
    return (
        out[None],
        grad_input[None],
        grad_qkv,
        grad_out,
        grad_gate,
        grad_up,
        grad_down,
        lax.dynamic_slice_in_dim(tiny[:D], mine, rows_d, 0),
        lax.dynamic_slice_in_dim(tiny[D : 2 * D], mine, rows_d, 0),
        tiny[2 * D : 2 * D + HD],
        tiny[2 * D + HD :],
    )


def solution(mesh):
    row = P("fsdp", "sp", None)
    shard = P("fsdp", None)
    grad = P(("sp", "fsdp"), None)
    return jax.shard_map(
        local,
        mesh=mesh,
        in_specs=(row, shard, row, shard, shard, shard, shard, shard, P("fsdp"), P("fsdp"), P(), P()),
        out_specs=(row, row, grad, grad, grad, grad, grad, P(("sp", "fsdp")), P(("sp", "fsdp")), P(), P()),
        check_vma=False,
    )
```

```python
import functools

import jax
import jax.numpy as jnp
from jax import lax
from jax.experimental import pallas as pl
from jax.experimental.pallas import tpu as pltpu
from jax.sharding import PartitionSpec as P

QUERY_HEADS = 16
KV_HEADS = 4
HD = 64
EPS = 1e-06
BLOCK = 256
VMEM_LIMIT = 60 << 20
MESH = pl.DeviceIdType.MESH
f32 = jnp.float32
bf16 = jnp.bfloat16


def params(collective=None, grid=0):
    return pltpu.CompilerParams(
        dimension_semantics=("arbitrary",) * grid if grid else None,
        vmem_limit_bytes=VMEM_LIMIT,
        collective_id=collective,
        has_side_effects=collective is not None,
    )


def cost(micros):
    return pl.CostEstimate(flops=0, bytes_accessed=int(micros * 3_600_000), transcendentals=0)


ANY = pl.BlockSpec(memory_space=pl.ANY)
VMEM = pl.BlockSpec(memory_space=pltpu.VMEM)
DMA = pltpu.SemaphoreType.DMA


def shape(dims, dtype=bf16):
    return jax.ShapeDtypeStruct(dims, dtype)


def dot(a, b):
    return jnp.dot(a, b, preferred_element_type=f32)


def dot_nt(a, b):
    return lax.dot_general(a, b, (((1,), (1,)), ((), ())), preferred_element_type=f32)


def greet(S, sibling):
    s, f = lax.axis_index("sp"), lax.axis_index("fsdp")
    barrier = pltpu.get_barrier_semaphore()
    for k in range(1, S):
        pl.semaphore_signal(barrier, inc=1, device_id={"sp": lax.rem(s + k, S)}, device_id_type=MESH)
    if sibling:
        pl.semaphore_signal(barrier, inc=1, device_id={"fsdp": f + 1 - 2 * lax.rem(f, 2)}, device_id_type=MESH)
    pl.semaphore_wait(barrier, S - 1 + int(sibling))


def to_peer(src, dst, send, recv, k, S):
    s = lax.axis_index("sp")
    return pltpu.make_async_remote_copy(
        src_ref=src, dst_ref=dst, send_sem=send, recv_sem=recv, device_id={"sp": lax.rem(s + k, S)}, device_id_type=MESH
    )


def mates(s):
    return s + 1 - 2 * lax.rem(s, 2), lax.rem(s + 2, 4), 3 - s


def push(src, dst, send, recv, where):
    return pltpu.make_async_remote_copy(
        src_ref=src, dst_ref=dst, send_sem=send, recv_sem=recv, device_id=where, device_id_type=MESH
    )


class Gather:
    def __init__(self, S, src, dst, sems, halves=False, inner=False):
        self.S, self.src, self.halves = S, src, halves
        self.slot = (lambda j: dst.at[:, j]) if inner else (lambda j: dst.at[j])
        self.send, self.recv, self.own, self.stage = sems[:4]
        self.swap_send, self.swap_recv = sems[4:] if halves else (None, None)
        self.s, self.f = lax.axis_index("sp"), lax.axis_index("fsdp")
        self.rows = src.shape[0] // (2 if halves else 1)
        self.size = self.rows // 2 if S == 4 else self.rows

    @staticmethod
    def sems(S, chunk, halves=False):
        count = 6 if S == 4 else S - 1
        base = [DMA((count,)), DMA((count,)), DMA((2,)), pltpu.VMEM(chunk.shape, chunk.dtype)]
        return base + [DMA((S - 1,)), DMA((S - 1,))] if halves else base

    def base(self, mine=True):
        if not self.halves:
            return 0
        core = lax.rem(self.f, 2)
        return (core if mine else 1 - core) * self.rows

    def piece(self, ref, n):
        return ref.at[pl.ds(self.base() + n * self.size, self.size)]

    def share(self, slot, mine):
        if not self.halves:
            return self.slot(slot)
        return self.slot(slot).at[pl.ds(self.base(mine), self.rows)]

    def steps(self):
        s, S = self.s, self.S
        if S != 4:
            return [(self.src, s, lax.rem(s + S - k, S), 0, lax.rem(s + k, S)) for k in range(1, S)]
        x, y, d = mates(s)
        return [
            (self.src, s, x, 0, x),
            (self.src, s, y, 1, y),
            (self.src, s, x, 1, x),
            (self.src, s, y, 0, y),
            (self.slot(x), x, d, 0, y),
            (self.slot(y), y, d, 1, x),
        ]

    def copy(self, n, here):
        src, there, lands, piece, target = self.steps()[n]
        slot = lands if here else there
        return push(
            self.piece(src, piece), self.piece(self.slot(slot), piece), self.send.at[n], self.recv.at[n], {"sp": target}
        )

    def passing(self, n, mine):
        slots = mates(self.s) if self.S == 4 else [lax.rem(self.s + self.S - k, self.S) for k in range(1, self.S)]
        sibling = {"fsdp": self.f + 1 - 2 * lax.rem(self.f, 2)}
        return push(
            self.share(slots[n], True), self.share(slots[n], mine), self.swap_send.at[n], self.swap_recv.at[n], sibling
        )

    def local(self, out):
        if out:
            return pltpu.make_async_copy(self.stage, self.slot(self.s), self.own.at[1])
        return pltpu.make_async_copy(self.src, self.stage, self.own.at[0])

    def start(self):
        for n in range(4 if self.S == 4 else self.S - 1):
            self.copy(n, False).start()
        self.local(False).start()

    def finish(self):
        self.local(False).wait()
        self.local(True).start()
        waits = {0: 4, 1: 5} if self.S == 4 else {}
        ready = {2: 0, 3: 1, 5: 2} if self.S == 4 else {n: n for n in range(self.S - 1)}
        for n in range(len(self.steps())):
            self.copy(n, True).wait_recv()
            if n in waits:
                self.copy(waits[n], False).start()
            if self.halves and n in ready:
                self.passing(ready[n], True).start()
        self.local(True).wait()
        for n in range(len(self.steps())):
            self.copy(n, False).wait_send()
        if self.halves:
            for n in range(self.S - 1):
                self.passing(n, True).wait_send()
                self.passing(n, False).wait_recv()


def gather_kernel(S, src, dst, *sems):
    greet(S, False)
    move = Gather(S, src, dst, sems)
    move.start()
    move.finish()


def gather_sp(S, x, collective):
    return pl.pallas_call(
        functools.partial(gather_kernel, S),
        in_specs=[ANY],
        out_specs=ANY,
        out_shape=shape((S,) + x.shape, x.dtype),
        scratch_shapes=Gather.sems(S, x),
        compiler_params=params(collective),
        cost_estimate=cost(45),
    )(x)


def forward_kernel(S, heads, x_ref, g_ref, w_ref, pos_ref, cos_ref, sin_ref, gq_ref, gk_ref, wout_ref, normed_t_ref, raw_ref, rot_ref, lse_ref, mix_t_ref, mix_all, wout_all, k_buf, vt_buf, mix_buf, mix_send, mix_recv, mix_own, *sems):
    i = pl.program_id(0)
    s = lax.axis_index("sp")
    qw = heads * HD
    half = HD // 2
    move = Gather(S, wout_ref, wout_all, sems, halves=True, inner=True)

    @pl.when(i == 0)
    def _():
        greet(S, True)
        move.start()

    x = x_ref[...].astype(f32)
    scale = lax.rsqrt(jnp.mean(x * x, axis=-1, keepdims=True) + EPS)
    scaled = x * scale * g_ref[...]
    normed = scaled.astype(bf16)
    normed_t_ref[...] = scaled.T.astype(bf16)
    raw = dot(normed, w_ref[...]).T
    raw_ref[...] = raw
    cosine, sine = cos_ref[...], sin_ref[...]

    def prep(u, gain):
        n = u * lax.rsqrt(jnp.mean(u * u, axis=0, keepdims=True) + EPS) * gain
        front, back = n[:half], n[half:]
        return jnp.concatenate([front * cosine - back * sine, back * cosine + front * sine], axis=0)

    q = [prep(raw[h * HD : (h + 1) * HD], gq_ref[...]).astype(bf16) for h in range(heads)]
    kt = prep(raw[qw : qw + HD], gk_ref[...])
    vt = raw[qw + HD :].astype(bf16)
    rot_ref[...] = jnp.concatenate(q + [kt.astype(bf16), vt], axis=0)
    blocks = pl.num_programs(0)
    steps = mix_buf.shape[0]

    x_mate, y_mate, d_mate = mates(s)

    def mix_copy(block, k, here):
        rows = pl.ds(block * BLOCK, BLOCK)
        n = block * (S - 1) + k - 1
        if S != 4:
            slot = lax.rem(s + S - k, S) if here else s
            return push(mix_buf.at[block], mix_all.at[slot, rows], mix_send.at[n], mix_recv.at[n], {"sp": lax.rem(s + k, S)})
        if k < 3:
            mate = x_mate if k == 1 else y_mate
            slot = mate if here else s
            return push(mix_buf.at[block], mix_all.at[slot, rows], mix_send.at[n], mix_recv.at[n], {"sp": mate})
        source, mate = (x_mate, y_mate) if block < steps // 2 else (y_mate, x_mate)
        slot = d_mate if here else source
        return push(mix_all.at[source, rows], mix_all.at[slot, rows], mix_send.at[n], mix_recv.at[n], {"sp": mate})

    def mix_local(block):
        return pltpu.make_async_copy(mix_buf.at[block], mix_all.at[s, pl.ds(block * BLOCK, BLOCK)], mix_own.at[block])

    for step in range(steps):

        @pl.when(i == step)
        def _():
            n = (step + 1) * BLOCK
            k_buf[step * BLOCK : n, :] = kt.T.astype(bf16)
            vt_buf[:, step * BLOCK : n] = vt
            col = lax.broadcasted_iota(jnp.int32, (n, BLOCK), 0)
            row = step * BLOCK + lax.broadcasted_iota(jnp.int32, (n, BLOCK), 1)
            bias = jnp.where((col <= row) & (row - col <= pos_ref[...]), 0.0, -1e30)
            keys, values = k_buf[:n, :], vt_buf[:, :n]
            mixes, lses = [], []
            for h in range(heads):
                e = jnp.exp(dot(keys, q[h] * 0.125) + bias)
                total = jnp.sum(e, axis=0, keepdims=True)
                p = (e * (1.0 / total)).astype(bf16)
                mixes.append(dot(values, p))
                lses.append(jnp.log(total))
            mix = jnp.concatenate(mixes, axis=0)
            mix_t_ref[...] = mix.astype(bf16)
            lse_ref[...] = jnp.concatenate(lses + [jnp.zeros((8 - heads, BLOCK), f32)], axis=0)
            mix_buf[step] = mix.T.astype(bf16)
            for k in range(1, 3 if S == 4 else S):
                mix_copy(step, k, False).start()
            mix_local(step).start()

    @pl.when(i == blocks - 1)
    def _():
        for block in range(steps):
            for k in range(1, 3 if S == 4 else S):
                mix_copy(block, k, True).wait_recv()
                if S == 4 and k == (1 if block < steps // 2 else 2):
                    mix_copy(block, 3, False).start()
        for block in range(steps):
            if S == 4:
                mix_copy(block, 3, True).wait_recv()
            for k in range(1, S):
                mix_copy(block, k, False).wait_send()
            mix_local(block).wait()
        move.finish()


def forward_attention(S, x, gain, w, pos, cosine, sine, gain_q, gain_k, wout, heads, collective):
    length, width = x.shape
    hw = w.shape[1]
    qw = heads * HD
    steps = length // BLOCK
    full = lambda i: (0, 0)
    rows = lambda i: (i, 0)
    cols = lambda i: (0, i)
    return pl.pallas_call(
        functools.partial(forward_kernel, S, heads),
        grid=(steps,),
        in_specs=[
            pl.BlockSpec((BLOCK, width), rows),
            pl.BlockSpec((1, width), full),
            pl.BlockSpec((width, hw), full),
            pl.BlockSpec((1, BLOCK), cols),
            pl.BlockSpec((HD // 2, BLOCK), cols),
            pl.BlockSpec((HD // 2, BLOCK), cols),
            pl.BlockSpec((HD, 1), full),
            pl.BlockSpec((HD, 1), full),
            ANY,
        ],
        out_specs=[
            pl.BlockSpec((width, BLOCK), cols),
            pl.BlockSpec((hw, BLOCK), cols),
            pl.BlockSpec((hw, BLOCK), cols),
            pl.BlockSpec((8, BLOCK), cols),
            pl.BlockSpec((qw, BLOCK), cols),
            ANY,
            ANY,
        ],
        out_shape=[
            shape((width, length)),
            shape((hw, length), f32),
            shape((hw, length)),
            shape((8, length), f32),
            shape((qw, length)),
            shape((S, length, qw)),
            shape((wout.shape[0], S) + wout.shape[1:]),
        ],
        scratch_shapes=[
            pltpu.VMEM((length, HD), bf16),
            pltpu.VMEM((HD, length), bf16),
            pltpu.VMEM((steps, BLOCK, qw), bf16),
            DMA((steps * (S - 1),)),
            DMA((steps * (S - 1),)),
            DMA((steps,)),
        ]
        + Gather.sems(S, wout, True),
        compiler_params=params(collective, 1),
        cost_estimate=cost(45),
    )(x, gain, w, pos, cosine, sine, gain_q, gain_k, wout)


def middle_kernel(S, T, x_ref, mix_ref, wout_ref, g_ref, ct_ref, mid_ref, ffn_ref, ffn_t_ref, ct_all, *sems):
    i = pl.program_id(0)
    s = lax.axis_index("sp")
    move = Gather(S, ct_ref, ct_all, sems)

    @pl.when(i == 0)
    def _():
        greet(S, False)
        move.start()

    middle = x_ref[...].astype(f32)
    total = dot(mix_ref[0], wout_ref[0])
    for j in range(1, S):
        total += dot(mix_ref[j], wout_ref[j])
    middle = middle + total

    @pl.when(i == s)
    def _():
        mid_ref[...] = middle

    scaled = middle * lax.rsqrt(jnp.mean(middle * middle, axis=-1, keepdims=True) + EPS) * g_ref[...]
    ffn_ref[...] = scaled.astype(bf16)
    ffn_t_ref[...] = scaled.T.astype(bf16)

    @pl.when(i == pl.num_programs(0) - 1)
    def _():
        move.finish()


def middle_rows(S, x, mix_all, wout_all, gain, ct, collective):
    length, width = x.shape
    T = length // S
    qw = mix_all.shape[2]
    return pl.pallas_call(
        functools.partial(middle_kernel, S, T),
        grid=(S,),
        in_specs=[
            pl.BlockSpec((T, width), lambda i: (i, 0)),
            pl.BlockSpec((S, T, qw), lambda i: (0, i, 0)),
            pl.BlockSpec((S, qw, width), lambda i: (0, 0, 0)),
            pl.BlockSpec((1, width), lambda i: (0, 0)),
            ANY,
        ],
        out_specs=[
            pl.BlockSpec((T, width), lambda i: (0, 0)),
            pl.BlockSpec((T, width), lambda i: (i, 0)),
            pl.BlockSpec((width, T), lambda i: (0, i)),
            ANY,
        ],
        out_shape=[shape((T, width), f32), shape((length, width)), shape((width, length)), shape((S, T, width))],
        scratch_shapes=Gather.sems(S, ct),
        compiler_params=params(collective, 1),
        cost_estimate=cost(45),
    )(x, mix_all, wout_all, gain, ct)


def ffn_kernel(S, ffn_ref, ct_ref, wg_ref, wu_ref, wqkv_ref, gate_ref, up_ref, hid_ref, down_ref, wqkv_all, *sems):
    i = pl.program_id(0)
    move = Gather(S, wqkv_ref, wqkv_all, sems, halves=True)

    @pl.when(i == 0)
    def _():
        greet(S, True)
        move.start()

    rows = ffn_ref[...]
    gate, up = dot(rows, wg_ref[...]), dot(rows, wu_ref[...])
    gate_ref[...] = gate
    up_ref[...] = up
    hidden = gate / (1.0 + jnp.exp(-gate)) * up
    hid_ref[...] = hidden.astype(bf16)
    down_ref[...] = dot(hidden.T.astype(bf16), ct_ref[...]).astype(bf16)

    @pl.when(i == pl.num_programs(0) - 1)
    def _():
        move.finish()


def ffn_forward(S, ffn_in, ct_all, w_gu, wqkv_s, collective):
    length, width = ffn_in.shape
    FFs = w_gu.shape[1] // 2
    tiles = FFs // BLOCK
    whole = lambda i: (0, 0)
    return pl.pallas_call(
        functools.partial(ffn_kernel, S),
        grid=(tiles,),
        in_specs=[
            pl.BlockSpec((length, width), whole),
            pl.BlockSpec((length, width), whole),
            pl.BlockSpec((width, BLOCK), lambda i: (0, i)),
            pl.BlockSpec((width, BLOCK), lambda i: (0, tiles + i)),
            ANY,
        ],
        out_specs=[
            pl.BlockSpec((length, BLOCK), lambda i: (0, i)),
            pl.BlockSpec((length, BLOCK), lambda i: (0, i)),
            pl.BlockSpec((length, BLOCK), lambda i: (0, i)),
            pl.BlockSpec((BLOCK, width), lambda i: (i, 0)),
            ANY,
        ],
        out_shape=[
            shape((length, FFs), f32),
            shape((length, FFs), f32),
            shape((length, FFs)),
            shape((FFs, width)),
            shape((S,) + wqkv_s.shape),
        ],
        scratch_shapes=Gather.sems(S, wqkv_s, True),
        compiler_params=params(collective, 1),
        cost_estimate=cost(20),
    )(ffn_in, ct_all, w_gu, w_gu, wqkv_s)


def ffn_back_kernel(S, F, ct_ref, wd_ref, gate_ref, up_ref, ffn_t_ref, dgu_ref, pgu_ref):
    gh = dot_nt(ct_ref[...], wd_ref[...])
    gate, up = gate_ref[...], up_ref[...]
    sig = 1.0 / (1.0 + jnp.exp(-gate))
    d_gate = (gh * up * sig * (1.0 + gate * (1.0 - sig))).astype(bf16)
    d_up = (gh * (gate * sig)).astype(bf16)
    dgu_ref[0] = d_gate
    dgu_ref[1] = d_up
    ffn_t = ffn_t_ref[...]
    rows = pgu_ref.shape[3]
    for n, d in enumerate((d_gate, d_up)):
        part = dot(ffn_t, d).astype(bf16)
        for j in range(S):
            for m in range(F):
                pgu_ref[m, j, n] = part[(j * F + m) * rows : (j * F + m + 1) * rows]


def ffn_backward(S, F, ct_all, w_dn, gate, up, ffn_t):
    length, FFs = gate.shape
    width = ct_all.shape[1]
    tiles = FFs // BLOCK
    rows = width // (S * F)
    whole = lambda i: (0, 0)
    col = lambda i: (0, i)
    return pl.pallas_call(
        functools.partial(ffn_back_kernel, S, F),
        grid=(tiles,),
        in_specs=[
            pl.BlockSpec((length, width), whole),
            pl.BlockSpec((BLOCK, width), lambda i: (i, 0)),
            pl.BlockSpec((length, BLOCK), col),
            pl.BlockSpec((length, BLOCK), col),
            pl.BlockSpec((width, length), whole),
        ],
        out_specs=[
            pl.BlockSpec((2, length, BLOCK), lambda i: (0, 0, i)),
            pl.BlockSpec((F, S, 2, rows, BLOCK), lambda i: (0, 0, 0, 0, i)),
        ],
        out_shape=[shape((2, length, FFs)), shape((F, S, 2, rows, FFs))],
        compiler_params=params(None, 1),
        cost_estimate=cost(1),
    )(ct_all, w_dn, gate, up, ffn_t)


def sum_over_sp(S, compute, acc, send_buf, recv_buf, send, recv):
    s = lax.axis_index("sp")
    if S != 4:

        def copy(k):
            return push(
                send_buf.at[k - 1], recv_buf.at[k - 1], send.at[k - 1], recv.at[k - 1], {"sp": lax.rem(s + k, S)}
            )

        for k in range(1, S):
            compute(lax.rem(s + k, S), send_buf.at[k - 1])
            copy(k).start()
        compute(s, acc)
        for k in range(1, S):
            copy(k).wait_recv()
            acc[...] += recv_buf[k - 1].astype(f32)
        return [copy(k) for k in range(1, S)]

    x, y, d = mates(s)
    half = acc.shape[0] // 2
    low, high = pl.ds(0, half), pl.ds(half, half)

    def copy(n):
        buf, rows, target = [(0, low, y), (0, high, x), (1, high, x), (2, low, y), (1, low, x), (2, high, y)][n]
        return push(send_buf.at[buf, rows], recv_buf.at[buf, rows], send.at[n], recv.at[n], {"sp": target})

    compute(d, send_buf.at[0])
    copy(0).start()
    copy(1).start()
    compute(x, send_buf.at[1])
    copy(2).start()
    compute(y, send_buf.at[2])
    copy(3).start()
    copy(0).wait_recv()
    send_buf[1, :half] = (send_buf[1, :half].astype(f32) + recv_buf[0, :half].astype(f32)).astype(bf16)
    copy(4).start()
    copy(1).wait_recv()
    send_buf[2, half:] = (send_buf[2, half:].astype(f32) + recv_buf[0, half:].astype(f32)).astype(bf16)
    copy(5).start()
    compute(s, acc)
    for n in range(2, 6):
        copy(n).wait_recv()
    acc[...] += recv_buf[1].astype(f32) + recv_buf[2].astype(f32)
    return [copy(n) for n in range(6)]


def middle_back_kernel(S, dgu_ref, wgu_ref, wout_ref, mid_ref, g_ref, ct_ref, gm_ref, dattn_ref, gg_ref, dmix_ref, acc, send_buf, recv_buf, mix_buf, send, recv, mix_send, mix_recv, mix_own):
    s = lax.axis_index("sp")
    T, width = mid_ref.shape
    FFs = dgu_ref.shape[2]
    tile = 512
    greet(S, False)

    def compute(chunk, out):
        rows = pl.ds(pl.multiple_of(chunk * T, T), T)
        d_gate, d_up = dgu_ref[0, rows, :], dgu_ref[1, rows, :]
        for c in range(0, width, tile):
            part = dot_nt(d_gate, wgu_ref[c : c + tile, :FFs]) + dot_nt(d_up, wgu_ref[c : c + tile, FFs:])
            out[:, c : c + tile] = part.astype(out.dtype)

    copies = sum_over_sp(S, compute, acc, send_buf, recv_buf, send, recv)
    v, e = mid_ref[...], acc[...]
    r = lax.rsqrt(jnp.mean(v * v, axis=-1, keepdims=True) + EPS)
    gg_ref[...] = jnp.sum(e * v * r, axis=0, keepdims=True)
    ge = g_ref[...] * e
    gm = ct_ref[...].astype(f32) + r * ge - v * (r * r * r * jnp.mean(ge * v, axis=-1, keepdims=True))
    gm_ref[...] = gm
    d_attn = gm.astype(bf16)
    dattn_ref[...] = d_attn

    def mix_copy(k, slot):
        rows = pl.ds(pl.multiple_of(slot * T, T), T)
        return to_peer(mix_buf.at[k], dmix_ref.at[rows], mix_send.at[k - 1], mix_recv.at[k - 1], k, S)

    for k in range(1, S):
        mix_buf[k] = dot_nt(d_attn, wout_ref[lax.rem(s + k, S)]).astype(bf16)
        mix_copy(k, s).start()
    mix_buf[0] = dot_nt(d_attn, wout_ref[s]).astype(bf16)
    own = pltpu.make_async_copy(mix_buf.at[0], dmix_ref.at[pl.ds(pl.multiple_of(s * T, T), T)], mix_own)
    own.start()
    for copy in copies:
        copy.wait_send()
    for k in range(1, S):
        mix_copy(k, s).wait_send()
        mix_copy(k, lax.rem(s + S - k, S)).wait_recv()
    own.wait()


def middle_back(S, dgu, w_gu, wout_all, mid, gain, ct, collective):
    T, width = mid.shape
    qw = wout_all.shape[1]
    return pl.pallas_call(
        functools.partial(middle_back_kernel, S),
        in_specs=[VMEM] * 6,
        out_specs=[VMEM, VMEM, VMEM, ANY],
        out_shape=[shape((T, width), f32), shape((T, width)), shape((1, width), f32), shape((S * T, qw))],
        scratch_shapes=[
            pltpu.VMEM((T, width), f32),
            pltpu.VMEM((S - 1, T, width), bf16),
            pltpu.VMEM((S - 1, T, width), bf16),
            pltpu.VMEM((S, T, qw), bf16),
            DMA((max(6, S - 1),)),
            DMA((max(6, S - 1),)),
            DMA((S - 1,)),
            DMA((S - 1,)),
            DMA,
        ],
        compiler_params=params(collective),
        cost_estimate=cost(1),
    )(dgu, w_gu, wout_all, mid, gain, ct)


def attn_back_kernel(S, heads, dmix_ref, rot_ref, raw_ref, lse_ref, pos_ref, cos_ref, sin_ref, gq_ref, gk_ref, dattn_ref, dproj_ref, gg_ref, dattn_all, k_buf, v_buf, dk_acc, dv_acc, *sems):
    i = pl.program_id(0)
    qw = heads * HD
    half = HD // 2
    length = rot_ref.shape[1]
    move = Gather(S, dattn_ref, dattn_all, sems)

    @pl.when(i == 0)
    def _():
        greet(S, False)
        move.start()
        k_buf[...] = rot_ref[qw : qw + HD, :].astype(f32).T.astype(bf16)
        v_buf[...] = rot_ref[qw + HD :, :].astype(f32).T.astype(bf16)
        dk_acc[...] = jnp.zeros_like(dk_acc)
        dv_acc[...] = jnp.zeros_like(dv_acc)
        gg_ref[...] = jnp.zeros_like(gg_ref)

    def unprep(e, u, gain, cosine, sine):
        front, back = e[:half], e[half:]
        e = jnp.concatenate([front * cosine + back * sine, back * cosine - front * sine], axis=0)
        r = lax.rsqrt(jnp.mean(u * u, axis=0, keepdims=True) + EPS)
        ge = gain * e
        du = r * ge - u * (r * r * r * jnp.mean(ge * u, axis=0, keepdims=True))
        return du, jnp.sum(e * u * r, axis=1, keepdims=True)

    for step in range(length // BLOCK):

        @pl.when(i == step)
        def _():
            n = (step + 1) * BLOCK
            here = slice(step * BLOCK, n)
            col = lax.broadcasted_iota(jnp.int32, (n, BLOCK), 0)
            row = step * BLOCK + lax.broadcasted_iota(jnp.int32, (n, BLOCK), 1)
            bias = jnp.where((col <= row) & (row - col <= pos_ref[:, here]), 0.0, -1e30)
            keys, values = k_buf[:n, :], v_buf[:n, :]
            kt = rot_ref[qw : qw + HD, :n]
            dmix = dmix_ref[...]
            dmix_t = dmix.astype(f32).T.astype(bf16)
            qt = rot_ref[:qw, here]
            q = qt.astype(f32).T.astype(bf16)
            cosine, sine = cos_ref[:, here], sin_ref[:, here]
            dqs, gain_sum = [], jnp.zeros((HD, 1), f32)
            dk, dv = jnp.zeros((n, HD), f32), jnp.zeros((n, HD), f32)
            for h in range(heads):
                part = slice(h * HD, (h + 1) * HD)
                p = jnp.exp(dot(keys, qt[part] * 0.125) + bias - lse_ref[h : h + 1, here])
                dv += dot(p.astype(bf16), dmix[:, part])
                dp = dot(values, dmix_t[part])
                inner = jnp.sum(dp * p, axis=0, keepdims=True)
                ds = (p * (dp - inner)).astype(bf16)
                dk += dot(ds, q[:, part])
                dq = (dot(kt, ds) * 0.125).astype(bf16).astype(f32)
                du, dg = unprep(dq, raw_ref[part, here], gq_ref[...], cosine, sine)
                dqs.append(du)
                gain_sum += dg
            dk_acc[:n, :] += dk
            dv_acc[:n, :] += dv
            gg_ref[:, :1] += gain_sum
            dproj_ref[here, :qw] = jnp.concatenate(dqs, axis=0).T.astype(bf16)

    @pl.when(i == pl.num_programs(0) - 1)
    def _():
        dk = (dk_acc[...] * 0.125).astype(bf16).astype(f32).T
        du, dg = unprep(dk, raw_ref[qw : qw + HD, :], gk_ref[...], cos_ref[...], sin_ref[...])
        gg_ref[:, 1:2] += dg
        dproj_ref[:, qw:] = jnp.concatenate([du.T, dv_acc[...].astype(bf16).astype(f32)], axis=1).astype(bf16)
        move.finish()


def attention_back(S, dmix, rot, raw, lse, pos, cosine, sine, gain_q, gain_k, d_attn, heads, collective):
    length = dmix.shape[0]
    hw = rot.shape[0]
    whole = lambda a: pl.BlockSpec(a.shape, lambda i: (0, 0))
    return pl.pallas_call(
        functools.partial(attn_back_kernel, S, heads),
        grid=(length // BLOCK,),
        in_specs=[pl.BlockSpec((BLOCK, heads * HD), lambda i: (i, 0))]
        + [whole(a) for a in (rot, raw, lse, pos, cosine, sine, gain_q, gain_k)]
        + [ANY],
        out_specs=[pl.BlockSpec((length, hw), lambda i: (0, 0)), pl.BlockSpec((HD, 128), lambda i: (0, 0)), ANY],
        out_shape=[shape((length, hw)), shape((HD, 128), f32), shape((S,) + d_attn.shape)],
        scratch_shapes=[
            pltpu.VMEM((length, HD), bf16),
            pltpu.VMEM((length, HD), bf16),
            pltpu.VMEM((length, HD), f32),
            pltpu.VMEM((length, HD), f32),
        ]
        + Gather.sems(S, d_attn),
        compiler_params=params(collective, 1),
        cost_estimate=cost(1),
    )(dmix, rot, raw, lse, pos, cosine, sine, gain_q, gain_k, d_attn)


def input_back_kernel(S, dproj_ref, dproj_hbm, mix_t_ref, dattn_ref, normed_t_ref, wqkv_ref, x_ref, g_ref, gm_ref, pout_ref, pqkv_ref, gin_ref, gg_ref, got, send, recv):
    s = lax.axis_index("sp")
    T, width = x_ref.shape
    greet(S, False)

    def copy(k, slot):
        rows = pl.ds(pl.multiple_of(lax.rem(s + k, S) * T, T), T)
        return to_peer(dproj_hbm.at[rows], got.at[slot], send.at[k - 1], recv.at[k - 1], k, S)

    for k in range(1, S):
        copy(k, s).start()
    tile = 512
    mix_t, dproj = mix_t_ref[...], dproj_ref[...]
    for c in range(0, width, tile):
        pout_ref[:, c : c + tile] = dot(mix_t, dattn_ref[:, c : c + tile]).astype(bf16)
    for c in range(0, width, tile):
        pqkv_ref[c : c + tile, :] = dot(normed_t_ref[c : c + tile, :], dproj).astype(bf16)
    e = dot_nt(dproj_ref[pl.ds(pl.multiple_of(s * T, T), T), :], wqkv_ref[s])
    for k in range(1, S):
        slot = lax.rem(s + S - k, S)
        copy(k, slot).wait_recv()
        e += dot_nt(got[slot], wqkv_ref[slot])
    v = x_ref[...].astype(f32)
    r = lax.rsqrt(jnp.mean(v * v, axis=-1, keepdims=True) + EPS)
    gg_ref[...] = jnp.sum(e * v * r, axis=0, keepdims=True)
    ge = g_ref[...] * e
    gin_ref[...] = gm_ref[...] + r * ge - v * (r * r * r * jnp.mean(ge * v, axis=-1, keepdims=True))
    for k in range(1, S):
        copy(k, s).wait_send()


def input_back(S, dproj, mix_t, dattn_all, normed_t, wqkv_all, x, gain, gm, collective):
    T, width = x.shape
    hw = dproj.shape[1]
    return pl.pallas_call(
        functools.partial(input_back_kernel, S),
        in_specs=[VMEM, ANY] + [VMEM] * 7,
        out_specs=[VMEM] * 4,
        out_shape=[shape((mix_t.shape[0], width)), shape((width, hw)), shape((T, width), f32), shape((1, width), f32)],
        scratch_shapes=[pltpu.VMEM((S, T, hw), bf16), DMA((S - 1,)), DMA((S - 1,))],
        compiler_params=params(collective),
        cost_estimate=cost(1),
    )(dproj, dproj, mix_t, dattn_all, normed_t, wqkv_all, x, gain, gm)


def output_kernel(S, hid_ref, wd_ref, mid_ref, out_ref, acc, send_buf, recv_buf, send, recv):
    s = lax.axis_index("sp")
    T, width = mid_ref.shape
    tile = 512
    greet(S, False)

    def compute(chunk, out):
        rows = hid_ref[pl.ds(pl.multiple_of(chunk * T, T), T), :]
        for c in range(0, width, tile):
            out[:, c : c + tile] = dot(rows, wd_ref[:, c : c + tile]).astype(out.dtype)

    copies = sum_over_sp(S, compute, acc, send_buf, recv_buf, send, recv)
    out_ref[...] = (mid_ref[...] + acc[...]).astype(bf16)
    for copy in copies:
        copy.wait_send()


def output_rows(S, hidden, w_dn, mid, collective):
    T, width = mid.shape
    return pl.pallas_call(
        functools.partial(output_kernel, S),
        in_specs=[VMEM] * 3,
        out_specs=VMEM,
        out_shape=shape((T, width)),
        scratch_shapes=[
            pltpu.VMEM((T, width), f32),
            pltpu.VMEM((S - 1, T, width), bf16),
            pltpu.VMEM((S - 1, T, width), bf16),
            DMA((max(6, S - 1),)),
            DMA((max(6, S - 1),)),
        ],
        compiler_params=params(collective),
        cost_estimate=cost(40),
    )(hidden, w_dn, mid)


def ordered(value, *after):
    return lax.optimization_barrier((value,) + after)[0]


def local(x_own, positions, ct_own, w_qkv, w_out, w_gate, w_up, w_down, gain_attn, gain_ffn, gain_query, gain_key):
    S, F = lax.axis_size("sp"), lax.axis_size("fsdp")
    s = lax.axis_index("sp")
    _, T, D = x_own.shape
    L = positions.shape[1]
    copies = max(1, S // KV_HEADS)
    QW = QUERY_HEADS * HD
    KW = KV_HEADS * HD
    heads = QUERY_HEADS // S
    qw = heads * HD
    hw = qw + 2 * HD
    FF = w_gate.shape[1]
    FFs = FF // S
    rows_d = D // (S * F)
    rows_o = QW // (S * F)
    x_own = x_own[0]
    ct_own = ct_own[0]

    def cut(w, start, size, axis):
        return lax.dynamic_slice_in_dim(w, start, size, axis)

    def own_rows(w):
        size = w.shape[0] // S
        return cut(w, s * size, size, 0)

    def gather_z(w):
        return lax.all_gather(w, "fsdp", axis=0, tiled=True)

    def reduce_z(w):
        return lax.psum_scatter(w, "fsdp", scatter_dimension=0, tiled=True)

    gains = jnp.pad(jnp.stack([gain_attn, gain_ffn], axis=1), ((0, 0), (0, 126)))
    kv = s // copies
    attn_part = jnp.concatenate(
        [
            cut(w_qkv, s * qw, qw, 1),
            cut(w_qkv, QW + kv * HD, HD, 1),
            cut(w_qkv, QW + KW + kv * HD, HD, 1),
            gains,
            own_rows(w_out).reshape(D // F, qw),
        ],
        axis=1,
    )
    attn_full = gather_z(attn_part)
    piece = FFs // F

    def own_columns(w):
        return cut(w.reshape(D // F, F, S, piece), s, 1, 2).reshape(D // F, FFs)

    gu_part = jnp.concatenate([own_columns(w_gate), own_columns(w_up)], axis=1)
    w_gu = gather_z(gu_part)
    w_dn = gather_z(own_rows(w_down))

    x_all = gather_sp(S, x_own, 0).reshape(L, D)
    frequency = 10000.0 ** (-2.0 * jnp.arange(HD // 2, dtype=f32) / HD)
    angles = frequency[:, None] * positions.astype(f32)
    cosine, sine = jnp.cos(angles), jnp.sin(angles)
    gain_q = gain_query.astype(f32)[:, None]
    gain_k = gain_key.astype(f32)[:, None]
    wqkv_s = attn_full[:, :hw]
    g_attn = attn_full[:, hw].astype(f32)[None]
    g_ffn = attn_full[:, hw + 1].astype(f32)[None]
    wout_s = attn_full[:, hw + 128 :].reshape(F, rows_o, D)
    normed_t, raw, rot, lse, mix_t, mix_all, wout_all = forward_attention(
        S, x_all, g_attn, wqkv_s, positions, cosine, sine, gain_q, gain_k, wout_s, heads, 1
    )
    wout_all = wout_all.reshape(S, qw, D)
    mid, ffn_in, ffn_t, ct_all = middle_rows(S, x_all, mix_all, wout_all, g_ffn, ct_own, 2)
    ct_all = ct_all.reshape(L, D)
    gate, up, hidden, part_down, wqkv_all = ffn_forward(S, ffn_in, ct_all, w_gu, wqkv_s, 3)
    grad_down = reduce_z(part_down)
    dgu, part_gu = ffn_backward(S, F, ct_all, w_dn, gate, up, ffn_t)
    grad_gu = reduce_z(part_gu.reshape(2 * D, FFs))
    gm, d_attn, grad_g_ffn, d_mix = middle_back(S, dgu, w_gu, wout_all, mid, g_ffn, ct_own, 4)
    d_proj, gain_sums, dattn_all = attention_back(
        S, ordered(d_mix, grad_down), rot, raw, lse, positions, cosine, sine, gain_q, gain_k, d_attn, heads, 5
    )
    part_out, part_qkv, grad_input, grad_g_attn = input_back(
        S, d_proj, mix_t, dattn_all.reshape(L, D), normed_t, wqkv_all, x_own, g_attn, gm, 6
    )

    W = 128
    n_q, n_o, n_g = S * rows_d * hw // W, rows_o * D // W, 16 * S
    small = jnp.concatenate([grad_g_attn, grad_g_ffn]).astype(bf16).reshape(2, S, F, rows_d)
    small = jnp.transpose(small, (2, 1, 0, 3)).reshape(F, S, 2 * rows_d)
    both = jnp.broadcast_to(gain_sums[:, :2].astype(bf16).T.reshape(1, 1, 2 * HD), (F, S, 2 * HD))
    small = jnp.concatenate([small, both], axis=2)
    small = jnp.pad(small, ((0, 0), (0, 0), (0, 16 * W - small.shape[2]))).reshape(F, n_g, W)
    part_qkv = jnp.transpose(part_qkv.reshape(S, F, rows_d, hw // W, W), (1, 0, 3, 2, 4)).reshape(F, n_q, W)
    part_out = jnp.transpose(part_out.reshape(F, rows_o, D // W, W), (0, 2, 1, 3)).reshape(F, n_o, W)
    packed = jnp.concatenate([part_qkv, part_out, small], axis=1).reshape(F * (n_q + n_o + n_g), W)
    mine = reduce_z(ordered(packed, grad_gu))
    out = output_rows(S, ordered(hidden, packed), w_dn, mid, 7)
    grad_gu = lax.all_to_all(grad_gu.reshape(S, 2, rows_d, FFs), "sp", split_axis=0, concat_axis=0)
    grad_out = jnp.swapaxes(mine[n_q : n_q + n_o].reshape(D // W, rows_o, W), 0, 1).reshape(rows_o, D).astype(f32)
    per_s = jnp.concatenate([mine[:n_q].reshape(S, n_q // S, W), mine[n_q + n_o :].reshape(S, 16, W)], axis=1)
    got = lax.all_to_all(per_s, "sp", split_axis=0, concat_axis=0)
    grad_qkv = jnp.swapaxes(got[:, :-16].reshape(S, hw // W, rows_d, W), 1, 2).reshape(S, rows_d, hw)
    tiny = jnp.sum(got[:, -16:].reshape(S, 16 * W)[:, : 2 * rows_d + 2 * HD].astype(f32), axis=0)
    grad_q = jnp.swapaxes(grad_qkv[:, :, :qw], 0, 1).reshape(rows_d, QW).astype(f32)
    grad_kv = jnp.sum(grad_qkv[:, :, qw:].reshape(KV_HEADS, copies, rows_d, 2, HD).astype(f32), axis=1)
    grad_kv = jnp.transpose(grad_kv, (1, 2, 0, 3)).reshape(rows_d, 2 * KW)
    grad_qkv = jnp.concatenate([grad_q, grad_kv], axis=1)
    grad_gu = jnp.transpose(grad_gu.reshape(S, 2, rows_d, F, piece), (1, 2, 3, 0, 4)).reshape(2, rows_d, FF).astype(f32)
    to_owner = [(i * F + j, j * S + i) for i in range(S) for j in range(F)]
    grad_down = lax.ppermute(grad_down, ("sp", "fsdp"), to_owner)
    return (
        out[None],
        grad_input[None],
        grad_qkv,
        grad_out,
        grad_gu[0],
        grad_gu[1],
        grad_down.astype(f32),
        tiny[:rows_d],
        tiny[rows_d : 2 * rows_d],
        tiny[2 * rows_d : 2 * rows_d + HD],
        tiny[2 * rows_d + HD :],
    )


def solution(mesh):
    row = P("fsdp", "sp", None)
    shard = P("fsdp", None)
    grad = P(("sp", "fsdp"), None)
    return jax.shard_map(
        local,
        mesh=mesh,
        in_specs=(row, shard, row, shard, shard, shard, shard, shard, P("fsdp"), P("fsdp"), P(), P()),
        out_specs=(row, row, grad, grad, grad, grad, grad, P(("sp", "fsdp")), P(("sp", "fsdp")), P(), P()),
        check_vma=False,
    )
```

```python
import functools

import jax
import jax.numpy as jnp
import numpy as np
from jax import lax
from jax.experimental import pallas as pl
from jax.experimental.pallas import tpu as pltpu
from jax.sharding import PartitionSpec as P

QUERY_HEADS = 16
KV_HEADS = 4
HD = 64
EPS = 1e-06
BLOCK = 256
VMEM_LIMIT = 60 << 20
MESH = pl.DeviceIdType.MESH
f32 = jnp.float32
bf16 = jnp.bfloat16


def params(collective=None, grid=0):
    return pltpu.CompilerParams(
        dimension_semantics=("arbitrary",) * grid if grid else None,
        vmem_limit_bytes=VMEM_LIMIT,
        collective_id=collective,
        has_side_effects=collective is not None,
    )


def cost(micros):
    return pl.CostEstimate(flops=0, bytes_accessed=int(micros * 3_600_000), transcendentals=0)


ANY = pl.BlockSpec(memory_space=pl.ANY)
VMEM = pl.BlockSpec(memory_space=pltpu.VMEM)
DMA = pltpu.SemaphoreType.DMA


def shape(dims, dtype=bf16):
    return jax.ShapeDtypeStruct(dims, dtype)


def dot(a, b):
    return jnp.dot(a, b, preferred_element_type=f32)


def dot_nt(a, b):
    return lax.dot_general(a, b, (((1,), (1,)), ((), ())), preferred_element_type=f32)


def sibling():
    f = lax.axis_index("fsdp")
    return {"fsdp": f + 1 - 2 * lax.rem(f, 2)}


def greet(S, F=0, with_sibling=False):
    s, f = lax.axis_index("sp"), lax.axis_index("fsdp")
    where = [{"sp": lax.rem(s + k, S)} for k in range(1, S)]
    where += [{"fsdp": lax.rem(f + 2 * k, F)} for k in range(1, F // 2)]
    if with_sibling:
        where.append(sibling())
    barrier = pltpu.get_barrier_semaphore()
    for target in where:
        pl.semaphore_signal(barrier, inc=1, device_id=target, device_id_type=MESH)
    pl.semaphore_wait(barrier, len(where))


def gain_row(g_ref, n):
    return jnp.concatenate([g_ref[j].astype(f32)[n : n + 1] for j in range(g_ref.shape[0])], axis=1)


def to_peer(src, dst, send, recv, k, S):
    s = lax.axis_index("sp")
    return pltpu.make_async_remote_copy(
        src_ref=src, dst_ref=dst, send_sem=send, recv_sem=recv, device_id={"sp": lax.rem(s + k, S)}, device_id_type=MESH
    )


def mates(s):
    return s + 1 - 2 * lax.rem(s, 2), lax.rem(s + 2, 4), 3 - s


def push(src, dst, send, recv, where):
    return pltpu.make_async_remote_copy(
        src_ref=src, dst_ref=dst, send_sem=send, recv_sem=recv, device_id=where, device_id_type=MESH
    )


class Gather:
    def __init__(self, S, src, dst, sems, halves=False, inner=False):
        self.S, self.src, self.halves = S, src, halves
        self.slot = (lambda j: dst.at[:, j]) if inner else (lambda j: dst.at[j])
        self.send, self.recv, self.own, self.stage = sems[:4]
        self.swap_send, self.swap_recv = sems[4:] if halves else (None, None)
        self.s, self.f = lax.axis_index("sp"), lax.axis_index("fsdp")
        self.rows = src.shape[0] // (2 if halves else 1)
        self.size = self.rows // 2 if S == 4 else self.rows

    @staticmethod
    def sems(S, chunk, halves=False):
        count = 6 if S == 4 else S - 1
        base = [DMA((count,)), DMA((count,)), DMA((2,)), pltpu.VMEM(chunk.shape, chunk.dtype)]
        return base + [DMA((S - 1,)), DMA((S - 1,))] if halves else base

    def base(self, mine=True):
        if not self.halves:
            return 0
        core = lax.rem(self.f, 2)
        return (core if mine else 1 - core) * self.rows

    def piece(self, ref, n):
        return ref.at[pl.ds(self.base() + n * self.size, self.size)]

    def share(self, slot, mine):
        if not self.halves:
            return self.slot(slot)
        return self.slot(slot).at[pl.ds(self.base(mine), self.rows)]

    def steps(self):
        s, S = self.s, self.S
        if S != 4:
            return [(self.src, s, lax.rem(s + S - k, S), 0, lax.rem(s + k, S)) for k in range(1, S)]
        x, y, d = mates(s)
        return [
            (self.src, s, x, 0, x),
            (self.src, s, y, 1, y),
            (self.src, s, x, 1, x),
            (self.src, s, y, 0, y),
            (self.slot(x), x, d, 0, y),
            (self.slot(y), y, d, 1, x),
        ]

    def copy(self, n, here):
        src, there, lands, piece, target = self.steps()[n]
        slot = lands if here else there
        return push(
            self.piece(src, piece), self.piece(self.slot(slot), piece), self.send.at[n], self.recv.at[n], {"sp": target}
        )

    def passing(self, n, mine):
        slots = mates(self.s) if self.S == 4 else [lax.rem(self.s + self.S - k, self.S) for k in range(1, self.S)]
        return push(
            self.share(slots[n], True), self.share(slots[n], mine), self.swap_send.at[n], self.swap_recv.at[n], sibling()
        )

    def local(self, out):
        if out:
            return pltpu.make_async_copy(self.stage, self.slot(self.s), self.own.at[1])
        return pltpu.make_async_copy(self.src, self.stage, self.own.at[0])

    def start(self):
        for n in range(4 if self.S == 4 else self.S - 1):
            self.copy(n, False).start()
        self.local(False).start()

    def relay(self):
        self.local(False).wait()
        self.local(True).start()
        if self.S == 4:
            for n in range(2):
                self.copy(n, True).wait_recv()
                self.copy(4 + n, False).start()

    def finish(self, relayed=False):
        if not relayed:
            self.relay()
        ready = {2: 0, 3: 1, 5: 2} if self.S == 4 else {n: n for n in range(self.S - 1)}
        for n in range(2 if self.S == 4 else 0, len(self.steps())):
            self.copy(n, True).wait_recv()
            if self.halves and n in ready:
                self.passing(ready[n], True).start()
        self.local(True).wait()
        for n in range(len(self.steps())):
            self.copy(n, False).wait_send()
        if self.halves:
            for n in range(self.S - 1):
                self.passing(n, True).wait_send()
                self.passing(n, False).wait_recv()


class GatherZ:
    def __init__(self, F, src, dst, sems):
        self.F, self.src, self.dst = F, src, dst
        self.send, self.recv, self.pass_send, self.pass_recv, self.own = sems
        self.f = lax.axis_index("fsdp")

    @staticmethod
    def sems(F):
        return [DMA((F // 2 - 1,)), DMA((F // 2 - 1,)), DMA((F // 2,)), DMA((F // 2,)), DMA]

    def sending(self, k):
        return push(
            self.src, self.dst.at[self.f], self.send.at[k - 1], self.recv.at[k - 1], {"fsdp": lax.rem(self.f + 2 * k, self.F)}
        )

    def landing(self, k):
        slot = lax.rem(self.f + self.F - 2 * k, self.F)
        return push(
            self.src, self.dst.at[slot], self.send.at[k - 1], self.recv.at[k - 1], {"fsdp": lax.rem(self.f + 2 * k, self.F)}
        )

    def passing(self, k, mine):
        f, F = self.f, self.F
        slot = lax.rem(f + F - 2 * k, F)
        other = f + 1 - 2 * lax.rem(f, 2)
        there = slot if mine else lax.rem(other + F - 2 * k, F)
        src = self.src if k == 0 else self.dst.at[slot]
        return push(src, self.dst.at[there], self.pass_send.at[k], self.pass_recv.at[k], sibling())

    def local(self):
        return pltpu.make_async_copy(self.src, self.dst.at[self.f], self.own)

    def start(self):
        for k in range(1, self.F // 2):
            self.sending(k).start()
        self.passing(0, True).start()
        self.local().start()

    def finish(self):
        for k in range(1, self.F // 2):
            self.landing(k).wait_recv()
            self.passing(k, True).start()
        self.local().wait()
        for k in range(1, self.F // 2):
            self.sending(k).wait_send()
        for k in range(self.F // 2):
            self.passing(k, True).wait_send()
            self.passing(k, False).wait_recv()


def first_kernel(S, F, heads, x_ref, wqkv_ref, wout_ref, ga_ref, gf_ref, pos_ref, freq_ref, x_all, wqkv_all, wout_all, gains_all, cos_ref, sin_ref, part, gains, *sems):
    s = lax.axis_index("sp")
    qw = heads * HD
    QW, KW = QUERY_HEADS * HD, KV_HEADS * HD
    kv = s // max(1, S // KV_HEADS)
    pair = kv // 2
    high = lax.rem(kv, 2)

    def cut(start):
        block = wqkv_ref[:, pl.ds(pl.multiple_of(start + pair * 128, 128), 128)].astype(f32)
        return jnp.where(high == 1, block[:, HD:], block[:, :HD])

    part[:, :qw] = wqkv_ref[:, pl.ds(pl.multiple_of(s * qw, 128), qw)]
    part[:, qw:] = jnp.concatenate([cut(QW), cut(QW + KW)], axis=1).astype(bf16)
    pad = jnp.zeros((14, ga_ref.shape[1]), f32)
    gains[...] = jnp.concatenate([ga_ref[...].astype(f32), gf_ref[...].astype(f32), pad], axis=0).astype(bf16)
    n = len(Gather.sems(S, shape((1, 1))))
    m = len(GatherZ.sems(F))
    move_x = Gather(S, x_ref, x_all, sems[:n])
    rows = wout_ref.shape[0] // S
    own_out = wout_ref.at[pl.ds(pl.multiple_of(s * rows, rows), rows)]
    moves_z = [
        GatherZ(F, part, wqkv_all, sems[n : n + m]),
        GatherZ(F, gains, gains_all, sems[n + m : n + 2 * m]),
        GatherZ(F, own_out, wout_all, sems[n + 2 * m :]),
    ]
    greet(S, F, True)
    move_x.start()
    for move in moves_z:
        move.start()
    angles = freq_ref[...] * pos_ref[...].astype(f32)
    cos_ref[...] = jnp.cos(angles)
    sin_ref[...] = jnp.sin(angles)
    move_x.relay()
    for move in moves_z:
        move.finish()
    move_x.finish(True)


def first_gathers(S, F, x, w_qkv, w_out, gain_attn, gain_ffn, positions, heads, collective):
    T, width = x.shape
    depth = w_qkv.shape[0]
    hw = (heads + 2) * HD
    length = positions.shape[1]
    frequency = jnp.asarray(10000.0 ** (-2.0 * np.arange(HD // 2) / HD), f32)[:, None]
    table = shape((HD // 2, length), f32)
    return pl.pallas_call(
        functools.partial(first_kernel, S, F, heads),
        in_specs=[ANY] + [VMEM] * 6,
        out_specs=[ANY] * 4 + [VMEM] * 2,
        out_shape=[
            shape((S, T, width)),
            shape((F, depth, hw)),
            shape((F, w_out.shape[0] // S, width)),
            shape((F, 16, depth)),
            table,
            table,
        ],
        scratch_shapes=[pltpu.VMEM((depth, hw), bf16), pltpu.VMEM((16, depth), bf16)]
        + Gather.sems(S, x)
        + GatherZ.sems(F) * 3,
        compiler_params=params(collective),
        cost_estimate=cost(45),
    )(x, w_qkv, w_out, gain_attn, gain_ffn, positions, frequency)


def columns_kernel(S, F, gate_hbm, up_hbm, out_hbm, buf, sem_in, sem_out):
    s = lax.axis_index("sp")
    piece = buf.shape[2] // F
    ins = []
    for n, ref in enumerate((gate_hbm, up_hbm)):
        for m in range(F):
            src = ref.at[:, pl.ds(pl.multiple_of((m * S + s) * piece, piece), piece)]
            ins.append(pltpu.make_async_copy(src, buf.at[n, :, pl.ds(m * piece, piece)], sem_in.at[n * F + m]))
    for copy in ins:
        copy.start()
    outs = []
    for n in range(2):
        for copy in ins[n * F : (n + 1) * F]:
            copy.wait()
        outs.append(pltpu.make_async_copy(buf.at[n], out_hbm.at[n], sem_out.at[n]))
        outs[-1].start()
    for copy in outs:
        copy.wait()


def own_columns(S, F, s, w_gate, w_up):
    depth, FF = w_gate.shape
    piece = FF // (S * F)
    if piece % 128:
        pick = lambda w: lax.dynamic_slice_in_dim(w.reshape(depth, F, S, piece), s, 1, 2).reshape(depth, FF // S)
        return jnp.stack([pick(w_gate), pick(w_up)])
    return pl.pallas_call(
        functools.partial(columns_kernel, S, F),
        in_specs=[ANY, ANY],
        out_specs=ANY,
        out_shape=shape((2, depth, FF // S)),
        scratch_shapes=[pltpu.VMEM((2, depth, FF // S), bf16), DMA((2 * F,)), DMA((2,))],
        compiler_params=params(),
        cost_estimate=cost(3),
    )(w_gate, w_up)


def forward_kernel(S, heads, x_ref, g_ref, w_ref, pos_ref, cos_ref, sin_ref, gq_ref, gk_ref, wout_ref, normed_t_ref, raw_ref, rot_ref, lse_ref, mix_t_ref, mix_all, wout_all, k_buf, vt_buf, mix_buf, mix_send, mix_recv, mix_own, *sems):
    i = pl.program_id(0)
    s = lax.axis_index("sp")
    qw = heads * HD
    half = HD // 2
    move = Gather(S, wout_ref, wout_all, sems, halves=True, inner=True)

    @pl.when(i == 0)
    def _():
        greet(S, 0, True)
        move.start()

    @pl.when(i == 2)
    def _():
        move.relay()

    x = x_ref[...].astype(f32)
    scale = lax.rsqrt(jnp.mean(x * x, axis=-1, keepdims=True) + EPS)
    scaled = x * scale * gain_row(g_ref, 0)
    normed = scaled.astype(bf16)
    normed_t_ref[...] = scaled.T.astype(bf16)
    raw = dot(normed, w_ref[...]).T
    raw_ref[...] = raw
    cosine, sine = cos_ref[...], sin_ref[...]

    def prep(u, gain):
        n = u * lax.rsqrt(jnp.mean(u * u, axis=0, keepdims=True) + EPS) * gain
        front, back = n[:half], n[half:]
        return jnp.concatenate([front * cosine - back * sine, back * cosine + front * sine], axis=0)

    q = [prep(raw[h * HD : (h + 1) * HD], gq_ref[...]).astype(bf16) for h in range(heads)]
    kt = prep(raw[qw : qw + HD], gk_ref[...])
    vt = raw[qw + HD :].astype(bf16)
    rot_ref[...] = jnp.concatenate(q + [kt.astype(bf16), vt], axis=0)
    blocks = pl.num_programs(0)
    steps = mix_buf.shape[0]

    x_mate, y_mate, d_mate = mates(s)

    def mix_copy(block, k, here):
        rows = pl.ds(block * BLOCK, BLOCK)
        n = block * (S - 1) + k - 1
        if S != 4:
            slot = lax.rem(s + S - k, S) if here else s
            return push(mix_buf.at[block], mix_all.at[slot, rows], mix_send.at[n], mix_recv.at[n], {"sp": lax.rem(s + k, S)})
        if k < 3:
            mate = x_mate if k == 1 else y_mate
            slot = mate if here else s
            return push(mix_buf.at[block], mix_all.at[slot, rows], mix_send.at[n], mix_recv.at[n], {"sp": mate})
        source, mate = (x_mate, y_mate) if block < steps // 2 else (y_mate, x_mate)
        slot = d_mate if here else source
        return push(mix_all.at[source, rows], mix_all.at[slot, rows], mix_send.at[n], mix_recv.at[n], {"sp": mate})

    def mix_local(block):
        return pltpu.make_async_copy(mix_buf.at[block], mix_all.at[s, pl.ds(block * BLOCK, BLOCK)], mix_own.at[block])

    for step in range(steps):

        @pl.when(i == step)
        def _():
            n = (step + 1) * BLOCK
            k_buf[step * BLOCK : n, :] = kt.T.astype(bf16)
            vt_buf[:, step * BLOCK : n] = vt
            col = lax.broadcasted_iota(jnp.int32, (n, BLOCK), 0)
            row = step * BLOCK + lax.broadcasted_iota(jnp.int32, (n, BLOCK), 1)
            bias = jnp.where((col <= row) & (row - col <= pos_ref[...]), 0.0, -1e30)
            keys, values = k_buf[:n, :], vt_buf[:, :n]
            mixes, lses = [], []
            for h in range(heads):
                e = jnp.exp(dot(keys, q[h] * 0.125) + bias)
                total = jnp.sum(e, axis=0, keepdims=True)
                p = (e * (1.0 / total)).astype(bf16)
                mixes.append(dot(values, p))
                lses.append(jnp.log(total))
            mix = jnp.concatenate(mixes, axis=0)
            mix_t_ref[...] = mix.astype(bf16)
            lse_ref[...] = jnp.concatenate(lses + [jnp.zeros((8 - heads, BLOCK), f32)], axis=0)
            mix_buf[step] = mix.T.astype(bf16)
            for k in range(1, 3 if S == 4 else S):
                mix_copy(step, k, False).start()
            mix_local(step).start()

    @pl.when(i == blocks - 1)
    def _():
        for block in range(steps):
            for k in range(1, 3 if S == 4 else S):
                mix_copy(block, k, True).wait_recv()
                if S == 4 and k == (1 if block < steps // 2 else 2):
                    mix_copy(block, 3, False).start()
        for block in range(steps):
            if S == 4:
                mix_copy(block, 3, True).wait_recv()
            for k in range(1, S):
                mix_copy(block, k, False).wait_send()
            mix_local(block).wait()
        move.finish(True)


def forward_attention(S, x, gain, w, pos, cosine, sine, gain_q, gain_k, wout, heads, collective):
    length, width = x.shape
    hw = w.shape[1]
    qw = heads * HD
    steps = length // BLOCK
    full = lambda i: (0, 0)
    rows = lambda i: (i, 0)
    cols = lambda i: (0, i)
    return pl.pallas_call(
        functools.partial(forward_kernel, S, heads),
        grid=(steps,),
        in_specs=[
            pl.BlockSpec((BLOCK, width), rows),
            pl.BlockSpec(gain.shape, lambda i: (0, 0, 0)),
            pl.BlockSpec((width, hw), full),
            pl.BlockSpec((1, BLOCK), cols),
            pl.BlockSpec((HD // 2, BLOCK), cols),
            pl.BlockSpec((HD // 2, BLOCK), cols),
            pl.BlockSpec((HD, 1), full),
            pl.BlockSpec((HD, 1), full),
            ANY,
        ],
        out_specs=[
            pl.BlockSpec((width, BLOCK), cols),
            pl.BlockSpec((hw, BLOCK), cols),
            pl.BlockSpec((hw, BLOCK), cols),
            pl.BlockSpec((8, BLOCK), cols),
            pl.BlockSpec((qw, BLOCK), cols),
            ANY,
            ANY,
        ],
        out_shape=[
            shape((width, length)),
            shape((hw, length), f32),
            shape((hw, length)),
            shape((8, length), f32),
            shape((qw, length)),
            shape((S, length, qw)),
            shape((wout.shape[0], S) + wout.shape[1:]),
        ],
        scratch_shapes=[
            pltpu.VMEM((length, HD), bf16),
            pltpu.VMEM((HD, length), bf16),
            pltpu.VMEM((steps, BLOCK, qw), bf16),
            DMA((steps * (S - 1),)),
            DMA((steps * (S - 1),)),
            DMA((steps,)),
        ]
        + Gather.sems(S, wout, True),
        compiler_params=params(collective, 1),
        cost_estimate=cost(45),
    )(x, gain, w, pos, cosine, sine, gain_q, gain_k, wout)


def middle_kernel(S, T, x_ref, mix_ref, wout_ref, g_ref, ct_ref, mid_ref, ffn_ref, ffn_t_ref, ct_all, *sems):
    i = pl.program_id(0)
    s = lax.axis_index("sp")
    move = Gather(S, ct_ref.at[:, pl.ds(ct_all.shape[2], ct_all.shape[2])], ct_all, sems)

    @pl.when(i == 0)
    def _():
        greet(S)
        move.start()

    @pl.when(i == pl.num_programs(0) - 1)
    def _():
        move.relay()

    middle = x_ref[...].astype(f32)
    total = dot(mix_ref[0], wout_ref[0])
    for j in range(1, S):
        total += dot(mix_ref[j], wout_ref[j])
    middle = middle + total

    @pl.when(i == s)
    def _():
        mid_ref[...] = middle

    scaled = middle * lax.rsqrt(jnp.mean(middle * middle, axis=-1, keepdims=True) + EPS) * gain_row(g_ref, 1)
    ffn_ref[...] = scaled.astype(bf16)
    ffn_t_ref[...] = scaled.T.astype(bf16)

    @pl.when(i == pl.num_programs(0) - 1)
    def _():
        move.finish(True)


def middle_rows(S, x, mix_all, wout_all, gain, ct, collective):
    length, width = x.shape
    T = length // S
    qw = mix_all.shape[2]
    return pl.pallas_call(
        functools.partial(middle_kernel, S, T),
        grid=(S,),
        in_specs=[
            pl.BlockSpec((T, width), lambda i: (i, 0)),
            pl.BlockSpec((S, T, qw), lambda i: (0, i, 0)),
            pl.BlockSpec((S, qw, width), lambda i: (0, 0, 0)),
            pl.BlockSpec(gain.shape, lambda i: (0, 0, 0)),
            ANY,
        ],
        out_specs=[
            pl.BlockSpec((T, width), lambda i: (0, 0)),
            pl.BlockSpec((T, width), lambda i: (i, 0)),
            pl.BlockSpec((width, T), lambda i: (0, i)),
            ANY,
        ],
        out_shape=[shape((T, width), f32), shape((length, width)), shape((width, length)), shape((S, T, width // 2))],
        scratch_shapes=Gather.sems(S, shape((T, width // 2))),
        compiler_params=params(collective, 1),
        cost_estimate=cost(45),
    )(x, mix_all, wout_all, gain, ct)


def ffn_kernel(S, ffn_ref, ct1_ref, wg_ref, wu_ref, ct_hbm, gate_ref, up_ref, hid_ref, down_ref, ct0_all, ct0, hid_t, out_sem, *sems):
    i = pl.program_id(0)
    last = pl.num_programs(0) - 1
    length, width = ffn_ref.shape
    half = width // 2
    T = length // S
    move = Gather(S, ct_hbm.at[:, pl.ds(0, half)], ct0, sems)

    @pl.when(i == 0)
    def _():
        greet(S)
        move.start()

    @pl.when(i == last - 1)
    def _():
        move.relay()

    rows = ffn_ref[...]
    gate, up = dot(rows, wg_ref[...].reshape(width, BLOCK)), dot(rows, wu_ref[...].reshape(width, BLOCK))
    gate_ref[...] = gate
    up_ref[...] = up
    hidden = gate / (1.0 + jnp.exp(-gate)) * up
    hid_ref[...] = hidden.astype(bf16)
    tile = pl.ds(pl.multiple_of(i * BLOCK, BLOCK), BLOCK)
    flipped = hidden.T.astype(bf16)
    hid_t[tile, :] = flipped
    down_ref[tile, half:] = dot(flipped, ct1_ref[...]).astype(bf16)

    @pl.when(i == last)
    def _():
        move.finish(True)
        back = pltpu.make_async_copy(ct0, ct0_all, out_sem)
        back.start()

        @pl.loop(0, hid_t.shape[0] // BLOCK)
        def _(n):
            at = pl.ds(pl.multiple_of(n * BLOCK, BLOCK), BLOCK)
            part = dot(hid_t[at, :T], ct0[0])
            for j in range(1, S):
                part += dot(hid_t[at, j * T : (j + 1) * T], ct0[j])
            down_ref[at, :half] = part.astype(bf16)

        back.wait()


def ffn_forward(S, ffn_in, ct1, w_gu, ct, collective):
    length, width = ffn_in.shape
    F, _, depth, FFs = w_gu.shape
    T = length // S
    whole = lambda i: (0, 0)
    col = pl.BlockSpec((length, BLOCK), lambda i: (0, i))
    return pl.pallas_call(
        functools.partial(ffn_kernel, S),
        grid=(FFs // BLOCK,),
        in_specs=[
            pl.BlockSpec((length, width), whole),
            pl.BlockSpec((length, width // 2), whole),
            pl.BlockSpec((F, 1, depth, BLOCK), lambda i: (0, 0, 0, i)),
            pl.BlockSpec((F, 1, depth, BLOCK), lambda i: (0, 1, 0, i)),
            ANY,
        ],
        out_specs=[col, col, col, pl.BlockSpec((FFs, width), whole), ANY],
        out_shape=[
            shape((length, FFs), f32),
            shape((length, FFs), f32),
            shape((length, FFs)),
            shape((FFs, width)),
            shape((S, T, width // 2)),
        ],
        scratch_shapes=[pltpu.VMEM((S, T, width // 2), bf16), pltpu.VMEM((FFs, length), bf16), DMA]
        + Gather.sems(S, shape((T, width // 2))),
        compiler_params=params(collective, 1),
        cost_estimate=cost(20),
    )(ffn_in, ct1, w_gu, w_gu, ct)


def ffn_back_kernel(S, F, ct0_ref, ct1_ref, wd_ref, gate_ref, up_ref, ffn_t_ref, wqkv_ref, dgu_ref, pgu_ref, wqkv_all, *sems):
    i = pl.program_id(0)
    last = pl.num_programs(0) - 1
    move = Gather(S, wqkv_ref, wqkv_all, sems, halves=True)

    @pl.when(i == 0)
    def _():
        greet(S, 0, True)
        move.start()

    @pl.when(i == last - 1)
    def _():
        move.relay()

    half = ct0_ref.shape[1]
    gh = dot_nt(ct0_ref[...], wd_ref[:, :half]) + dot_nt(ct1_ref[...], wd_ref[:, half:])
    gate, up = gate_ref[...], up_ref[...]
    sig = 1.0 / (1.0 + jnp.exp(-gate))
    d_gate = (gh * up * sig * (1.0 + gate * (1.0 - sig))).astype(bf16)
    d_up = (gh * (gate * sig)).astype(bf16)
    dgu_ref[0] = d_gate
    dgu_ref[1] = d_up
    ffn_t = ffn_t_ref[...]
    rows = pgu_ref.shape[3]
    for n, d in enumerate((d_gate, d_up)):
        part = dot(ffn_t, d).astype(bf16)
        for j in range(S):
            for m in range(F):
                pgu_ref[m, j, n] = part[(j * F + m) * rows : (j * F + m + 1) * rows]

    @pl.when(i == last)
    def _():
        move.finish(True)


def ffn_backward(S, F, ct0, ct1, w_dn, gate, up, ffn_t, wqkv_s, collective):
    length, FFs = gate.shape
    width = w_dn.shape[1]
    tiles = FFs // BLOCK
    rows = width // (S * F)
    whole = lambda i: (0, 0)
    col = lambda i: (0, i)
    return pl.pallas_call(
        functools.partial(ffn_back_kernel, S, F),
        grid=(tiles,),
        in_specs=[
            pl.BlockSpec((length, width // 2), whole),
            pl.BlockSpec((length, width // 2), whole),
            pl.BlockSpec((BLOCK, width), lambda i: (i, 0)),
            pl.BlockSpec((length, BLOCK), col),
            pl.BlockSpec((length, BLOCK), col),
            pl.BlockSpec((width, length), whole),
            ANY,
        ],
        out_specs=[
            pl.BlockSpec((2, length, BLOCK), lambda i: (0, 0, i)),
            pl.BlockSpec((F, S, 2, rows, BLOCK), lambda i: (0, 0, 0, 0, i)),
            ANY,
        ],
        out_shape=[shape((2, length, FFs)), shape((F, S, 2, rows, FFs)), shape((S,) + wqkv_s.shape)],
        scratch_shapes=Gather.sems(S, wqkv_s, True),
        compiler_params=params(collective, 1),
        cost_estimate=cost(1),
    )(ct0, ct1, w_dn, gate, up, ffn_t, wqkv_s)


def sum_over_sp(S, compute, acc, send_buf, recv_buf, send, recv):
    s = lax.axis_index("sp")
    if S != 4:

        def copy(k):
            return push(
                send_buf.at[k - 1], recv_buf.at[k - 1], send.at[k - 1], recv.at[k - 1], {"sp": lax.rem(s + k, S)}
            )

        for k in range(1, S):
            compute(lax.rem(s + k, S), send_buf.at[k - 1])
            copy(k).start()
        compute(s, acc)
        for k in range(1, S):
            copy(k).wait_recv()
            acc[...] += recv_buf[k - 1].astype(f32)
        return [copy(k) for k in range(1, S)]

    x, y, d = mates(s)
    half = acc.shape[0] // 2
    low, high = pl.ds(0, half), pl.ds(half, half)

    def copy(n):
        buf, rows, target = [(0, low, y), (0, high, x), (1, high, x), (2, low, y), (1, low, x), (2, high, y)][n]
        return push(send_buf.at[buf, rows], recv_buf.at[buf, rows], send.at[n], recv.at[n], {"sp": target})

    compute(d, send_buf.at[0])
    copy(0).start()
    copy(1).start()
    compute(x, send_buf.at[1])
    copy(2).start()
    compute(y, send_buf.at[2])
    copy(3).start()
    copy(0).wait_recv()
    send_buf[1, :half] = (send_buf[1, :half].astype(f32) + recv_buf[0, :half].astype(f32)).astype(bf16)
    copy(4).start()
    copy(1).wait_recv()
    send_buf[2, half:] = (send_buf[2, half:].astype(f32) + recv_buf[0, half:].astype(f32)).astype(bf16)
    copy(5).start()
    compute(s, acc)
    for n in range(2, 6):
        copy(n).wait_recv()
    acc[...] += recv_buf[1].astype(f32) + recv_buf[2].astype(f32)
    return [copy(n) for n in range(6)]


def middle_back_kernel(S, F, dgu_hbm, wgu_hbm, wout_hbm, mid_hbm, ct_hbm, g_ref, gm_ref, dattn_ref, gg_ref, dmix_ref, dgu, wgu, wout, mid, ct, acc, send_buf, recv_buf, mix_buf, send, recv, mix_send, mix_recv, mix_own, load):
    s = lax.axis_index("sp")
    T, width = mid.shape
    depth = wgu.shape[2]
    greet(S)
    if S == 4:
        x, y, d = mates(s)
        order = [d, x, y, s]
    else:
        order = [lax.rem(s + k, S) for k in range(1, S)] + [s]

    def chunk_load(n):
        rows = pl.ds(pl.multiple_of(order[n] * T, T), T)
        return pltpu.make_async_copy(dgu_hbm.at[:, rows], dgu.at[n], load.at[n])

    def weight_load(c):
        return pltpu.make_async_copy(wgu_hbm.at[c], wgu.at[c], load.at[S + c])

    others = [
        pltpu.make_async_copy(mid_hbm, mid, load.at[S + F]),
        pltpu.make_async_copy(ct_hbm, ct, load.at[S + F + 1]),
        pltpu.make_async_copy(wout_hbm, wout, load.at[S + F + 2]),
    ]
    chunk_load(0).start()
    for c in range(F):
        weight_load(c).start()
    for n in range(1, S):
        chunk_load(n).start()
    for copy in others:
        copy.start()
    calls = []

    def compute(chunk, out):
        n = len(calls)
        calls.append(n)
        chunk_load(n).wait()
        for c in range(F):
            if n == 0:
                weight_load(c).wait()
            part = dot_nt(dgu[n, 0], wgu[c, 0]) + dot_nt(dgu[n, 1], wgu[c, 1])
            out[:, c * depth : (c + 1) * depth] = part.astype(out.dtype)

    copies = sum_over_sp(S, compute, acc, send_buf, recv_buf, send, recv)
    for copy in others:
        copy.wait()
    v, e = mid[...], acc[...]
    r = lax.rsqrt(jnp.mean(v * v, axis=-1, keepdims=True) + EPS)
    gg_ref[...] = jnp.sum(e * v * r, axis=0, keepdims=True)
    ge = gain_row(g_ref, 1) * e
    gm = ct[...].astype(f32) + r * ge - v * (r * r * r * jnp.mean(ge * v, axis=-1, keepdims=True))
    gm_ref[...] = gm
    d_attn = gm.astype(bf16)
    dattn_ref[...] = d_attn

    def mix_copy(k, slot):
        rows = pl.ds(pl.multiple_of(slot * T, T), T)
        return to_peer(mix_buf.at[k], dmix_ref.at[rows], mix_send.at[k - 1], mix_recv.at[k - 1], k, S)

    for k in range(1, S):
        mix_buf[k] = dot_nt(d_attn, wout[lax.rem(s + k, S)]).astype(bf16)
        mix_copy(k, s).start()
    mix_buf[0] = dot_nt(d_attn, wout[s]).astype(bf16)
    own = pltpu.make_async_copy(mix_buf.at[0], dmix_ref.at[pl.ds(pl.multiple_of(s * T, T), T)], mix_own)
    own.start()
    for copy in copies:
        copy.wait_send()
    for k in range(1, S):
        mix_copy(k, s).wait_send()
        mix_copy(k, lax.rem(s + S - k, S)).wait_recv()
    own.wait()


def middle_back(S, dgu, w_gu, wout_all, mid, gain, ct, collective):
    T, width = mid.shape
    F = w_gu.shape[0]
    FFs = dgu.shape[2]
    qw = wout_all.shape[1]
    n = max(6, S - 1)
    return pl.pallas_call(
        functools.partial(middle_back_kernel, S, F),
        in_specs=[ANY] * 5 + [VMEM],
        out_specs=[VMEM, VMEM, VMEM, ANY],
        out_shape=[shape((T, width), f32), shape((T, width)), shape((1, width), f32), shape((S * T, qw))],
        scratch_shapes=[
            pltpu.VMEM((S, 2, T, FFs), bf16),
            pltpu.VMEM(w_gu.shape, bf16),
            pltpu.VMEM(wout_all.shape, bf16),
            pltpu.VMEM((T, width), f32),
            pltpu.VMEM((T, width), bf16),
            pltpu.VMEM((T, width), f32),
            pltpu.VMEM((S - 1, T, width), bf16),
            pltpu.VMEM((S - 1, T, width), bf16),
            pltpu.VMEM((S, T, qw), bf16),
            DMA((n,)),
            DMA((n,)),
            DMA((S - 1,)),
            DMA((S - 1,)),
            DMA,
            DMA((S + F + 3,)),
        ],
        compiler_params=params(collective),
        cost_estimate=cost(1),
    )(dgu, w_gu, wout_all, mid, ct, gain)


def attn_back_kernel(S, F, heads, dmix_ref, rot_ref, raw_ref, lse_ref, pos_ref, cos_ref, sin_ref, gq_ref, gk_ref, g_ref, ggf_ref, mix_t_ref, x_hbm, gm_hbm, normed_hbm, wqkv_hbm, dattn_hbm, packed_ref, gin_ref, k_buf, v_buf, dk_acc, dv_acc, gg, dproj, dattn_all, got, x, gm, normed_t, wqkv, send, recv, load, *sems):
    i = pl.program_id(0)
    s = lax.axis_index("sp")
    qw = heads * HD
    hw = qw + 2 * HD
    half = HD // 2
    length = rot_ref.shape[1]
    T, width = gin_ref.shape
    move = Gather(S, dattn_hbm, dattn_all, sems)
    loads = [
        pltpu.make_async_copy(a, b, load.at[n])
        for n, (a, b) in enumerate([(normed_hbm, normed_t), (wqkv_hbm, wqkv), (x_hbm, x), (gm_hbm, gm)])
    ]

    @pl.when(i == 0)
    def _():
        greet(S)
        move.start()
        for copy in loads:
            copy.start()
        k_buf[...] = rot_ref[qw : qw + HD, :].astype(f32).T.astype(bf16)
        v_buf[...] = rot_ref[qw + HD :, :].astype(f32).T.astype(bf16)
        dk_acc[...] = jnp.zeros_like(dk_acc)
        dv_acc[...] = jnp.zeros_like(dv_acc)
        gg[...] = jnp.zeros_like(gg)

    def unprep(e, u, gain, cosine, sine):
        front, back = e[:half], e[half:]
        e = jnp.concatenate([front * cosine + back * sine, back * cosine - front * sine], axis=0)
        r = lax.rsqrt(jnp.mean(u * u, axis=0, keepdims=True) + EPS)
        ge = gain * e
        du = r * ge - u * (r * r * r * jnp.mean(ge * u, axis=0, keepdims=True))
        return du, jnp.sum(e * u * r, axis=1, keepdims=True)

    for step in range(length // BLOCK):

        @pl.when(i == step)
        def _():
            n = (step + 1) * BLOCK
            here = slice(step * BLOCK, n)
            col = lax.broadcasted_iota(jnp.int32, (n, BLOCK), 0)
            row = step * BLOCK + lax.broadcasted_iota(jnp.int32, (n, BLOCK), 1)
            bias = jnp.where((col <= row) & (row - col <= pos_ref[:, here]), 0.0, -1e30)
            keys, values = k_buf[:n, :], v_buf[:n, :]
            kt = rot_ref[qw : qw + HD, :n]
            dmix = dmix_ref[...]
            dmix_t = dmix.astype(f32).T.astype(bf16)
            qt = rot_ref[:qw, here]
            q = qt.astype(f32).T.astype(bf16)
            cosine, sine = cos_ref[:, here], sin_ref[:, here]
            dqs, gain_sum = [], jnp.zeros((HD, 1), f32)
            dk, dv = jnp.zeros((n, HD), f32), jnp.zeros((n, HD), f32)
            for h in range(heads):
                part = slice(h * HD, (h + 1) * HD)
                p = jnp.exp(dot(keys, qt[part] * 0.125) + bias - lse_ref[h : h + 1, here])
                dv += dot(p.astype(bf16), dmix[:, part])
                dp = dot(values, dmix_t[part])
                inner = jnp.sum(dp * p, axis=0, keepdims=True)
                ds = (p * (dp - inner)).astype(bf16)
                dk += dot(ds, q[:, part])
                dq = (dot(kt, ds) * 0.125).astype(bf16).astype(f32)
                du, dg = unprep(dq, raw_ref[part, here], gq_ref[...], cosine, sine)
                dqs.append(du)
                gain_sum += dg
            dk_acc[:n, :] += dk
            dv_acc[:n, :] += dv
            gg[:, :1] += gain_sum
            dproj[here, :qw] = jnp.concatenate(dqs, axis=0).T.astype(bf16)

    def exchange(k, slot):
        rows = pl.ds(pl.multiple_of(lax.rem(s + k, S) * T, T), T)
        return to_peer(dproj.at[rows], got.at[slot], send.at[k - 1], recv.at[k - 1], k, S)

    @pl.when(i == pl.num_programs(0) - 1)
    def _():
        dk = (dk_acc[...] * 0.125).astype(bf16).astype(f32).T
        du, dg = unprep(dk, raw_ref[qw : qw + HD, :], gk_ref[...], cos_ref[...], sin_ref[...])
        gg[:, 1:2] += dg
        dproj[:, qw:] = jnp.concatenate([du.T, dv_acc[...].astype(bf16).astype(f32)], axis=1).astype(bf16)
        for k in range(1, S):
            exchange(k, s).start()
        move.relay()
        W = 128
        rows_d, rows_o = width // (S * F), qw // F
        blocks = hw // W
        n_q, n_o = S * rows_d * blocks, rows_o * width // W
        tile = 512
        for copy in loads:
            copy.wait()
        d_all = dproj[...]
        for c in range(0, width, tile):
            part = dot(normed_t[c : c + tile, :], d_all).astype(bf16)
            for b in range(tile // rows_d):
                j, m = divmod(c // rows_d + b, F)
                for cb in range(blocks):
                    at = (j * blocks + cb) * rows_d
                    packed_ref[m, at : at + rows_d] = part[b * rows_d : (b + 1) * rows_d, cb * W : (cb + 1) * W]
        e = dot_nt(dproj[pl.ds(pl.multiple_of(s * T, T), T), :], wqkv[s])
        for k in range(1, S):
            slot = lax.rem(s + S - k, S)
            exchange(k, slot).wait_recv()
            e += dot_nt(got[slot], wqkv[slot])
        v = x[...].astype(f32)
        r = lax.rsqrt(jnp.mean(v * v, axis=-1, keepdims=True) + EPS)
        ga = jnp.sum(e * v * r, axis=0, keepdims=True)
        ge = gain_row(g_ref, 0) * e
        gin_ref[...] = gm[...] + r * ge - v * (r * r * r * jnp.mean(ge * v, axis=-1, keepdims=True))
        heads_t = gg[...].T
        second = jnp.concatenate([heads_t[0:1], heads_t[1:2]], axis=1)
        gf = ggf_ref[...]
        for j in range(S):
            for m in range(F):
                cut = slice((j * F + m) * rows_d, (j * F + m + 1) * rows_d)
                first = [ga[:, cut], gf[:, cut]]
                if 2 * rows_d < W:
                    first.append(jnp.zeros((1, W - 2 * rows_d), f32))
                rows = jnp.concatenate([jnp.concatenate(first, axis=1), second, jnp.zeros((14, W), f32)], axis=0)
                packed_ref[m, n_q + n_o + 16 * j : n_q + n_o + 16 * (j + 1)] = rows.astype(bf16)
        move.finish(True)
        mix_t = mix_t_ref[...]
        for c in range(0, width, tile):
            part = jnp.zeros((qw, tile), f32)
            for j in range(S):
                part += dot(mix_t[:, j * T : (j + 1) * T], dattn_all[j, :, c : c + tile])
            for m in range(F):
                cuts = [part[m * rows_o : (m + 1) * rows_o, cb * W : (cb + 1) * W] for cb in range(tile // W)]
                at = n_q + c // W * rows_o
                packed_ref[m, at : at + rows_o * tile // W] = jnp.concatenate(cuts, axis=0).astype(bf16)
        for k in range(1, S):
            exchange(k, s).wait_send()


def attention_back(S, F, dmix, rot, raw, lse, pos, cosine, sine, gain_q, gain_k, gain, grad_gf, mix_t, x, gm, normed_t, wqkv_all, d_attn, heads, collective):
    length = dmix.shape[0]
    hw = rot.shape[0]
    T, width = x.shape
    rows_d, rows_o = width // (S * F), heads * HD // F
    total = S * rows_d * hw // 128 + rows_o * width // 128 + 16 * S
    whole = lambda a: pl.BlockSpec(a.shape, lambda i: (0,) * a.ndim)
    return pl.pallas_call(
        functools.partial(attn_back_kernel, S, F, heads),
        grid=(length // BLOCK,),
        in_specs=[pl.BlockSpec((BLOCK, heads * HD), lambda i: (i, 0))]
        + [whole(a) for a in (rot, raw, lse, pos, cosine, sine, gain_q, gain_k, gain, grad_gf, mix_t)]
        + [ANY] * 5,
        out_specs=[pl.BlockSpec((F, total, 128), lambda i: (0, 0, 0)), pl.BlockSpec((T, width), lambda i: (0, 0))],
        out_shape=[shape((F, total, 128)), shape((T, width), f32)],
        scratch_shapes=[
            pltpu.VMEM((length, HD), bf16),
            pltpu.VMEM((length, HD), bf16),
            pltpu.VMEM((length, HD), f32),
            pltpu.VMEM((length, HD), f32),
            pltpu.VMEM((HD, 128), f32),
            pltpu.VMEM((length, hw), bf16),
            pltpu.VMEM((S, T, width), bf16),
            pltpu.VMEM((S, T, hw), bf16),
            pltpu.VMEM((T, width), bf16),
            pltpu.VMEM((T, width), f32),
            pltpu.VMEM(normed_t.shape, bf16),
            pltpu.VMEM(wqkv_all.shape, bf16),
            DMA((S - 1,)),
            DMA((S - 1,)),
            DMA((4,)),
        ]
        + Gather.sems(S, d_attn),
        compiler_params=params(collective, 1),
        cost_estimate=cost(1),
    )(dmix, rot, raw, lse, pos, cosine, sine, gain_q, gain_k, gain, grad_gf, mix_t, x, gm, normed_t, wqkv_all, d_attn)


def output_kernel(S, F, hid_ref, wd_ref, mid_ref, gu_hbm, down_hbm, out_ref, down_out, *refs):
    count = len(refs) - 10
    grads = refs[:count]
    got, acc, send_buf, recv_buf, send, recv, gu_send, gu_recv, gu_own, far = refs[count:]
    s, f = lax.axis_index("sp"), lax.axis_index("fsdp")
    T, width = mid_ref.shape
    tile = 512
    block, mine = f * S + s, s * F + f
    far_send = push(down_hbm, down_out, far.at[0], far.at[1], {"sp": block // F, "fsdp": lax.rem(block, F)})
    far_keep = pltpu.make_async_copy(down_hbm, down_out, far.at[0])

    barrier = pltpu.get_barrier_semaphore()
    for k in range(1, S):
        pl.semaphore_signal(barrier, inc=1, device_id={"sp": lax.rem(s + k, S)}, device_id_type=MESH)

    @pl.when(block == mine)
    def _():
        pl.semaphore_wait(barrier, S - 1)
        far_keep.start()

    @pl.when(block != mine)
    def _():
        source = {"sp": lax.rem(mine, S), "fsdp": mine // S}
        pl.semaphore_signal(barrier, inc=1, device_id=source, device_id_type=MESH)
        pl.semaphore_wait(barrier, S)
        far_send.start()

    def exchange(k, slot):
        return to_peer(gu_hbm.at[lax.rem(s + k, S)], got.at[slot], gu_send.at[k - 1], gu_recv.at[k - 1], k, S)

    own = pltpu.make_async_copy(gu_hbm.at[s], got.at[s], gu_own)
    own.start()

    def compute(chunk, out):
        rows = hid_ref[pl.ds(pl.multiple_of(chunk * T, T), T), :]
        for c in range(0, width, tile):
            out[:, c : c + tile] = dot(rows, wd_ref[:, c : c + tile]).astype(out.dtype)

    for k in range(1, S):
        exchange(k, s).start()
    copies = sum_over_sp(S, compute, acc, send_buf, recv_buf, send, recv)
    out_ref[...] = (mid_ref[...] + acc[...]).astype(bf16)
    own.wait()
    for k in range(1, S):
        exchange(k, lax.rem(s + S - k, S)).wait_recv()
    if count == 2:
        FFs = got.shape[3]
        piece = FFs // F
        for n in range(2):
            for j in range(S):
                for m in range(F):
                    at = (m * S + j) * piece
                    grads[n][:, at : at + piece] = got[j, n, :, m * piece : (m + 1) * piece].astype(f32)
    else:
        grads[0][...] = got[...]
    for copy in copies:
        copy.wait_send()
    for k in range(1, S):
        exchange(k, s).wait_send()

    @pl.when(block == mine)
    def _():
        far_keep.wait()

    @pl.when(block != mine)
    def _():
        far_send.wait_send()
        far_send.wait_recv()


def output_rows(S, F, hidden, w_dn, mid, grad_gu, down, collective):
    T, width = mid.shape
    _, _, rows_d, FFs = grad_gu.shape
    FF = FFs * S
    n = max(6, S - 1)
    if FFs // F % 128:
        grads = [shape(grad_gu.shape)]
    else:
        grads = [shape((rows_d, FF), f32)] * 2
    got = pl.pallas_call(
        functools.partial(output_kernel, S, F),
        in_specs=[VMEM] * 3 + [ANY] * 2,
        out_specs=[VMEM, ANY] + [VMEM] * len(grads),
        out_shape=[shape((T, width)), shape(down.shape)] + grads,
        scratch_shapes=[
            pltpu.VMEM(grad_gu.shape, bf16),
            pltpu.VMEM((T, width), f32),
            pltpu.VMEM((S - 1, T, width), bf16),
            pltpu.VMEM((S - 1, T, width), bf16),
            DMA((n,)),
            DMA((n,)),
            DMA((S - 1,)),
            DMA((S - 1,)),
            DMA,
            DMA((2,)),
        ],
        compiler_params=params(collective),
        cost_estimate=cost(40),
    )(hidden, w_dn, mid, grad_gu, down)
    if len(grads) == 2:
        return got
    grad = jnp.transpose(got[2].reshape(S, 2, rows_d, F, FFs // F), (1, 2, 3, 0, 4)).reshape(2, rows_d, FF)
    return got[0], got[1], grad[0].astype(f32), grad[1].astype(f32)


def last_kernel(S, F, heads, mine_ref, mine_hbm, qkv_ref, out_ref, tiny_ref, got, send, recv):
    s = lax.axis_index("sp")
    W = 128
    qw = heads * HD
    QW, KW = QUERY_HEADS * HD, KV_HEADS * HD
    blocks = (qw + 2 * HD) // W
    rows_d = qkv_ref.shape[0]
    rows_o, width = out_ref.shape
    n_s = blocks * rows_d
    n_q, n_o = S * n_s, rows_o * width // W
    greet(S)

    def rows_of(j):
        return pl.ds(pl.multiple_of(j * n_s, n_s), n_s), pl.ds(pl.multiple_of(n_q + n_o + 16 * j, 16), 16)

    def exchange(k, slot, part):
        to = (slice(0, n_s), slice(n_s, n_s + 16))[part]
        n = 2 * (k - 1) + part
        src = mine_hbm.at[rows_of(lax.rem(s + k, S))[part]]
        return to_peer(src, got.at[slot, to], send.at[n], recv.at[n], k, S)

    for k in range(1, S):
        for part in range(2):
            exchange(k, s, part).start()
    main, small = rows_of(s)
    got[s, :n_s] = mine_ref[main, :]
    got[s, n_s:] = mine_ref[small, :]
    for c in range(0, width // W, 2):
        rows = mine_ref[n_q + c * rows_o : n_q + (c + 2) * rows_o, :].astype(f32)
        out_ref[:, c * W : (c + 1) * W] = rows[:rows_o]
        out_ref[:, (c + 1) * W : (c + 2) * W] = rows[rows_o:]
    for k in range(1, S):
        for part in range(2):
            exchange(k, lax.rem(s + S - k, S), part).wait_recv()
    copies = max(1, S // KV_HEADS)
    tiny = jnp.zeros((16, W), f32)
    kvs = []
    for j in range(S):
        for cb in range(blocks - 1):
            at = j * qw + cb * W
            qkv_ref[:, at : at + W] = got[j, cb * rows_d : (cb + 1) * rows_d].astype(f32)
        kv = got[j, (blocks - 1) * rows_d : blocks * rows_d].astype(f32)
        if j % copies:
            kvs[-1] = kvs[-1] + kv
        else:
            kvs.append(kv)
        tiny += got[j, n_s : n_s + 16].astype(f32)
    for h in range(0, KV_HEADS, 2):
        at = QW + h * HD
        qkv_ref[:, at : at + W] = jnp.concatenate([kvs[h][:, :HD], kvs[h + 1][:, :HD]], axis=1)
        qkv_ref[:, at + KW : at + KW + W] = jnp.concatenate([kvs[h][:, HD:], kvs[h + 1][:, HD:]], axis=1)
    tiny_ref[...] = tiny
    for k in range(1, S):
        for part in range(2):
            exchange(k, s, part).wait_send()


def last_exchange(S, F, mine, rows_d, rows_o, width, heads, collective):
    n_s = rows_d * (heads + 2) * HD // 128
    return pl.pallas_call(
        functools.partial(last_kernel, S, F, heads),
        in_specs=[VMEM, ANY],
        out_specs=[VMEM] * 3,
        out_shape=[
            shape((rows_d, (QUERY_HEADS + 2 * KV_HEADS) * HD), f32),
            shape((rows_o, width), f32),
            shape((16, 128), f32),
        ],
        scratch_shapes=[pltpu.VMEM((S, n_s + 16, 128), bf16), DMA((2 * (S - 1),)), DMA((2 * (S - 1),))],
        compiler_params=params(collective),
        cost_estimate=cost(10),
    )(mine, mine)


def ordered(value, *after):
    return lax.optimization_barrier((value,) + after)[0]


def local(x_own, positions, ct_own, w_qkv, w_out, w_gate, w_up, w_down, gain_attn, gain_ffn, gain_query, gain_key):
    S, F = lax.axis_size("sp"), lax.axis_size("fsdp")
    s = lax.axis_index("sp")
    _, T, D = x_own.shape
    L = positions.shape[1]
    heads = QUERY_HEADS // S
    qw = heads * HD
    hw = qw + 2 * HD
    FFs = w_gate.shape[1] // S
    rows_d = D // (S * F)
    rows_o = qw // F
    x_own = x_own[0]
    ct_own = ct_own[0]

    def gather_z(w):
        return lax.all_gather(w, "fsdp", axis=0, tiled=True)

    def reduce_z(w):
        return lax.psum_scatter(w, "fsdp", scatter_dimension=0, tiled=True)

    gu_part = own_columns(S, F, s, w_gate, w_up)
    w_gu = gather_z(gu_part).reshape(F, 2, D // F, FFs)
    rows_w = w_down.shape[0] // S
    w_dn = gather_z(lax.dynamic_slice_in_dim(w_down, s * rows_w, rows_w, 0))

    x_all, wqkv_s, wout_s, gains, cosine, sine = first_gathers(
        S, F, x_own, ordered(w_qkv, gu_part), w_out, gain_attn[None], gain_ffn[None], positions, heads, 0
    )
    x_all = x_all.reshape(L, D)
    wqkv_s = wqkv_s.reshape(D, hw)
    gain_q = gain_query.astype(f32)[:, None]
    gain_k = gain_key.astype(f32)[:, None]
    normed_t, raw, rot, lse, mix_t, mix_all, wout_all = forward_attention(
        S, x_all, gains, wqkv_s, positions, cosine, sine, gain_q, gain_k, wout_s, heads, 1
    )
    wout_all = wout_all.reshape(S, qw, D)
    mid, ffn_in, ffn_t, ct1 = middle_rows(S, x_all, mix_all, wout_all, gains, ct_own, 2)
    ct1 = ct1.reshape(L, D // 2)
    gate, up, hidden, part_down, ct0 = ffn_forward(S, ffn_in, ct1, w_gu, ct_own, 3)
    ct0 = ct0.reshape(L, D // 2)
    grad_down = reduce_z(part_down)
    dgu, part_gu, wqkv_all = ffn_backward(S, F, ct0, ct1, w_dn, gate, up, ffn_t, wqkv_s, 4)
    grad_gu = reduce_z(part_gu.reshape(2 * D, FFs))
    gm, d_attn, grad_gf, d_mix = middle_back(S, dgu, w_gu, wout_all, mid, gains, ct_own, 5)
    packed, grad_input = attention_back(
        S, F, ordered(d_mix, grad_down), rot, raw, lse, positions, cosine, sine, gain_q, gain_k,
        gains, grad_gf, mix_t, x_own, gm, normed_t, wqkv_all, d_attn, heads, 6,
    )
    mine = reduce_z(ordered(packed.reshape(-1, 128), grad_gu))
    out, grad_down, grad_gate, grad_up = output_rows(
        S, F, ordered(hidden, packed), w_dn, mid, grad_gu.reshape(S, 2, rows_d, FFs), grad_down, 7
    )
    grad_qkv, grad_out, tiny = last_exchange(S, F, mine, rows_d, rows_o, D, heads, 8)
    return (
        out[None],
        grad_input[None],
        grad_qkv,
        grad_out,
        grad_gate,
        grad_up,
        grad_down.astype(f32),
        tiny[0, :rows_d],
        tiny[0, rows_d : 2 * rows_d],
        tiny[1, :HD],
        tiny[1, HD:],
    )


def solution(mesh):
    row = P("fsdp", "sp", None)
    shard = P("fsdp", None)
    grad = P(("sp", "fsdp"), None)
    return jax.shard_map(
        local,
        mesh=mesh,
        in_specs=(row, shard, row, shard, shard, shard, shard, shard, P("fsdp"), P("fsdp"), P(), P()),
        out_specs=(row, row, grad, grad, grad, grad, grad, P(("sp", "fsdp")), P(("sp", "fsdp")), P(), P()),
        check_vma=False,
    )
```

```python
import functools

import jax
import jax.numpy as jnp
import numpy as np
from jax import lax
from jax.experimental import pallas as pl
from jax.experimental.pallas import tpu as pltpu
from jax.sharding import PartitionSpec as P

QUERY_HEADS = 16
KV_HEADS = 4
HD = 64
EPS = 1e-06
BLOCK = 256
VMEM_LIMIT = 60 << 20
MESH = pl.DeviceIdType.MESH
f32 = jnp.float32
bf16 = jnp.bfloat16


def params(collective=None, grid=0):
    return pltpu.CompilerParams(
        dimension_semantics=("arbitrary",) * grid if grid else None,
        vmem_limit_bytes=VMEM_LIMIT,
        collective_id=collective,
        has_side_effects=collective is not None,
    )


def cost(micros):
    return pl.CostEstimate(flops=0, bytes_accessed=int(micros * 3_600_000), transcendentals=0)


ANY = pl.BlockSpec(memory_space=pl.ANY)
VMEM = pl.BlockSpec(memory_space=pltpu.VMEM)
DMA = pltpu.SemaphoreType.DMA


def shape(dims, dtype=bf16):
    return jax.ShapeDtypeStruct(dims, dtype)


def dot(a, b):
    return jnp.dot(a, b, preferred_element_type=f32)


def dot_nt(a, b):
    return lax.dot_general(a, b, (((1,), (1,)), ((), ())), preferred_element_type=f32)


def sibling():
    f = lax.axis_index("fsdp")
    return {"fsdp": f + 1 - 2 * lax.rem(f, 2)}


def greet(S, F=0, with_sibling=False):
    s, f = lax.axis_index("sp"), lax.axis_index("fsdp")
    where = [{"sp": lax.rem(s + k, S)} for k in range(1, S)]
    where += [{"fsdp": lax.rem(f + 2 * k, F)} for k in range(1, F // 2)]
    if with_sibling:
        where.append(sibling())
    barrier = pltpu.get_barrier_semaphore()
    for target in where:
        pl.semaphore_signal(barrier, inc=1, device_id=target, device_id_type=MESH)
    pl.semaphore_wait(barrier, len(where))


def gain_row(g_ref, n):
    return jnp.concatenate([g_ref[j].astype(f32)[n : n + 1] for j in range(g_ref.shape[0])], axis=1)


def to_peer(src, dst, send, recv, k, S):
    s = lax.axis_index("sp")
    return pltpu.make_async_remote_copy(
        src_ref=src, dst_ref=dst, send_sem=send, recv_sem=recv, device_id={"sp": lax.rem(s + k, S)}, device_id_type=MESH
    )


def mates(s):
    return s + 1 - 2 * lax.rem(s, 2), lax.rem(s + 2, 4), 3 - s


def push(src, dst, send, recv, where):
    return pltpu.make_async_remote_copy(
        src_ref=src, dst_ref=dst, send_sem=send, recv_sem=recv, device_id=where, device_id_type=MESH
    )


class Gather:
    def __init__(self, S, src, dst, sems, halves=False, inner=False, staged=True):
        self.S, self.src, self.halves = S, src, halves
        self.slot = (lambda j: dst.at[:, j]) if inner else (lambda j: dst.at[j])
        self.stage = sems[-1] if staged else None
        self.send, self.recv, self.own = sems[:3]
        self.swap_send, self.swap_recv = sems[3:5] if halves else (None, None)
        self.s, self.f = lax.axis_index("sp"), lax.axis_index("fsdp")
        self.rows = src.shape[0] // (2 if halves else 1)
        self.size = self.rows // 2 if S == 4 else self.rows

    @staticmethod
    def sems(S, chunk, halves=False):
        count = 6 if S == 4 else S - 1
        base = [DMA((count,)), DMA((count,)), DMA((2,))]
        base += [DMA((S - 1,)), DMA((S - 1,))] if halves else []
        return base if chunk is None else base + [pltpu.VMEM(chunk.shape, chunk.dtype)]

    def base(self, mine=True):
        if not self.halves:
            return 0
        core = lax.rem(self.f, 2)
        return (core if mine else 1 - core) * self.rows

    def piece(self, ref, n):
        return ref.at[pl.ds(self.base() + n * self.size, self.size)]

    def share(self, slot, mine):
        if not self.halves:
            return self.slot(slot)
        return self.slot(slot).at[pl.ds(self.base(mine), self.rows)]

    def steps(self):
        s, S = self.s, self.S
        if S != 4:
            return [(self.src, s, lax.rem(s + S - k, S), 0, lax.rem(s + k, S)) for k in range(1, S)]
        x, y, d = mates(s)
        return [
            (self.src, s, x, 0, x),
            (self.src, s, y, 1, y),
            (self.src, s, x, 1, x),
            (self.src, s, y, 0, y),
            (self.slot(x), x, d, 0, y),
            (self.slot(y), y, d, 1, x),
        ]

    def copy(self, n, here):
        src, there, lands, piece, target = self.steps()[n]
        slot = lands if here else there
        return push(
            self.piece(src, piece), self.piece(self.slot(slot), piece), self.send.at[n], self.recv.at[n], {"sp": target}
        )

    def passing(self, n, mine):
        slots = mates(self.s) if self.S == 4 else [lax.rem(self.s + self.S - k, self.S) for k in range(1, self.S)]
        return push(
            self.share(slots[n], True), self.share(slots[n], mine), self.swap_send.at[n], self.swap_recv.at[n], sibling()
        )

    def local(self, out):
        if self.stage is None:
            return pltpu.make_async_copy(self.src, self.slot(self.s), self.own.at[0])
        if out:
            return pltpu.make_async_copy(self.stage, self.slot(self.s), self.own.at[1])
        return pltpu.make_async_copy(self.src, self.stage, self.own.at[0])

    def start(self):
        for n in range(4 if self.S == 4 else self.S - 1):
            self.copy(n, False).start()
        self.local(False).start()

    def relay(self):
        if self.stage is not None:
            self.local(False).wait()
            self.local(True).start()
        if self.S == 4:
            for n in range(2):
                self.copy(n, True).wait_recv()
                self.copy(4 + n, False).start()

    def spread(self):
        if self.S == 4:
            for n in range(2):
                self.copy(2 + n, True).wait_recv()
                if self.halves:
                    self.passing(n, True).start()

    def finish(self, relayed=False, spread=False):
        if not relayed:
            self.relay()
        if not spread:
            self.spread()
        ready = {5: 2} if self.S == 4 else {n: n for n in range(self.S - 1)}
        for n in range(4 if self.S == 4 else 0, len(self.steps())):
            self.copy(n, True).wait_recv()
            if self.halves and n in ready:
                self.passing(ready[n], True).start()
        self.local(True).wait()
        for n in range(len(self.steps())):
            self.copy(n, False).wait_send()
        if self.halves:
            for n in range(self.S - 1):
                self.passing(n, True).wait_send()
                self.passing(n, False).wait_recv()


class GatherZ:
    def __init__(self, F, src, dst, sems):
        self.F, self.src, self.dst = F, src, dst
        self.send, self.recv, self.pass_send, self.pass_recv, self.own = sems
        self.f = lax.axis_index("fsdp")

    @staticmethod
    def sems(F):
        return [DMA((F // 2 - 1,)), DMA((F // 2 - 1,)), DMA((F // 2,)), DMA((F // 2,)), DMA]

    def sending(self, k):
        return push(
            self.src, self.dst.at[self.f], self.send.at[k - 1], self.recv.at[k - 1], {"fsdp": lax.rem(self.f + 2 * k, self.F)}
        )

    def landing(self, k):
        slot = lax.rem(self.f + self.F - 2 * k, self.F)
        return push(
            self.src, self.dst.at[slot], self.send.at[k - 1], self.recv.at[k - 1], {"fsdp": lax.rem(self.f + 2 * k, self.F)}
        )

    def passing(self, k, mine):
        f, F = self.f, self.F
        slot = lax.rem(f + F - 2 * k, F)
        other = f + 1 - 2 * lax.rem(f, 2)
        there = slot if mine else lax.rem(other + F - 2 * k, F)
        src = self.src if k == 0 else self.dst.at[slot]
        return push(src, self.dst.at[there], self.pass_send.at[k], self.pass_recv.at[k], sibling())

    def local(self):
        return pltpu.make_async_copy(self.src, self.dst.at[self.f], self.own)

    def start(self):
        for k in range(1, self.F // 2):
            self.sending(k).start()
        self.passing(0, True).start()
        self.local().start()

    def finish(self):
        for k in range(1, self.F // 2):
            self.landing(k).wait_recv()
            self.passing(k, True).start()
        self.local().wait()
        for k in range(1, self.F // 2):
            self.sending(k).wait_send()
        for k in range(self.F // 2):
            self.passing(k, True).wait_send()
            self.passing(k, False).wait_recv()


def first_kernel(S, F, heads, x_ref, wqkv_ref, ga_ref, gf_ref, pos_ref, freq_ref, x_all, wqkv_all, gains_all, cos_ref, sin_ref, part, gains, *sems):
    s = lax.axis_index("sp")
    qw = heads * HD
    QW, KW = QUERY_HEADS * HD, KV_HEADS * HD
    kv = s // max(1, S // KV_HEADS)
    pair = kv // 2
    high = lax.rem(kv, 2)

    def cut(start):
        block = wqkv_ref[:, pl.ds(pl.multiple_of(start + pair * 128, 128), 128)].astype(f32)
        return jnp.where(high == 1, block[:, HD:], block[:, :HD])

    part[:, :qw] = wqkv_ref[:, pl.ds(pl.multiple_of(s * qw, 128), qw)]
    part[:, qw:] = jnp.concatenate([cut(QW), cut(QW + KW)], axis=1).astype(bf16)
    pad = jnp.zeros((14, ga_ref.shape[1]), f32)
    gains[...] = jnp.concatenate([ga_ref[...].astype(f32), gf_ref[...].astype(f32), pad], axis=0).astype(bf16)
    n = len(Gather.sems(S, shape((1, 1))))
    m = len(GatherZ.sems(F))
    move_x = Gather(S, x_ref, x_all, sems[:n])
    moves_z = [
        GatherZ(F, part, wqkv_all, sems[n : n + m]),
        GatherZ(F, gains, gains_all, sems[n + m :]),
    ]
    greet(S, F, True)
    move_x.start()
    for move in moves_z:
        move.start()
    angles = freq_ref[...] * pos_ref[...].astype(f32)
    cos_ref[...] = jnp.cos(angles)
    sin_ref[...] = jnp.sin(angles)
    move_x.relay()
    for move in moves_z:
        move.finish()
    move_x.finish(True)


def first_gathers(S, F, x, w_qkv, gain_attn, gain_ffn, positions, heads, collective):
    T, width = x.shape
    depth = w_qkv.shape[0]
    hw = (heads + 2) * HD
    length = positions.shape[1]
    frequency = jnp.asarray(10000.0 ** (-2.0 * np.arange(HD // 2) / HD), f32)[:, None]
    table = shape((HD // 2, length), f32)
    return pl.pallas_call(
        functools.partial(first_kernel, S, F, heads),
        in_specs=[ANY] + [VMEM] * 5,
        out_specs=[ANY] * 3 + [VMEM] * 2,
        out_shape=[
            shape((S, T, width)),
            shape((F, depth, hw)),
            shape((F, 16, depth)),
            table,
            table,
        ],
        scratch_shapes=[pltpu.VMEM((depth, hw), bf16), pltpu.VMEM((16, depth), bf16)]
        + Gather.sems(S, x)
        + GatherZ.sems(F) * 2,
        compiler_params=params(collective),
        cost_estimate=cost(45),
    )(x, w_qkv, gain_attn, gain_ffn, positions, frequency)


def columns_kernel(S, F, gate_hbm, up_hbm, out_hbm, buf, sem_in, sem_out):
    s = lax.axis_index("sp")
    piece = buf.shape[2] // F
    ins = []
    for n, ref in enumerate((gate_hbm, up_hbm)):
        for m in range(F):
            src = ref.at[:, pl.ds(pl.multiple_of((m * S + lax.rem(s + m // 2, S)) * piece, piece), piece)]
            ins.append(pltpu.make_async_copy(src, buf.at[n, :, pl.ds(m * piece, piece)], sem_in.at[n * F + m]))
    for copy in ins:
        copy.start()
    outs = []
    for n in range(2):
        for copy in ins[n * F : (n + 1) * F]:
            copy.wait()
        outs.append(pltpu.make_async_copy(buf.at[n], out_hbm.at[n], sem_out.at[n]))
        outs[-1].start()
    for copy in outs:
        copy.wait()


def own_columns(S, F, s, w_gate, w_up):
    depth, FF = w_gate.shape
    piece = FF // (S * F)
    if piece % 128:
        def pick(w):
            starts = [(m * S + lax.rem(s + m // 2, S)) * piece for m in range(F)]
            return jnp.concatenate([lax.dynamic_slice_in_dim(w, at, piece, 1) for at in starts], axis=1)

        return jnp.stack([pick(w_gate), pick(w_up)])
    return pl.pallas_call(
        functools.partial(columns_kernel, S, F),
        in_specs=[ANY, ANY],
        out_specs=ANY,
        out_shape=shape((2, depth, FF // S)),
        scratch_shapes=[pltpu.VMEM((2, depth, FF // S), bf16), DMA((2 * F,)), DMA((2,))],
        compiler_params=params(),
        cost_estimate=cost(3),
    )(w_gate, w_up)


def forward_kernel(S, F, heads, x_ref, g_ref, w_ref, pos_ref, cos_ref, sin_ref, gq_ref, gk_ref, wout_ref, ct_ref, normed_t_ref, raw_ref, rot_ref, lse_ref, mix_t_ref, mix_all, wout_all, ct_all, k_buf, vt_buf, mix_buf, mix_send, mix_recv, mix_own, wout_s, *sems):
    i = pl.program_id(0)
    s = lax.axis_index("sp")
    qw = heads * HD
    half = HD // 2
    blocks = pl.num_programs(0)
    n_z = len(GatherZ.sems(F))
    rows_o = wout_s.shape[1]
    own_out = wout_ref.at[pl.ds(pl.multiple_of(s * rows_o, rows_o), rows_o)]
    move_z = GatherZ(F, own_out, wout_s, sems[:n_z])
    n_w = n_z + len(Gather.sems(S, None, True))
    move = Gather(S, wout_s, wout_all, sems[n_z:n_w], halves=True, inner=True, staged=False)
    move_ct = Gather(S, ct_ref.at[:, pl.ds(0, ct_all.shape[2])], ct_all, sems[n_w:])

    @pl.when(i == 0)
    def _():
        greet(S, F, True)
        move_z.start()
        move_ct.start()

    @pl.when(i == blocks - 1)
    def _():
        move_ct.relay()

    x = x_ref[...].astype(f32)
    scale = lax.rsqrt(jnp.mean(x * x, axis=-1, keepdims=True) + EPS)
    scaled = x * scale * gain_row(g_ref, 0)
    normed = scaled.astype(bf16)
    normed_t_ref[...] = scaled.T.astype(bf16)
    raw = dot(normed, w_ref[...]).T
    raw_ref[...] = raw
    cosine, sine = cos_ref[...], sin_ref[...]

    def prep(u, gain):
        n = u * lax.rsqrt(jnp.mean(u * u, axis=0, keepdims=True) + EPS) * gain
        front, back = n[:half], n[half:]
        return jnp.concatenate([front * cosine - back * sine, back * cosine + front * sine], axis=0)

    q = [prep(raw[h * HD : (h + 1) * HD], gq_ref[...]).astype(bf16) for h in range(heads)]
    kt = prep(raw[qw : qw + HD], gk_ref[...])
    vt = raw[qw + HD :].astype(bf16)
    rot_ref[...] = jnp.concatenate(q + [kt.astype(bf16), vt], axis=0)
    steps = mix_buf.shape[0]

    x_mate, y_mate, d_mate = mates(s)

    def mix_copy(block, k, here):
        rows = pl.ds(block * BLOCK, BLOCK)
        n = block * (S - 1) + k - 1
        if S != 4:
            slot = lax.rem(s + S - k, S) if here else s
            return push(mix_buf.at[block], mix_all.at[slot, rows], mix_send.at[n], mix_recv.at[n], {"sp": lax.rem(s + k, S)})
        if k < 3:
            mate = x_mate if k == 1 else y_mate
            slot = mate if here else s
            return push(mix_buf.at[block], mix_all.at[slot, rows], mix_send.at[n], mix_recv.at[n], {"sp": mate})
        source, mate = (x_mate, y_mate) if block < steps // 2 else (y_mate, x_mate)
        slot = d_mate if here else source
        return push(mix_all.at[source, rows], mix_all.at[slot, rows], mix_send.at[n], mix_recv.at[n], {"sp": mate})

    def mix_local(block):
        return pltpu.make_async_copy(mix_buf.at[block], mix_all.at[s, pl.ds(block * BLOCK, BLOCK)], mix_own.at[block])

    for step in range(steps):

        @pl.when(i == step)
        def _():
            n = (step + 1) * BLOCK
            k_buf[step * BLOCK : n, :] = kt.T.astype(bf16)
            vt_buf[:, step * BLOCK : n] = vt
            col = lax.broadcasted_iota(jnp.int32, (n, BLOCK), 0)
            row = step * BLOCK + lax.broadcasted_iota(jnp.int32, (n, BLOCK), 1)
            bias = jnp.where((col <= row) & (row - col <= pos_ref[...]), 0.0, -1e30)
            keys, values = k_buf[:n, :], vt_buf[:, :n]
            mixes, lses = [], []
            for h in range(heads):
                e = jnp.exp(dot(keys, q[h] * 0.125) + bias)
                total = jnp.sum(e, axis=0, keepdims=True)
                p = (e * (1.0 / total)).astype(bf16)
                mixes.append(dot(values, p))
                lses.append(jnp.log(total))
            mix = jnp.concatenate(mixes, axis=0)
            mix_t_ref[...] = mix.astype(bf16)
            lse_ref[...] = jnp.concatenate(lses + [jnp.zeros((8 - heads, BLOCK), f32)], axis=0)
            mix_buf[step] = mix.T.astype(bf16)
            for k in range(1, 3 if S == 4 else S):
                mix_copy(step, k, False).start()
            mix_local(step).start()

    @pl.when(i == blocks - 1)
    def _():
        move_z.finish()
        move.start()
        for block in range(steps):
            for k in range(1, 3 if S == 4 else S):
                mix_copy(block, k, True).wait_recv()
                if S == 4 and k == (1 if block < steps // 2 else 2):
                    mix_copy(block, 3, False).start()
        move.relay()
        for block in range(steps):
            if S == 4:
                mix_copy(block, 3, True).wait_recv()
            for k in range(1, S):
                mix_copy(block, k, False).wait_send()
            mix_local(block).wait()
        move.finish(True)
        move_ct.finish(True)


def forward_attention(S, F, x, gain, w, pos, cosine, sine, gain_q, gain_k, wout, ct, heads, collective):
    length, width = x.shape
    hw = w.shape[1]
    qw = heads * HD
    steps = length // BLOCK
    full = lambda i: (0, 0)
    rows = lambda i: (i, 0)
    cols = lambda i: (0, i)
    return pl.pallas_call(
        functools.partial(forward_kernel, S, F, heads),
        grid=(steps,),
        in_specs=[
            pl.BlockSpec((BLOCK, width), rows),
            pl.BlockSpec(gain.shape, lambda i: (0, 0, 0)),
            pl.BlockSpec((width, hw), full),
            pl.BlockSpec((1, BLOCK), cols),
            pl.BlockSpec((HD // 2, BLOCK), cols),
            pl.BlockSpec((HD // 2, BLOCK), cols),
            pl.BlockSpec((HD, 1), full),
            pl.BlockSpec((HD, 1), full),
            pl.BlockSpec(wout.shape, full),
            ANY,
        ],
        out_specs=[
            pl.BlockSpec((width, BLOCK), cols),
            pl.BlockSpec((hw, BLOCK), cols),
            pl.BlockSpec((hw, BLOCK), cols),
            pl.BlockSpec((8, BLOCK), cols),
            pl.BlockSpec((qw, BLOCK), cols),
            ANY,
            ANY,
            ANY,
        ],
        out_shape=[
            shape((width, length)),
            shape((hw, length), f32),
            shape((hw, length)),
            shape((8, length), f32),
            shape((qw, length)),
            shape((S, length, qw)),
            shape((F, S, wout.shape[0] // S, width)),
            shape((S,) + ct.shape[:1] + (width // 2,)),
        ],
        scratch_shapes=[
            pltpu.VMEM((length, HD), bf16),
            pltpu.VMEM((HD, length), bf16),
            pltpu.VMEM((steps, BLOCK, qw), bf16),
            DMA((steps * (S - 1),)),
            DMA((steps * (S - 1),)),
            DMA((steps,)),
            pltpu.VMEM((F, wout.shape[0] // S, width), bf16),
        ]
        + GatherZ.sems(F)
        + Gather.sems(S, None, True)
        + Gather.sems(S, shape((ct.shape[0], width // 2))),
        compiler_params=params(collective, 1),
        cost_estimate=cost(45),
    )(x, gain, w, pos, cosine, sine, gain_q, gain_k, wout, ct)


def middle_kernel(S, T, x_ref, mix_ref, wout_ref, g_ref, ct_ref, mid_ref, ffn_ref, ffn_t_ref, ct_all, *sems):
    i = pl.program_id(0)
    s = lax.axis_index("sp")
    move = Gather(S, ct_ref.at[:, pl.ds(ct_all.shape[2], ct_all.shape[2])], ct_all, sems)

    @pl.when(i == 0)
    def _():
        greet(S)
        move.start()

    @pl.when(i == pl.num_programs(0) - 1)
    def _():
        move.relay()

    middle = x_ref[...].astype(f32)
    total = dot(mix_ref[0], wout_ref[0])
    for j in range(1, S):
        total += dot(mix_ref[j], wout_ref[j])
    middle = middle + total

    @pl.when(i == s)
    def _():
        mid_ref[...] = middle

    scaled = middle * lax.rsqrt(jnp.mean(middle * middle, axis=-1, keepdims=True) + EPS) * gain_row(g_ref, 1)
    ffn_ref[...] = scaled.astype(bf16)
    ffn_t_ref[...] = scaled.T.astype(bf16)

    @pl.when(i == pl.num_programs(0) - 1)
    def _():
        move.finish(True)


def middle_rows(S, x, mix_all, wout_all, gain, ct, collective):
    length, width = x.shape
    T = length // S
    qw = mix_all.shape[2]
    return pl.pallas_call(
        functools.partial(middle_kernel, S, T),
        grid=(S,),
        in_specs=[
            pl.BlockSpec((T, width), lambda i: (i, 0)),
            pl.BlockSpec((S, T, qw), lambda i: (0, i, 0)),
            pl.BlockSpec((S, qw, width), lambda i: (0, 0, 0)),
            pl.BlockSpec(gain.shape, lambda i: (0, 0, 0)),
            ANY,
        ],
        out_specs=[
            pl.BlockSpec((T, width), lambda i: (0, 0)),
            pl.BlockSpec((T, width), lambda i: (i, 0)),
            pl.BlockSpec((width, T), lambda i: (0, i)),
            ANY,
        ],
        out_shape=[shape((T, width), f32), shape((length, width)), shape((width, length)), shape((S, T, width // 2))],
        scratch_shapes=Gather.sems(S, shape((T, width // 2))),
        compiler_params=params(collective, 1),
        cost_estimate=cost(45),
    )(x, mix_all, wout_all, gain, ct)


def ffn_kernel(S, F, ffn_ref, ct0_ref, ct1_ref, wg_ref, wu_ref, gate_ref, up_ref, hid_ref, down_ref):
    i = pl.program_id(0)
    s = lax.axis_index("sp")
    length, width = ffn_ref.shape
    half = width // 2
    rows = ffn_ref[...]
    gate, up = dot(rows, wg_ref[...].reshape(width, BLOCK)), dot(rows, wu_ref[...].reshape(width, BLOCK))
    gate_ref[...] = gate
    up_ref[...] = up
    hidden = gate / (1.0 + jnp.exp(-gate)) * up
    hid_ref[...] = hidden.astype(bf16)
    flipped = hidden.T.astype(bf16)
    piece = down_ref.shape[1]
    for n, ref in enumerate((ct0_ref, ct1_ref)):
        part = dot(flipped, ref[...]).astype(bf16)
        for m in range(BLOCK // piece):
            block = i * (BLOCK // piece) + m
            owner = lax.rem(block, 2) * S + lax.rem(s + block // 2, S)
            down_ref[owner, :, n * half : (n + 1) * half] = part[m * piece : (m + 1) * piece]


def ffn_forward(S, ffn_in, ct0, ct1, w_gu):
    length, width = ffn_in.shape
    F, _, depth, FFs = w_gu.shape
    whole = lambda i: (0, 0)
    col = pl.BlockSpec((length, BLOCK), lambda i: (0, i))
    return pl.pallas_call(
        functools.partial(ffn_kernel, S, F),
        grid=(FFs // BLOCK,),
        in_specs=[
            pl.BlockSpec((length, width), whole),
            pl.BlockSpec((length, width // 2), whole),
            pl.BlockSpec((length, width // 2), whole),
            pl.BlockSpec((F, 1, depth, BLOCK), lambda i: (0, 0, 0, i)),
            pl.BlockSpec((F, 1, depth, BLOCK), lambda i: (0, 1, 0, i)),
        ],
        out_specs=[col, col, col, pl.BlockSpec((F, FFs // F, width), lambda i: (0, 0, 0))],
        out_shape=[
            shape((length, FFs), f32),
            shape((length, FFs), f32),
            shape((length, FFs)),
            shape((F, FFs // F, width)),
        ],
        compiler_params=params(None, 1),
        cost_estimate=cost(20),
    )(ffn_in, ct0, ct1, w_gu, w_gu)


def ffn_back_kernel(S, F, ct0_ref, ct1_ref, wd_ref, gate_ref, up_ref, ffn_t_ref, wqkv_ref, dgu_ref, pgu_ref, wqkv_all, *sems):
    i = pl.program_id(0)
    last = pl.num_programs(0) - 1
    move = Gather(S, wqkv_ref, wqkv_all, sems, halves=True)

    @pl.when(i == 0)
    def _():
        greet(S, 0, True)
        move.start()

    @pl.when(i == last - 1)
    def _():
        move.relay()

    @pl.when(i == last)
    def _():
        move.spread()

    half = ct0_ref.shape[1]
    gh = dot_nt(ct0_ref[...], wd_ref[:, :half]) + dot_nt(ct1_ref[...], wd_ref[:, half:])
    gate, up = gate_ref[...], up_ref[...]
    sig = 1.0 / (1.0 + jnp.exp(-gate))
    d_gate = (gh * up * sig * (1.0 + gate * (1.0 - sig))).astype(bf16)
    d_up = (gh * (gate * sig)).astype(bf16)
    dgu_ref[0] = d_gate
    dgu_ref[1] = d_up
    ffn_t = ffn_t_ref[...]
    rows = pgu_ref.shape[3]
    for n, d in enumerate((d_gate, d_up)):
        part = dot(ffn_t, d).astype(bf16)
        for j in range(S):
            for m in range(F):
                pgu_ref[m, j, n] = part[(j * F + m) * rows : (j * F + m + 1) * rows]

    @pl.when(i == last)
    def _():
        move.finish(True, True)


def ffn_backward(S, F, ct0, ct1, w_dn, gate, up, ffn_t, wqkv_s, collective):
    length, FFs = gate.shape
    width = w_dn.shape[1]
    tiles = FFs // BLOCK
    rows = width // (S * F)
    whole = lambda i: (0, 0)
    col = lambda i: (0, i)
    return pl.pallas_call(
        functools.partial(ffn_back_kernel, S, F),
        grid=(tiles,),
        in_specs=[
            pl.BlockSpec((length, width // 2), whole),
            pl.BlockSpec((length, width // 2), whole),
            pl.BlockSpec((BLOCK, width), lambda i: (i, 0)),
            pl.BlockSpec((length, BLOCK), col),
            pl.BlockSpec((length, BLOCK), col),
            pl.BlockSpec((width, length), whole),
            ANY,
        ],
        out_specs=[
            pl.BlockSpec((2, length, BLOCK), lambda i: (0, 0, i)),
            pl.BlockSpec((F, S, 2, rows, BLOCK), lambda i: (0, 0, 0, 0, i)),
            ANY,
        ],
        out_shape=[shape((2, length, FFs)), shape((F, S, 2, rows, FFs)), shape((S,) + wqkv_s.shape)],
        scratch_shapes=Gather.sems(S, wqkv_s, True),
        compiler_params=params(collective, 1),
        cost_estimate=cost(1),
    )(ct0, ct1, w_dn, gate, up, ffn_t, wqkv_s)


def sum_over_sp(S, compute, acc, send_buf, recv_buf, send, recv, between=None):
    s = lax.axis_index("sp")
    if S != 4:

        def copy(k):
            return push(
                send_buf.at[k - 1], recv_buf.at[k - 1], send.at[k - 1], recv.at[k - 1], {"sp": lax.rem(s + k, S)}
            )

        for k in range(1, S):
            compute(lax.rem(s + k, S), send_buf.at[k - 1])
            copy(k).start()
        compute(s, acc)
        if between is not None:
            between()
        for k in range(1, S):
            copy(k).wait_recv()
            acc[...] += recv_buf[k - 1].astype(f32)
        return [copy(k) for k in range(1, S)]

    x, y, d = mates(s)
    half = acc.shape[0] // 2
    low, high = pl.ds(0, half), pl.ds(half, half)

    def copy(n):
        buf, rows, target = [(0, low, y), (0, high, x), (1, high, x), (2, low, y), (1, low, x), (2, high, y)][n]
        return push(send_buf.at[buf, rows], recv_buf.at[buf, rows], send.at[n], recv.at[n], {"sp": target})

    compute(d, send_buf.at[0])
    copy(0).start()
    copy(1).start()
    compute(x, send_buf.at[1])
    copy(2).start()
    compute(y, send_buf.at[2])
    copy(3).start()
    copy(0).wait_recv()
    send_buf[1, :half] = (send_buf[1, :half].astype(f32) + recv_buf[0, :half].astype(f32)).astype(bf16)
    copy(4).start()
    copy(1).wait_recv()
    send_buf[2, half:] = (send_buf[2, half:].astype(f32) + recv_buf[0, half:].astype(f32)).astype(bf16)
    copy(5).start()
    compute(s, acc)
    if between is not None:
        between()
    for n in range(2, 6):
        copy(n).wait_recv()
    acc[...] += recv_buf[1].astype(f32) + recv_buf[2].astype(f32)
    return [copy(n) for n in range(6)]


def middle_back_kernel(S, F, dgu_hbm, wgu_hbm, wout_hbm, mid_hbm, ct_hbm, g_ref, gm_ref, dattn_ref, gg_ref, dmix_ref, dgu, wgu, wout, mid, ct, acc, send_buf, recv_buf, send, recv, load):
    s = lax.axis_index("sp")
    T, width = mid.shape
    depth = wgu.shape[2]
    greet(S)
    if S == 4:
        x, y, d = mates(s)
        order = [d, x, y, s]
    else:
        order = [lax.rem(s + k, S) for k in range(1, S)] + [s]

    def chunk_load(n):
        rows = pl.ds(pl.multiple_of(order[n] * T, T), T)
        return pltpu.make_async_copy(dgu_hbm.at[:, rows], dgu.at[n], load.at[n])

    def weight_load(c):
        return pltpu.make_async_copy(wgu_hbm.at[c], wgu.at[c], load.at[S + c])

    others = [
        pltpu.make_async_copy(mid_hbm, mid, load.at[S + F]),
        pltpu.make_async_copy(ct_hbm, ct, load.at[S + F + 1]),
        pltpu.make_async_copy(wout_hbm, wout, load.at[S + F + 2]),
    ]
    chunk_load(0).start()
    for c in range(F):
        weight_load(c).start()
    for n in range(1, S):
        chunk_load(n).start()
    for copy in others:
        copy.start()
    calls = []

    def compute(chunk, out):
        n = len(calls)
        calls.append(n)
        chunk_load(n).wait()
        for c in range(F):
            if n == 0:
                weight_load(c).wait()
            part = dot_nt(dgu[n, 0], wgu[c, 0]) + dot_nt(dgu[n, 1], wgu[c, 1])
            out[:, c * depth : (c + 1) * depth] = part.astype(out.dtype)

    copies = sum_over_sp(S, compute, acc, send_buf, recv_buf, send, recv)
    for copy in others:
        copy.wait()
    v, e = mid[...], acc[...]
    r = lax.rsqrt(jnp.mean(v * v, axis=-1, keepdims=True) + EPS)
    gg_ref[...] = jnp.sum(e * v * r, axis=0, keepdims=True)
    ge = gain_row(g_ref, 1) * e
    gm = ct[...].astype(f32) + r * ge - v * (r * r * r * jnp.mean(ge * v, axis=-1, keepdims=True))
    gm_ref[...] = gm
    d_attn = gm.astype(bf16)
    dattn_ref[...] = d_attn

    for j in range(S):
        dmix_ref[j] = dot_nt(d_attn, wout[j]).astype(bf16)
    for copy in copies:
        copy.wait_send()


def middle_back(S, dgu, w_gu, wout_all, mid, gain, ct, collective):
    T, width = mid.shape
    F = w_gu.shape[0]
    FFs = dgu.shape[2]
    qw = wout_all.shape[1]
    n = max(6, S - 1)
    return pl.pallas_call(
        functools.partial(middle_back_kernel, S, F),
        in_specs=[ANY] * 5 + [VMEM],
        out_specs=[VMEM] * 4,
        out_shape=[shape((T, width), f32), shape((T, width)), shape((1, width), f32), shape((S, T, qw))],
        scratch_shapes=[
            pltpu.VMEM((S, 2, T, FFs), bf16),
            pltpu.VMEM(w_gu.shape, bf16),
            pltpu.VMEM(wout_all.shape, bf16),
            pltpu.VMEM((T, width), f32),
            pltpu.VMEM((T, width), bf16),
            pltpu.VMEM((T, width), f32),
            pltpu.VMEM((S - 1, T, width), bf16),
            pltpu.VMEM((S - 1, T, width), bf16),
            DMA((n,)),
            DMA((n,)),
            DMA((S + F + 3,)),
        ],
        compiler_params=params(collective),
        cost_estimate=cost(1),
    )(dgu, w_gu, wout_all, mid, ct, gain)


def attn_back_kernel(S, F, heads, rot_ref, raw_ref, lse_ref, pos_ref, cos_ref, sin_ref, gq_ref, gk_ref, g_ref, ggf_ref, mix_t_ref, x_hbm, gm_hbm, normed_hbm, wqkv_hbm, dattn_hbm, dmix_hbm, packed_ref, gin_ref, k_buf, v_buf, dk_acc, dv_acc, gg, dproj, dattn_all, got, x, gm, normed_t, wqkv, dmix_all, send, recv, load, mix_send, mix_recv, *sems):
    i = pl.program_id(0)
    s = lax.axis_index("sp")
    qw = heads * HD
    hw = qw + 2 * HD
    half = HD // 2
    length = rot_ref.shape[1]
    T, width = gin_ref.shape
    move = Gather(S, dattn_hbm, dattn_all, sems)
    loads = [
        pltpu.make_async_copy(a, b, load.at[n])
        for n, (a, b) in enumerate([(normed_hbm, normed_t), (wqkv_hbm, wqkv), (x_hbm, x), (gm_hbm, gm)])
    ]

    def mix_copy(k, slot):
        return to_peer(dmix_hbm.at[lax.rem(s + k, S)], dmix_all.at[slot], mix_send.at[k - 1], mix_recv.at[k - 1], k, S)

    mix_own = pltpu.make_async_copy(dmix_hbm.at[s], dmix_all.at[s], load.at[4])

    @pl.when(i == 0)
    def _():
        greet(S)
        for k in range(1, S):
            mix_copy(k, s).start()
        mix_own.start()
        move.start()
        for copy in loads:
            copy.start()
        k_buf[...] = rot_ref[qw : qw + HD, :].astype(f32).T.astype(bf16)
        v_buf[...] = rot_ref[qw + HD :, :].astype(f32).T.astype(bf16)
        dk_acc[...] = jnp.zeros_like(dk_acc)
        dv_acc[...] = jnp.zeros_like(dv_acc)
        gg[...] = jnp.zeros_like(gg)
        mix_own.wait()
        for k in range(1, S):
            mix_copy(k, lax.rem(s + S - k, S)).wait_recv()

    def unprep(e, u, gain, cosine, sine):
        front, back = e[:half], e[half:]
        e = jnp.concatenate([front * cosine + back * sine, back * cosine - front * sine], axis=0)
        r = lax.rsqrt(jnp.mean(u * u, axis=0, keepdims=True) + EPS)
        ge = gain * e
        du = r * ge - u * (r * r * r * jnp.mean(ge * u, axis=0, keepdims=True))
        return du, jnp.sum(e * u * r, axis=1, keepdims=True)

    for step in range(length // BLOCK):

        @pl.when(i == step)
        def _():
            n = (step + 1) * BLOCK
            here = slice(step * BLOCK, n)
            col = lax.broadcasted_iota(jnp.int32, (n, BLOCK), 0)
            row = step * BLOCK + lax.broadcasted_iota(jnp.int32, (n, BLOCK), 1)
            bias = jnp.where((col <= row) & (row - col <= pos_ref[:, here]), 0.0, -1e30)
            keys, values = k_buf[:n, :], v_buf[:n, :]
            kt = rot_ref[qw : qw + HD, :n]
            per = BLOCK // T
            dmix = dmix_all[step] if per == 1 else jnp.concatenate([dmix_all[step * per + j] for j in range(per)], axis=0)
            dmix_t = dmix.astype(f32).T.astype(bf16)
            qt = rot_ref[:qw, here]
            q = qt.astype(f32).T.astype(bf16)
            cosine, sine = cos_ref[:, here], sin_ref[:, here]
            dqs, gain_sum = [], jnp.zeros((HD, 1), f32)
            dk, dv = jnp.zeros((n, HD), f32), jnp.zeros((n, HD), f32)
            for h in range(heads):
                part = slice(h * HD, (h + 1) * HD)
                p = jnp.exp(dot(keys, qt[part] * 0.125) + bias - lse_ref[h : h + 1, here])
                dv += dot(p.astype(bf16), dmix[:, part])
                dp = dot(values, dmix_t[part])
                inner = jnp.sum(dp * p, axis=0, keepdims=True)
                ds = (p * (dp - inner)).astype(bf16)
                dk += dot(ds, q[:, part])
                dq = (dot(kt, ds) * 0.125).astype(bf16).astype(f32)
                du, dg = unprep(dq, raw_ref[part, here], gq_ref[...], cosine, sine)
                dqs.append(du)
                gain_sum += dg
            dk_acc[:n, :] += dk
            dv_acc[:n, :] += dv
            gg[:, :1] += gain_sum
            dproj[here, :qw] = jnp.concatenate(dqs, axis=0).T.astype(bf16)

    def exchange(k, slot):
        rows = pl.ds(pl.multiple_of(lax.rem(s + k, S) * T, T), T)
        return to_peer(dproj.at[rows], got.at[slot], send.at[k - 1], recv.at[k - 1], k, S)

    @pl.when(i == pl.num_programs(0) - 1)
    def _():
        dk = (dk_acc[...] * 0.125).astype(bf16).astype(f32).T
        du, dg = unprep(dk, raw_ref[qw : qw + HD, :], gk_ref[...], cos_ref[...], sin_ref[...])
        gg[:, 1:2] += dg
        dproj[:, qw:] = jnp.concatenate([du.T, dv_acc[...].astype(bf16).astype(f32)], axis=1).astype(bf16)
        for k in range(1, S):
            exchange(k, s).start()
        move.relay()
        W = 128
        rows_d, rows_o = width // (S * F), qw // F
        blocks = hw // W
        n_q, n_o = S * rows_d * blocks, rows_o * width // W
        tile = 512
        for copy in loads:
            copy.wait()
        d_all = dproj[...]
        for c in range(0, width, tile):
            part = dot(normed_t[c : c + tile, :], d_all).astype(bf16)
            for b in range(tile // rows_d):
                j, m = divmod(c // rows_d + b, F)
                for cb in range(blocks):
                    at = (j * blocks + cb) * rows_d
                    packed_ref[m, at : at + rows_d] = part[b * rows_d : (b + 1) * rows_d, cb * W : (cb + 1) * W]
        e = dot_nt(dproj[pl.ds(pl.multiple_of(s * T, T), T), :], wqkv[s])
        for k in range(1, S):
            slot = lax.rem(s + S - k, S)
            exchange(k, slot).wait_recv()
            e += dot_nt(got[slot], wqkv[slot])
        v = x[...].astype(f32)
        r = lax.rsqrt(jnp.mean(v * v, axis=-1, keepdims=True) + EPS)
        ga = jnp.sum(e * v * r, axis=0, keepdims=True)
        ge = gain_row(g_ref, 0) * e
        gin_ref[...] = gm[...] + r * ge - v * (r * r * r * jnp.mean(ge * v, axis=-1, keepdims=True))
        heads_t = gg[...].T
        second = jnp.concatenate([heads_t[0:1], heads_t[1:2]], axis=1)
        gf = ggf_ref[...]
        for j in range(S):
            for m in range(F):
                cut = slice((j * F + m) * rows_d, (j * F + m + 1) * rows_d)
                first = [ga[:, cut], gf[:, cut]]
                if 2 * rows_d < W:
                    first.append(jnp.zeros((1, W - 2 * rows_d), f32))
                rows = jnp.concatenate([jnp.concatenate(first, axis=1), second, jnp.zeros((14, W), f32)], axis=0)
                packed_ref[m, n_q + n_o + 16 * j : n_q + n_o + 16 * (j + 1)] = rows.astype(bf16)
        move.finish(True)
        mix_t = mix_t_ref[...]
        for c in range(0, width, tile):
            part = jnp.zeros((qw, tile), f32)
            for j in range(S):
                part += dot(mix_t[:, j * T : (j + 1) * T], dattn_all[j, :, c : c + tile])
            for m in range(F):
                cuts = [part[m * rows_o : (m + 1) * rows_o, cb * W : (cb + 1) * W] for cb in range(tile // W)]
                at = n_q + c // W * rows_o
                packed_ref[m, at : at + rows_o * tile // W] = jnp.concatenate(cuts, axis=0).astype(bf16)
        for k in range(1, S):
            exchange(k, s).wait_send()
            mix_copy(k, s).wait_send()


def attention_back(S, F, dmix, rot, raw, lse, pos, cosine, sine, gain_q, gain_k, gain, grad_gf, mix_t, x, gm, normed_t, wqkv_all, d_attn, heads, collective):
    length = rot.shape[1]
    hw = rot.shape[0]
    T, width = x.shape
    rows_d, rows_o = width // (S * F), heads * HD // F
    total = S * rows_d * hw // 128 + rows_o * width // 128 + 16 * S
    whole = lambda a: pl.BlockSpec(a.shape, lambda i: (0,) * a.ndim)
    return pl.pallas_call(
        functools.partial(attn_back_kernel, S, F, heads),
        grid=(length // BLOCK,),
        in_specs=[whole(a) for a in (rot, raw, lse, pos, cosine, sine, gain_q, gain_k, gain, grad_gf, mix_t)] + [ANY] * 6,
        out_specs=[pl.BlockSpec((F, total, 128), lambda i: (0, 0, 0)), pl.BlockSpec((T, width), lambda i: (0, 0))],
        out_shape=[shape((F, total, 128)), shape((T, width), f32)],
        scratch_shapes=[
            pltpu.VMEM((length, HD), bf16),
            pltpu.VMEM((length, HD), bf16),
            pltpu.VMEM((length, HD), f32),
            pltpu.VMEM((length, HD), f32),
            pltpu.VMEM((HD, 128), f32),
            pltpu.VMEM((length, hw), bf16),
            pltpu.VMEM((S, T, width), bf16),
            pltpu.VMEM((S, T, hw), bf16),
            pltpu.VMEM((T, width), bf16),
            pltpu.VMEM((T, width), f32),
            pltpu.VMEM(normed_t.shape, bf16),
            pltpu.VMEM(wqkv_all.shape, bf16),
            pltpu.VMEM(dmix.shape, bf16),
            DMA((S - 1,)),
            DMA((S - 1,)),
            DMA((5,)),
            DMA((S - 1,)),
            DMA((S - 1,)),
        ]
        + Gather.sems(S, d_attn),
        compiler_params=params(collective, 1),
        cost_estimate=cost(1),
    )(rot, raw, lse, pos, cosine, sine, gain_q, gain_k, gain, grad_gf, mix_t, x, gm, normed_t, wqkv_all, d_attn, dmix)


def sum_kernel(S, F, heads, hid_ref, wd_ref, mid_ref, gu_hbm, down_hbm, packed_hbm, out_ref, qkv_ref, gout_ref, tiny_ref, down_out, got_hbm, *refs):
    (
        got, gu_send, gu_recv, gu_own, acc, send_buf, recv_buf, packed, twin, pairs, from_z, mine, mine_all,
        send, recv, far, load, twin_send, twin_recv, z_send, z_recv, end_sems,
    ) = refs
    s, f = lax.axis_index("sp"), lax.axis_index("fsdp")
    T, width = mid_ref.shape
    W = 128
    chips = F // 2
    core = lax.rem(f, 2)
    tile = 512

    def exchange(k, slot):
        return to_peer(gu_hbm.at[lax.rem(s + k, S)], got.at[slot], gu_send.at[k - 1], gu_recv.at[k - 1], k, S)

    def twins(n):
        there = 2 * n + 1 - core
        return push(packed_hbm.at[there], twin.at[n], twin_send.at[n], twin_recv.at[n], sibling())

    def over_z(k):
        target = lax.rem(f + 2 * k, F)
        return push(pairs.at[target // 2], from_z.at[k - 1], z_send.at[k - 1], z_recv.at[k - 1], {"fsdp": target})

    fill = pltpu.make_async_copy(packed_hbm, packed, load)
    fill.start()
    own = pltpu.make_async_copy(gu_hbm.at[s], got.at[s], gu_own.at[0])
    own.start()
    back = pltpu.make_async_copy(got, got_hbm, gu_own.at[1])
    owner = lax.rem(lax.rem(f, S) - s + S, S)
    far_send = push(down_hbm, down_out, far.at[0], far.at[1], {"sp": owner})
    far_keep = pltpu.make_async_copy(down_hbm, down_out, far.at[0])
    greet(S, F, True)

    @pl.when(owner == s)
    def _():
        far_keep.start()

    for n in range(chips):
        twins(n).start()
    fill.wait()
    for n in range(chips):
        twins(n).wait_recv()
        pairs[n] = (packed[2 * n + core].astype(f32) + twin[n].astype(f32)).astype(bf16)
    for k in range(1, chips):
        over_z(k).start()

    def compute(chunk, out):
        rows = hid_ref[pl.ds(pl.multiple_of(chunk * T, T), T), :]
        for c in range(0, width, tile):
            out[:, c : c + tile] = dot(rows, wd_ref[:, c : c + tile]).astype(out.dtype)
    rows_d = qkv_ref.shape[0]
    rows_o = gout_ref.shape[0]
    qw = heads * HD
    QW, KW = QUERY_HEADS * HD, KV_HEADS * HD
    blocks = (qw + 2 * HD) // W
    n_s = blocks * rows_d
    n_q, n_o = S * n_s, rows_o * width // W

    def rows_of(j):
        return pl.ds(pl.multiple_of(j * n_s, n_s), n_s), pl.ds(pl.multiple_of(n_q + n_o + 16 * j, 16), 16)

    def end(k, slot, part):
        to = (slice(0, n_s), slice(n_s, n_s + 16))[part]
        n = 2 * (k - 1) + part
        src = mine.at[rows_of(lax.rem(s + k, S))[part]]
        return to_peer(src, mine_all.at[slot, to], end_sems.at[0, n], end_sems.at[1, n], k, S)

    def reduce_z():
        total = pairs[f // 2].astype(f32)
        for k in range(1, chips):
            over_z(k).wait_recv()
            total += from_z[k - 1].astype(f32)
        mine[...] = total.astype(bf16)
        for k in range(1, S):
            for part in range(2):
                end(k, s, part).start()
        for k in range(1, S):
            exchange(k, s).start()

        @pl.when(owner != s)
        def _():
            far_send.start()

    copies = sum_over_sp(S, compute, acc, send_buf, recv_buf, send, recv, reduce_z)
    out_ref[...] = (mid_ref[...] + acc[...]).astype(bf16)
    main, small = rows_of(s)
    mine_all[s, :n_s] = mine[main, :]
    mine_all[s, n_s:] = mine[small, :]
    for c in range(0, width // W, 2):
        rows = mine[n_q + c * rows_o : n_q + (c + 2) * rows_o, :].astype(f32)
        gout_ref[:, c * W : (c + 1) * W] = rows[:rows_o]
        gout_ref[:, (c + 1) * W : (c + 2) * W] = rows[rows_o:]
    for k in range(1, S):
        for part in range(2):
            end(k, lax.rem(s + S - k, S), part).wait_recv()
    shared = max(1, S // KV_HEADS)
    tiny = jnp.zeros((16, W), f32)
    kvs = []
    for j in range(S):
        for cb in range(blocks - 1):
            at = j * qw + cb * W
            qkv_ref[:, at : at + W] = mine_all[j, cb * rows_d : (cb + 1) * rows_d].astype(f32)
        kv = mine_all[j, (blocks - 1) * rows_d : blocks * rows_d].astype(f32)
        if j % shared:
            kvs[-1] = kvs[-1] + kv
        else:
            kvs.append(kv)
        tiny += mine_all[j, n_s : n_s + 16].astype(f32)
    for h in range(0, KV_HEADS, 2):
        at = QW + h * HD
        qkv_ref[:, at : at + W] = jnp.concatenate([kvs[h][:, :HD], kvs[h + 1][:, :HD]], axis=1)
        qkv_ref[:, at + KW : at + KW + W] = jnp.concatenate([kvs[h][:, HD:], kvs[h + 1][:, HD:]], axis=1)
    tiny_ref[...] = tiny
    own.wait()
    for k in range(1, S):
        exchange(k, lax.rem(s + S - k, S)).wait_recv()
    back.start()
    for k in range(1, S):
        exchange(k, s).wait_send()
    back.wait()
    for copy in copies:
        copy.wait_send()
    for n in range(chips):
        twins(n).wait_send()
    for k in range(1, chips):
        over_z(k).wait_send()
    for k in range(1, S):
        for part in range(2):
            end(k, s, part).wait_send()

    @pl.when(owner == s)
    def _():
        far_keep.wait()

    @pl.when(owner != s)
    def _():
        far_send.wait_send()
        far_send.wait_recv()


def sum_rows(S, F, hidden, w_dn, mid, grad_gu, down, packed, rows_d, rows_o, heads, collective):
    T, width = mid.shape
    n = max(6, S - 1)
    chips = F // 2
    part = packed.shape[1:]
    n_s = rows_d * (heads + 2) * HD // 128
    return pl.pallas_call(
        functools.partial(sum_kernel, S, F, heads),
        in_specs=[VMEM] * 3 + [ANY] * 3,
        out_specs=[VMEM] * 4 + [ANY] * 2,
        out_shape=[
            shape((T, width)),
            shape((rows_d, (QUERY_HEADS + 2 * KV_HEADS) * HD), f32),
            shape((rows_o, width), f32),
            shape((16, 128), f32),
            shape(down.shape),
            shape(grad_gu.shape),
        ],
        scratch_shapes=[
            pltpu.VMEM(grad_gu.shape, bf16),
            DMA((S - 1,)),
            DMA((S - 1,)),
            DMA((2,)),
            pltpu.VMEM((T, width), f32),
            pltpu.VMEM((S - 1, T, width), bf16),
            pltpu.VMEM((S - 1, T, width), bf16),
            pltpu.VMEM(packed.shape, bf16),
            pltpu.VMEM((chips,) + part, bf16),
            pltpu.VMEM((chips,) + part, bf16),
            pltpu.VMEM((chips - 1,) + part, bf16),
            pltpu.VMEM(part, bf16),
            pltpu.VMEM((S, n_s + 16, 128), bf16),
            DMA((n,)),
            DMA((n,)),
            DMA((2,)),
            DMA,
            DMA((chips,)),
            DMA((chips,)),
            DMA((chips - 1,)),
            DMA((chips - 1,)),
            DMA((2, 2 * (S - 1))),
        ],
        compiler_params=params(collective),
        cost_estimate=cost(40),
    )(hidden, w_dn, mid, grad_gu, down, packed)


def write_kernel(S, F, kept, *refs):
    ins, refs = refs[: kept + 2], refs[kept + 2 :]
    outs, refs = refs[: kept + 3], refs[kept + 3 :]
    stages, wide, sem_in, sem_out = refs[: kept + 2], refs[kept + 2 : kept + 5], refs[-2], refs[-1]
    loads = [pltpu.make_async_copy(ins[n], stages[n], sem_in.at[n]) for n in range(kept + 2)]
    for copy in loads[::-1]:
        copy.start()
    stores = []

    def store(n, src):
        stores.append(pltpu.make_async_copy(src, outs[n], sem_out.at[n]))
        stores[-1].start()

    loads[kept + 1].wait()
    got = stages[kept + 1]
    piece = got.shape[3] // F
    for n in range(2):
        for j in range(S):
            for m in range(F):
                at = (m * S + (j + m // 2) % S) * piece
                wide[1 + n][:, at : at + piece] = got[j, n, :, m * piece : (m + 1) * piece].astype(f32)
        store(kept + 1 + n, wide[1 + n])
    loads[kept].wait()
    wide[0][...] = stages[kept][...].astype(f32)
    store(kept, wide[0])
    for n in range(kept):
        loads[n].wait()
        store(n, stages[n])
    for copy in stores:
        copy.wait()


def write_outputs(S, F, kept, down, got):
    _, _, rows_d, FFs = got.shape
    wide = [shape(down.shape, f32)] + [shape((rows_d, FFs * S), f32)] * 2
    if FFs // F % 128:
        parts = got.reshape(S, 2, rows_d, F, FFs // F)
        parts = [parts[(t - m // 2) % S, :, :, m] for m in range(F) for t in range(S)]
        grad = jnp.concatenate(parts, axis=2).astype(f32)
        return list(kept) + [down.astype(f32), grad[0], grad[1]]
    outs = [shape(a.shape, a.dtype) for a in kept] + wide
    ins = list(kept) + [down, got]
    return pl.pallas_call(
        functools.partial(write_kernel, S, F, len(kept)),
        in_specs=[ANY] * len(ins),
        out_specs=[ANY] * len(outs),
        out_shape=outs,
        scratch_shapes=[pltpu.VMEM(a.shape, a.dtype) for a in ins]
        + [pltpu.VMEM(a.shape, f32) for a in wide]
        + [DMA((len(ins),)), DMA((len(outs),))],
        compiler_params=params(),
        cost_estimate=cost(5),
    )(*ins)


def ordered(value, *after):
    return lax.optimization_barrier((value,) + after)[0]


def local(x_own, positions, ct_own, w_qkv, w_out, w_gate, w_up, w_down, gain_attn, gain_ffn, gain_query, gain_key):
    S, F = lax.axis_size("sp"), lax.axis_size("fsdp")
    assert F == 2 * S
    s, f = lax.axis_index("sp"), lax.axis_index("fsdp")
    _, T, D = x_own.shape
    L = positions.shape[1]
    heads = QUERY_HEADS // S
    qw = heads * HD
    hw = qw + 2 * HD
    FFs = w_gate.shape[1] // S
    rows_d = D // (S * F)
    rows_o = qw // F
    x_own = x_own[0]
    ct_own = ct_own[0]

    def gather_z(w):
        return lax.all_gather(w, "fsdp", axis=0, tiled=True)

    def reduce_z(w):
        return lax.psum_scatter(w, "fsdp", scatter_dimension=0, tiled=True)

    gu_part = own_columns(S, F, s, w_gate, w_up)
    w_gu = gather_z(gu_part).reshape(F, 2, D // F, FFs)
    rows_w = w_down.shape[0] // S
    w_dn = gather_z(lax.dynamic_slice_in_dim(w_down, lax.rem(s + f // 2, S) * rows_w, rows_w, 0))

    x_all, wqkv_s, gains, cosine, sine = first_gathers(
        S, F, x_own, ordered(w_qkv, gu_part), gain_attn[None], gain_ffn[None], positions, heads, 0
    )
    x_all = x_all.reshape(L, D)
    wqkv_s = wqkv_s.reshape(D, hw)
    gain_q = gain_query.astype(f32)[:, None]
    gain_k = gain_key.astype(f32)[:, None]
    normed_t, raw, rot, lse, mix_t, mix_all, wout_all, ct0 = forward_attention(
        S, F, x_all, gains, wqkv_s, positions, cosine, sine, gain_q, gain_k, w_out, ct_own, heads, 1
    )
    wout_all = wout_all.reshape(S, qw, D)
    ct0 = ct0.reshape(L, D // 2)
    mid, ffn_in, ffn_t, ct1 = middle_rows(S, x_all, mix_all, wout_all, gains, ct_own, 2)
    ct1 = ct1.reshape(L, D // 2)
    gate, up, hidden, part_down = ffn_forward(S, ffn_in, ct0, ct1, w_gu)
    grad_down = reduce_z(part_down.reshape(FFs, D))
    dgu, part_gu, wqkv_all = ffn_backward(S, F, ct0, ct1, w_dn, gate, up, ffn_t, wqkv_s, 4)
    grad_gu = reduce_z(part_gu.reshape(2 * D, FFs))
    gm, d_attn, grad_gf, d_mix = middle_back(S, dgu, w_gu, wout_all, mid, gains, ct_own, 5)
    packed, grad_input = attention_back(
        S, F, ordered(d_mix, grad_down), rot, raw, lse, positions, cosine, sine, gain_q, gain_k,
        gains, grad_gf, mix_t, x_own, gm, normed_t, wqkv_all, d_attn, heads, 6,
    )
    out, grad_qkv, grad_out, tiny, grad_down, got = sum_rows(
        S, F, hidden, w_dn, mid, grad_gu.reshape(S, 2, rows_d, FFs), grad_down, packed, rows_d, rows_o, heads, 7
    )
    grad_input, out, grad_qkv, grad_out, grad_down, grad_gate, grad_up = write_outputs(
        S, F, (grad_input, out, grad_qkv, grad_out), grad_down, got
    )
    return (
        out[None],
        grad_input[None],
        grad_qkv,
        grad_out,
        grad_gate,
        grad_up,
        grad_down,
        tiny[0, :rows_d],
        tiny[0, rows_d : 2 * rows_d],
        tiny[1, :HD],
        tiny[1, HD:],
    )


def solution(mesh):
    row = P("fsdp", "sp", None)
    shard = P("fsdp", None)
    grad = P(("sp", "fsdp"), None)
    return jax.shard_map(
        local,
        mesh=mesh,
        in_specs=(row, shard, row, shard, shard, shard, shard, shard, P("fsdp"), P("fsdp"), P(), P()),
        out_specs=(row, row, grad, grad, grad, grad, grad, P(("sp", "fsdp")), P(("sp", "fsdp")), P(), P()),
        check_vma=False,
    )
```

```python
import functools

import jax
import jax.numpy as jnp
import numpy as np
from jax import lax
from jax.experimental import pallas as pl
from jax.experimental.pallas import tpu as pltpu
from jax.sharding import PartitionSpec as P

QUERY_HEADS = 16
KV_HEADS = 4
HD = 64
EPS = 1e-06
BLOCK = 256
VMEM_LIMIT = 60 << 20
MESH = pl.DeviceIdType.MESH
f32 = jnp.float32
bf16 = jnp.bfloat16


def params(collective=None, grid=0):
    return pltpu.CompilerParams(
        dimension_semantics=("arbitrary",) * grid if grid else None,
        vmem_limit_bytes=VMEM_LIMIT,
        collective_id=collective,
        has_side_effects=collective is not None,
    )


def cost(micros):
    return pl.CostEstimate(flops=0, bytes_accessed=int(micros * 3_600_000), transcendentals=0)


ANY = pl.BlockSpec(memory_space=pl.ANY)
VMEM = pl.BlockSpec(memory_space=pltpu.VMEM)
DMA = pltpu.SemaphoreType.DMA


def shape(dims, dtype=bf16):
    return jax.ShapeDtypeStruct(dims, dtype)


def dot(a, b):
    return jnp.dot(a, b, preferred_element_type=f32)


def dot_nt(a, b):
    return lax.dot_general(a, b, (((1,), (1,)), ((), ())), preferred_element_type=f32)


def sibling():
    f = lax.axis_index("fsdp")
    return {"fsdp": f + 1 - 2 * lax.rem(f, 2)}


def greet(S, F=0, with_sibling=False):
    s, f = lax.axis_index("sp"), lax.axis_index("fsdp")
    where = [{"sp": lax.rem(s + k, S)} for k in range(1, S)]
    where += [{"fsdp": lax.rem(f + 2 * k, F)} for k in range(1, F // 2)]
    if with_sibling:
        where.append(sibling())
    barrier = pltpu.get_barrier_semaphore()
    for target in where:
        pl.semaphore_signal(barrier, inc=1, device_id=target, device_id_type=MESH)
    pl.semaphore_wait(barrier, len(where))


def gain_row(g_ref, n):
    return jnp.concatenate([g_ref[j].astype(f32)[n : n + 1] for j in range(g_ref.shape[0])], axis=1)


def to_peer(src, dst, send, recv, k, S):
    s = lax.axis_index("sp")
    return pltpu.make_async_remote_copy(
        src_ref=src, dst_ref=dst, send_sem=send, recv_sem=recv, device_id={"sp": lax.rem(s + k, S)}, device_id_type=MESH
    )


def mates(s):
    return s + 1 - 2 * lax.rem(s, 2), lax.rem(s + 2, 4), 3 - s


def xor(a, b):
    return (a + b) % 2 + 2 * ((a // 2 + b // 2) % 2)


def hidden_block(S, s, q):
    if S != 4:
        return (s + q) % S
    x = xor(s, q)
    return (x % 3 + 1) * ((x + 3) // 4)


def hidden_owner(S, s, f):
    i = f % S
    if S != 4:
        return (i - s + S) % S
    return xor(s, ((i + 1) % 3 + 1) * ((i + 3) // 4))


def push(src, dst, send, recv, where):
    return pltpu.make_async_remote_copy(
        src_ref=src, dst_ref=dst, send_sem=send, recv_sem=recv, device_id=where, device_id_type=MESH
    )


class Gather:
    def __init__(self, S, src, dst, sems, halves=False, inner=False, staged=True):
        self.S, self.src, self.halves = S, src, halves
        self.slot = (lambda j: dst.at[:, j]) if inner else (lambda j: dst.at[j])
        self.stage = sems[-1] if staged else None
        self.send, self.recv, self.own = sems[:3]
        self.swap_send, self.swap_recv = sems[3:5] if halves else (None, None)
        self.s, self.f = lax.axis_index("sp"), lax.axis_index("fsdp")
        self.rows = src.shape[0] // (2 if halves else 1)
        self.size = self.rows // 2 if S == 4 else self.rows

    @staticmethod
    def sems(S, chunk, halves=False):
        count = 6 if S == 4 else S - 1
        base = [DMA((count,)), DMA((count,)), DMA((2,))]
        base += [DMA((S - 1,)), DMA((S - 1,))] if halves else []
        return base if chunk is None else base + [pltpu.VMEM(chunk.shape, chunk.dtype)]

    def base(self, mine=True):
        if not self.halves:
            return 0
        core = lax.rem(self.f, 2)
        return (core if mine else 1 - core) * self.rows

    def piece(self, ref, n):
        return ref.at[pl.ds(self.base() + n * self.size, self.size)]

    def share(self, slot, mine):
        if not self.halves:
            return self.slot(slot)
        return self.slot(slot).at[pl.ds(self.base(mine), self.rows)]

    def steps(self):
        s, S = self.s, self.S
        if S != 4:
            return [(self.src, s, lax.rem(s + S - k, S), 0, lax.rem(s + k, S)) for k in range(1, S)]
        x, y, d = mates(s)
        return [
            (self.src, s, x, 0, x),
            (self.src, s, y, 1, y),
            (self.src, s, x, 1, x),
            (self.src, s, y, 0, y),
            (self.slot(x), x, d, 0, y),
            (self.slot(y), y, d, 1, x),
        ]

    def copy(self, n, here):
        src, there, lands, piece, target = self.steps()[n]
        slot = lands if here else there
        return push(
            self.piece(src, piece), self.piece(self.slot(slot), piece), self.send.at[n], self.recv.at[n], {"sp": target}
        )

    def passing(self, n, mine):
        slots = mates(self.s) if self.S == 4 else [lax.rem(self.s + self.S - k, self.S) for k in range(1, self.S)]
        return push(
            self.share(slots[n], True), self.share(slots[n], mine), self.swap_send.at[n], self.swap_recv.at[n], sibling()
        )

    def local(self, out):
        if self.stage is None:
            return pltpu.make_async_copy(self.src, self.slot(self.s), self.own.at[0])
        if out:
            return pltpu.make_async_copy(self.stage, self.slot(self.s), self.own.at[1])
        return pltpu.make_async_copy(self.src, self.stage, self.own.at[0])

    def start(self):
        for n in range(4 if self.S == 4 else self.S - 1):
            self.copy(n, False).start()
        self.local(False).start()

    def relay(self):
        if self.stage is not None:
            self.local(False).wait()
            self.local(True).start()
        if self.S == 4:
            for n in range(2):
                self.copy(n, True).wait_recv()
                self.copy(4 + n, False).start()

    def spread(self):
        if self.S == 4:
            for n in range(2):
                self.copy(2 + n, True).wait_recv()
                if self.halves:
                    self.passing(n, True).start()

    def finish(self, relayed=False, spread=False):
        if not relayed:
            self.relay()
        if not spread:
            self.spread()
        ready = {5: 2} if self.S == 4 else {n: n for n in range(self.S - 1)}
        for n in range(4 if self.S == 4 else 0, len(self.steps())):
            self.copy(n, True).wait_recv()
            if self.halves and n in ready:
                self.passing(ready[n], True).start()
        self.local(True).wait()
        for n in range(len(self.steps())):
            self.copy(n, False).wait_send()
        if self.halves:
            for n in range(self.S - 1):
                self.passing(n, True).wait_send()
                self.passing(n, False).wait_recv()


class GatherZ:
    def __init__(self, F, src, dst, sems):
        self.F, self.src, self.dst = F, src, dst
        self.send, self.recv, self.pass_send, self.pass_recv, self.own = sems
        self.f = lax.axis_index("fsdp")

    @staticmethod
    def sems(F):
        return [DMA((F // 2 - 1,)), DMA((F // 2 - 1,)), DMA((F // 2,)), DMA((F // 2,)), DMA]

    def sending(self, k):
        return push(
            self.src, self.dst.at[self.f], self.send.at[k - 1], self.recv.at[k - 1], {"fsdp": lax.rem(self.f + 2 * k, self.F)}
        )

    def landing(self, k):
        slot = lax.rem(self.f + self.F - 2 * k, self.F)
        return push(
            self.src, self.dst.at[slot], self.send.at[k - 1], self.recv.at[k - 1], {"fsdp": lax.rem(self.f + 2 * k, self.F)}
        )

    def passing(self, k, mine):
        f, F = self.f, self.F
        slot = lax.rem(f + F - 2 * k, F)
        other = f + 1 - 2 * lax.rem(f, 2)
        there = slot if mine else lax.rem(other + F - 2 * k, F)
        src = self.src if k == 0 else self.dst.at[slot]
        return push(src, self.dst.at[there], self.pass_send.at[k], self.pass_recv.at[k], sibling())

    def local(self):
        return pltpu.make_async_copy(self.src, self.dst.at[self.f], self.own)

    def start(self):
        for k in range(1, self.F // 2):
            self.sending(k).start()
        self.passing(0, True).start()
        self.local().start()

    def finish(self):
        for k in range(1, self.F // 2):
            self.landing(k).wait_recv()
            self.passing(k, True).start()
        self.local().wait()
        for k in range(1, self.F // 2):
            self.sending(k).wait_send()
        for k in range(self.F // 2):
            self.passing(k, True).wait_send()
            self.passing(k, False).wait_recv()


def first_kernel(S, F, heads, x_ref, wqkv_ref, ga_ref, gf_ref, pos_ref, freq_ref, x_all, wqkv_all, gains_all, cos_ref, sin_ref, part, gains, *sems):
    s = lax.axis_index("sp")
    qw = heads * HD
    QW, KW = QUERY_HEADS * HD, KV_HEADS * HD
    kv = s // max(1, S // KV_HEADS)
    pair = kv // 2
    high = lax.rem(kv, 2)

    def cut(start):
        block = wqkv_ref[:, pl.ds(pl.multiple_of(start + pair * 128, 128), 128)].astype(f32)
        return jnp.where(high == 1, block[:, HD:], block[:, :HD])

    part[:, :qw] = wqkv_ref[:, pl.ds(pl.multiple_of(s * qw, 128), qw)]
    part[:, qw:] = jnp.concatenate([cut(QW), cut(QW + KW)], axis=1).astype(bf16)
    pad = jnp.zeros((14, ga_ref.shape[1]), f32)
    gains[...] = jnp.concatenate([ga_ref[...].astype(f32), gf_ref[...].astype(f32), pad], axis=0).astype(bf16)
    n = len(Gather.sems(S, shape((1, 1))))
    m = len(GatherZ.sems(F))
    move_x = Gather(S, x_ref, x_all, sems[:n])
    moves_z = [
        GatherZ(F, part, wqkv_all, sems[n : n + m]),
        GatherZ(F, gains, gains_all, sems[n + m :]),
    ]
    greet(S, F, True)
    move_x.start()
    for move in moves_z:
        move.start()
    angles = freq_ref[...] * pos_ref[...].astype(f32)
    cos_ref[...] = jnp.cos(angles)
    sin_ref[...] = jnp.sin(angles)
    move_x.relay()
    for move in moves_z:
        move.finish()
    move_x.finish(True)


def first_gathers(S, F, x, w_qkv, gain_attn, gain_ffn, positions, heads, collective):
    T, width = x.shape
    depth = w_qkv.shape[0]
    hw = (heads + 2) * HD
    length = positions.shape[1]
    frequency = jnp.asarray(10000.0 ** (-2.0 * np.arange(HD // 2) / HD), f32)[:, None]
    table = shape((HD // 2, length), f32)
    return pl.pallas_call(
        functools.partial(first_kernel, S, F, heads),
        in_specs=[ANY] + [VMEM] * 5,
        out_specs=[ANY] * 3 + [VMEM] * 2,
        out_shape=[
            shape((S, T, width)),
            shape((F, depth, hw)),
            shape((F, 16, depth)),
            table,
            table,
        ],
        scratch_shapes=[pltpu.VMEM((depth, hw), bf16), pltpu.VMEM((16, depth), bf16)]
        + Gather.sems(S, x)
        + GatherZ.sems(F) * 2,
        compiler_params=params(collective),
        cost_estimate=cost(45),
    )(x, w_qkv, gain_attn, gain_ffn, positions, frequency)


def columns_kernel(S, F, gate_hbm, up_hbm, out_hbm, buf, sem_in, sem_out):
    s = lax.axis_index("sp")
    piece = buf.shape[2] // F
    ins = []
    for n, ref in enumerate((gate_hbm, up_hbm)):
        for m in range(F):
            src = ref.at[:, pl.ds(pl.multiple_of((m * S + hidden_block(S, s, m // 2)) * piece, piece), piece)]
            ins.append(pltpu.make_async_copy(src, buf.at[n, :, pl.ds(m * piece, piece)], sem_in.at[n * F + m]))
    for copy in ins:
        copy.start()
    outs = []
    for n in range(2):
        for copy in ins[n * F : (n + 1) * F]:
            copy.wait()
        outs.append(pltpu.make_async_copy(buf.at[n], out_hbm.at[n], sem_out.at[n]))
        outs[-1].start()
    for copy in outs:
        copy.wait()


def own_columns(S, F, s, w_gate, w_up):
    depth, FF = w_gate.shape
    piece = FF // (S * F)
    if piece % 128:
        def pick(w):
            starts = [(m * S + hidden_block(S, s, m // 2)) * piece for m in range(F)]
            return jnp.concatenate([lax.dynamic_slice_in_dim(w, at, piece, 1) for at in starts], axis=1)

        return jnp.stack([pick(w_gate), pick(w_up)])
    return pl.pallas_call(
        functools.partial(columns_kernel, S, F),
        in_specs=[ANY, ANY],
        out_specs=ANY,
        out_shape=shape((2, depth, FF // S)),
        scratch_shapes=[pltpu.VMEM((2, depth, FF // S), bf16), DMA((2 * F,)), DMA((2,))],
        compiler_params=params(),
        cost_estimate=cost(3),
    )(w_gate, w_up)


def forward_kernel(S, F, heads, x_ref, g_ref, w_ref, pos_ref, cos_ref, sin_ref, gq_ref, gk_ref, wout_ref, ct_ref, normed_t_ref, raw_ref, rot_ref, lse_ref, mix_t_ref, mix_all, wout_all, ct_all, k_buf, vt_buf, mix_buf, mix_send, mix_recv, mix_own, wout_s, *sems):
    i = pl.program_id(0)
    s = lax.axis_index("sp")
    qw = heads * HD
    half = HD // 2
    blocks = pl.num_programs(0)
    n_z = len(GatherZ.sems(F))
    rows_o = wout_s.shape[1]
    own_out = wout_ref.at[pl.ds(pl.multiple_of(s * rows_o, rows_o), rows_o)]
    move_z = GatherZ(F, own_out, wout_s, sems[:n_z])
    n_w = n_z + len(Gather.sems(S, None, True))
    move = Gather(S, wout_s, wout_all, sems[n_z:n_w], halves=True, inner=True, staged=False)
    move_ct = Gather(S, ct_ref.at[:, pl.ds(0, ct_all.shape[2])], ct_all, sems[n_w:])

    @pl.when(i == 0)
    def _():
        greet(S, F, True)
        move_z.start()
        move_ct.start()

    @pl.when(i == blocks - 1)
    def _():
        move_ct.relay()

    x = x_ref[...].astype(f32)
    scale = lax.rsqrt(jnp.mean(x * x, axis=-1, keepdims=True) + EPS)
    scaled = x * scale * gain_row(g_ref, 0)
    normed = scaled.astype(bf16)
    normed_t_ref[...] = scaled.T.astype(bf16)
    raw = dot(normed, w_ref[...]).T
    raw_ref[...] = raw
    cosine, sine = cos_ref[...], sin_ref[...]

    def prep(u, gain):
        n = u * lax.rsqrt(jnp.mean(u * u, axis=0, keepdims=True) + EPS) * gain
        front, back = n[:half], n[half:]
        return jnp.concatenate([front * cosine - back * sine, back * cosine + front * sine], axis=0)

    q = [prep(raw[h * HD : (h + 1) * HD], gq_ref[...]).astype(bf16) for h in range(heads)]
    kt = prep(raw[qw : qw + HD], gk_ref[...])
    vt = raw[qw + HD :].astype(bf16)
    rot_ref[...] = jnp.concatenate(q + [kt.astype(bf16), vt], axis=0)
    steps = mix_buf.shape[0]

    x_mate, y_mate, d_mate = mates(s)

    def mix_copy(block, k, here):
        rows = pl.ds(block * BLOCK, BLOCK)
        n = block * (S - 1) + k - 1
        if S != 4:
            slot = lax.rem(s + S - k, S) if here else s
            return push(mix_buf.at[block], mix_all.at[slot, rows], mix_send.at[n], mix_recv.at[n], {"sp": lax.rem(s + k, S)})
        if k < 3:
            mate = x_mate if k == 1 else y_mate
            slot = mate if here else s
            return push(mix_buf.at[block], mix_all.at[slot, rows], mix_send.at[n], mix_recv.at[n], {"sp": mate})
        source, mate = (x_mate, y_mate) if block < steps // 2 else (y_mate, x_mate)
        slot = d_mate if here else source
        return push(mix_all.at[source, rows], mix_all.at[slot, rows], mix_send.at[n], mix_recv.at[n], {"sp": mate})

    def mix_local(block):
        return pltpu.make_async_copy(mix_buf.at[block], mix_all.at[s, pl.ds(block * BLOCK, BLOCK)], mix_own.at[block])

    for step in range(steps):

        @pl.when(i == step)
        def _():
            n = (step + 1) * BLOCK
            k_buf[step * BLOCK : n, :] = kt.T.astype(bf16)
            vt_buf[:, step * BLOCK : n] = vt
            col = lax.broadcasted_iota(jnp.int32, (n, BLOCK), 0)
            row = step * BLOCK + lax.broadcasted_iota(jnp.int32, (n, BLOCK), 1)
            bias = jnp.where((col <= row) & (row - col <= pos_ref[...]), 0.0, -1e30)
            keys, values = k_buf[:n, :], vt_buf[:, :n]
            mixes, lses = [], []
            for h in range(heads):
                e = jnp.exp(dot(keys, q[h] * 0.125) + bias)
                total = jnp.sum(e, axis=0, keepdims=True)
                p = (e * (1.0 / total)).astype(bf16)
                mixes.append(dot(values, p))
                lses.append(jnp.log(total))
            mix = jnp.concatenate(mixes, axis=0)
            mix_t_ref[...] = mix.astype(bf16)
            lse_ref[...] = jnp.concatenate(lses + [jnp.zeros((8 - heads, BLOCK), f32)], axis=0)
            mix_buf[step] = mix.T.astype(bf16)
            for k in range(1, 3 if S == 4 else S):
                mix_copy(step, k, False).start()
            mix_local(step).start()

    @pl.when(i == blocks - 1)
    def _():
        move_z.finish()
        move.start()
        for block in range(steps):
            for k in range(1, 3 if S == 4 else S):
                mix_copy(block, k, True).wait_recv()
                if S == 4 and k == (1 if block < steps // 2 else 2):
                    mix_copy(block, 3, False).start()
        move.relay()
        for block in range(steps):
            if S == 4:
                mix_copy(block, 3, True).wait_recv()
            for k in range(1, S):
                mix_copy(block, k, False).wait_send()
            mix_local(block).wait()
        move.finish(True)
        move_ct.finish(True)


def forward_attention(S, F, x, gain, w, pos, cosine, sine, gain_q, gain_k, wout, ct, heads, collective):
    length, width = x.shape
    hw = w.shape[1]
    qw = heads * HD
    steps = length // BLOCK
    full = lambda i: (0, 0)
    rows = lambda i: (i, 0)
    cols = lambda i: (0, i)
    return pl.pallas_call(
        functools.partial(forward_kernel, S, F, heads),
        grid=(steps,),
        in_specs=[
            pl.BlockSpec((BLOCK, width), rows),
            pl.BlockSpec(gain.shape, lambda i: (0, 0, 0)),
            pl.BlockSpec((width, hw), full),
            pl.BlockSpec((1, BLOCK), cols),
            pl.BlockSpec((HD // 2, BLOCK), cols),
            pl.BlockSpec((HD // 2, BLOCK), cols),
            pl.BlockSpec((HD, 1), full),
            pl.BlockSpec((HD, 1), full),
            pl.BlockSpec(wout.shape, full),
            ANY,
        ],
        out_specs=[
            pl.BlockSpec((width, BLOCK), cols),
            pl.BlockSpec((hw, BLOCK), cols),
            pl.BlockSpec((hw, BLOCK), cols),
            pl.BlockSpec((8, BLOCK), cols),
            pl.BlockSpec((qw, BLOCK), cols),
            ANY,
            ANY,
            ANY,
        ],
        out_shape=[
            shape((width, length)),
            shape((hw, length), f32),
            shape((hw, length)),
            shape((8, length), f32),
            shape((qw, length)),
            shape((S, length, qw)),
            shape((F, S, wout.shape[0] // S, width)),
            shape((S,) + ct.shape[:1] + (width // 2,)),
        ],
        scratch_shapes=[
            pltpu.VMEM((length, HD), bf16),
            pltpu.VMEM((HD, length), bf16),
            pltpu.VMEM((steps, BLOCK, qw), bf16),
            DMA((steps * (S - 1),)),
            DMA((steps * (S - 1),)),
            DMA((steps,)),
            pltpu.VMEM((F, wout.shape[0] // S, width), bf16),
        ]
        + GatherZ.sems(F)
        + Gather.sems(S, None, True)
        + Gather.sems(S, shape((ct.shape[0], width // 2))),
        compiler_params=params(collective, 1),
        cost_estimate=cost(45),
    )(x, gain, w, pos, cosine, sine, gain_q, gain_k, wout, ct)


def middle_kernel(S, T, x_ref, mix_ref, wout_ref, g_ref, ct_ref, mid_ref, ffn_ref, ffn_t_ref, ct_all, *sems):
    i = pl.program_id(0)
    s = lax.axis_index("sp")
    move = Gather(S, ct_ref.at[:, pl.ds(ct_all.shape[2], ct_all.shape[2])], ct_all, sems)

    @pl.when(i == 0)
    def _():
        greet(S)
        move.start()

    @pl.when(i == pl.num_programs(0) - 1)
    def _():
        move.relay()

    middle = x_ref[...].astype(f32)
    total = dot(mix_ref[0], wout_ref[0])
    for j in range(1, S):
        total += dot(mix_ref[j], wout_ref[j])
    middle = middle + total

    @pl.when(i == s)
    def _():
        mid_ref[...] = middle

    scaled = middle * lax.rsqrt(jnp.mean(middle * middle, axis=-1, keepdims=True) + EPS) * gain_row(g_ref, 1)
    ffn_ref[...] = scaled.astype(bf16)
    ffn_t_ref[...] = scaled.T.astype(bf16)

    @pl.when(i == pl.num_programs(0) - 1)
    def _():
        move.finish(True)


def middle_rows(S, x, mix_all, wout_all, gain, ct, collective):
    length, width = x.shape
    T = length // S
    qw = mix_all.shape[2]
    return pl.pallas_call(
        functools.partial(middle_kernel, S, T),
        grid=(S,),
        in_specs=[
            pl.BlockSpec((T, width), lambda i: (i, 0)),
            pl.BlockSpec((S, T, qw), lambda i: (0, i, 0)),
            pl.BlockSpec((S, qw, width), lambda i: (0, 0, 0)),
            pl.BlockSpec(gain.shape, lambda i: (0, 0, 0)),
            ANY,
        ],
        out_specs=[
            pl.BlockSpec((T, width), lambda i: (0, 0)),
            pl.BlockSpec((T, width), lambda i: (i, 0)),
            pl.BlockSpec((width, T), lambda i: (0, i)),
            ANY,
        ],
        out_shape=[shape((T, width), f32), shape((length, width)), shape((width, length)), shape((S, T, width // 2))],
        scratch_shapes=Gather.sems(S, shape((T, width // 2))),
        compiler_params=params(collective, 1),
        cost_estimate=cost(45),
    )(x, mix_all, wout_all, gain, ct)


def ffn_kernel(S, F, ffn_ref, ct0_ref, ct1_ref, wg_ref, wu_ref, wqkv_hbm, gate_ref, up_ref, hid_ref, down_ref, wqkv_all, *sems):
    i = pl.program_id(0)
    last = pl.num_programs(0) - 1
    s = lax.axis_index("sp")
    move = Gather(S, wqkv_hbm.at[pl.ds(0, wqkv_all.shape[1])], wqkv_all, sems, halves=True)

    @pl.when(i == 0)
    def _():
        greet(S, 0, True)
        move.start()

    @pl.when(i == last)
    def _():
        move.relay()

    length, width = ffn_ref.shape
    half = width // 2
    rows = ffn_ref[...]
    gate, up = dot(rows, wg_ref[...].reshape(width, BLOCK)), dot(rows, wu_ref[...].reshape(width, BLOCK))
    gate_ref[...] = gate
    up_ref[...] = up
    hidden = gate / (1.0 + jnp.exp(-gate)) * up
    hid_ref[...] = hidden.astype(bf16)
    flipped = hidden.T.astype(bf16)
    piece = down_ref.shape[1]
    for n, ref in enumerate((ct0_ref, ct1_ref)):
        part = dot(flipped, ref[...]).astype(bf16)
        for m in range(BLOCK // piece):
            block = i * (BLOCK // piece) + m
            owner = lax.rem(block, 2) * S + hidden_block(S, s, block // 2)
            down_ref[owner, :, n * half : (n + 1) * half] = part[m * piece : (m + 1) * piece]

    @pl.when(i == last)
    def _():
        move.finish(True)


def ffn_forward(S, ffn_in, ct0, ct1, w_gu, wqkv_s, collective):
    length, width = ffn_in.shape
    F, _, depth, FFs = w_gu.shape
    whole = lambda i: (0, 0)
    col = pl.BlockSpec((length, BLOCK), lambda i: (0, i))
    return pl.pallas_call(
        functools.partial(ffn_kernel, S, F),
        grid=(FFs // BLOCK,),
        in_specs=[
            pl.BlockSpec((length, width), whole),
            pl.BlockSpec((length, width // 2), whole),
            pl.BlockSpec((length, width // 2), whole),
            pl.BlockSpec((F, 1, depth, BLOCK), lambda i: (0, 0, 0, i)),
            pl.BlockSpec((F, 1, depth, BLOCK), lambda i: (0, 1, 0, i)),
            ANY,
        ],
        out_specs=[col, col, col, pl.BlockSpec((F, FFs // F, width), lambda i: (0, 0, 0)), ANY],
        out_shape=[
            shape((length, FFs), f32),
            shape((length, FFs), f32),
            shape((length, FFs)),
            shape((F, FFs // F, width)),
            shape((S, width // 2, wqkv_s.shape[1])),
        ],
        scratch_shapes=Gather.sems(S, shape((width // 2, wqkv_s.shape[1])), True),
        compiler_params=params(collective, 1),
        cost_estimate=cost(20),
    )(ffn_in, ct0, ct1, w_gu, w_gu, wqkv_s)


def ffn_back_kernel(S, F, ct0_ref, ct1_ref, wd_ref, gate_ref, up_ref, ffn_t_ref, wqkv_ref, hid_hbm, wd_hbm, dgu_ref, pgu_ref, wqkv_all, *refs):
    i = pl.program_id(0)
    last = pl.num_programs(0) - 1
    s = lax.axis_index("sp")
    split = S == 4
    if split:
        across, hid, wd, send_buf, send, recv, load = refs[:7]
        x_mate, y_mate, d_mate = mates(s)
        T = send_buf.shape[0]
        loads = [
            pltpu.make_async_copy(hid_hbm.at[pl.ds(pl.multiple_of(d_mate * T, T), T)], hid, load.at[0]),
            pltpu.make_async_copy(wd_hbm, wd, load.at[1]),
        ]
        low, high = pl.ds(0, T // 2), pl.ds(T // 2, T // 2)
        ahead = [
            push(send_buf.at[low], across.at[low], send.at[0], recv.at[0], {"sp": y_mate}),
            push(send_buf.at[high], across.at[high], send.at[1], recv.at[1], {"sp": x_mate}),
        ]
    depth = wqkv_all.shape[1]
    move = Gather(S, wqkv_ref.at[pl.ds(depth, depth)], wqkv_all, refs[7 if split else 0 :], halves=True)

    @pl.when(i == 0)
    def _():
        greet(S, 0, True)
        move.start()
        if split:
            for copy in loads:
                copy.start()

    @pl.when(i == last - 1)
    def _():
        move.relay()

    @pl.when(i == last)
    def _():
        move.spread()

    half = ct0_ref.shape[1]
    gh = dot_nt(ct0_ref[...], wd_ref[:, :half]) + dot_nt(ct1_ref[...], wd_ref[:, half:])
    gate, up = gate_ref[...], up_ref[...]
    sig = 1.0 / (1.0 + jnp.exp(-gate))
    d_gate = (gh * up * sig * (1.0 + gate * (1.0 - sig))).astype(bf16)
    d_up = (gh * (gate * sig)).astype(bf16)
    dgu_ref[0] = d_gate
    dgu_ref[1] = d_up
    ffn_t = ffn_t_ref[...]
    rows = pgu_ref.shape[3]
    for n, d in enumerate((d_gate, d_up)):
        part = dot(ffn_t, d).astype(bf16)
        for j in range(S):
            for m in range(F):
                pgu_ref[m, j, n] = part[(j * F + m) * rows : (j * F + m + 1) * rows]

    if split:

        @pl.when(i == 0)
        def _():
            for copy in loads:
                copy.wait()
            for c in range(0, wd.shape[1], 512):
                send_buf[:, c : c + 512] = dot(hid[...], wd[:, c : c + 512]).astype(bf16)
            for copy in ahead:
                copy.start()

    @pl.when(i == last)
    def _():
        move.finish(True, True)
        if split:
            for copy in ahead:
                copy.wait_recv()
                copy.wait_send()


def ffn_backward(S, F, ct0, ct1, w_dn, gate, up, ffn_t, wqkv_s, hidden, collective):
    length, FFs = gate.shape
    width = w_dn.shape[1]
    tiles = FFs // BLOCK
    rows = width // (S * F)
    whole = lambda i: (0, 0)
    col = lambda i: (0, i)
    T = length // S
    if S == 4:
        extra = [shape((T, width))]
        scratch = [pltpu.VMEM((T, FFs), bf16), pltpu.VMEM((FFs, width), bf16), pltpu.VMEM((T, width), bf16)]
        scratch += [DMA((2,)), DMA((2,)), DMA((2,))]
    else:
        extra, scratch = [], []
    return pl.pallas_call(
        functools.partial(ffn_back_kernel, S, F),
        grid=(tiles,),
        in_specs=[
            pl.BlockSpec((length, width // 2), whole),
            pl.BlockSpec((length, width // 2), whole),
            pl.BlockSpec((BLOCK, width), lambda i: (i, 0)),
            pl.BlockSpec((length, BLOCK), col),
            pl.BlockSpec((length, BLOCK), col),
            pl.BlockSpec((width, length), whole),
            ANY,
            ANY,
            ANY,
        ],
        out_specs=[
            pl.BlockSpec((2, length, BLOCK), lambda i: (0, 0, i)),
            pl.BlockSpec((F, S, 2, rows, BLOCK), lambda i: (0, 0, 0, 0, i)),
            ANY,
        ]
        + [ANY] * len(extra),
        out_shape=[shape((2, length, FFs)), shape((F, S, 2, rows, FFs)), shape((S, width // 2, wqkv_s.shape[1]))] + extra,
        scratch_shapes=scratch + Gather.sems(S, shape((width // 2, wqkv_s.shape[1])), True),
        compiler_params=params(collective, 1),
        cost_estimate=cost(1),
    )(ct0, ct1, w_dn, gate, up, ffn_t, wqkv_s, hidden, w_dn)


def sum_over_sp(S, compute, acc, send_buf, recv_buf, send, recv, between=None, across=None):
    s = lax.axis_index("sp")
    if S != 4:

        def copy(k):
            return push(
                send_buf.at[k - 1], recv_buf.at[k - 1], send.at[k - 1], recv.at[k - 1], {"sp": lax.rem(s + k, S)}
            )

        for k in range(1, S):
            compute(lax.rem(s + k, S), send_buf.at[k - 1])
            copy(k).start()
        compute(s, acc)
        if between is not None:
            between()
        for k in range(1, S):
            copy(k).wait_recv()
            acc[...] += recv_buf[k - 1].astype(f32)
        return [copy(k) for k in range(1, S)]

    x, y, d = mates(s)
    half = acc.shape[0] // 2
    low, high = pl.ds(0, half), pl.ds(half, half)
    if across is not None:

        def whole(n):
            return push(send_buf.at[n], recv_buf.at[n], send.at[n], recv.at[n], {"sp": x if n == 0 else y})

        compute(x, acc)
        send_buf[0, half:] = acc[half:].astype(bf16)
        send_buf[0, :half] = (acc[:half] + across[:half].astype(f32)).astype(bf16)
        whole(0).start()
        compute(y, acc)
        send_buf[1, :half] = acc[:half].astype(bf16)
        send_buf[1, half:] = (acc[half:] + across[half:].astype(f32)).astype(bf16)
        whole(1).start()
        compute(s, acc)
        if between is not None:
            between()
        for n in range(2):
            whole(n).wait_recv()
        acc[...] += recv_buf[0].astype(f32) + recv_buf[1].astype(f32)
        return [whole(n) for n in range(2)]

    def copy(n):
        buf, rows, target = [(0, low, y), (0, high, x), (1, high, x), (2, low, y), (1, low, x), (2, high, y)][n]
        return push(send_buf.at[buf, rows], recv_buf.at[buf, rows], send.at[n], recv.at[n], {"sp": target})

    compute(d, send_buf.at[0])
    copy(0).start()
    copy(1).start()
    compute(x, send_buf.at[1])
    copy(2).start()
    compute(y, send_buf.at[2])
    copy(3).start()
    copy(0).wait_recv()
    send_buf[1, :half] = (send_buf[1, :half].astype(f32) + recv_buf[0, :half].astype(f32)).astype(bf16)
    copy(4).start()
    copy(1).wait_recv()
    send_buf[2, half:] = (send_buf[2, half:].astype(f32) + recv_buf[0, half:].astype(f32)).astype(bf16)
    copy(5).start()
    compute(s, acc)
    if between is not None:
        between()
    for n in range(2, 6):
        copy(n).wait_recv()
    acc[...] += recv_buf[1].astype(f32) + recv_buf[2].astype(f32)
    return [copy(n) for n in range(6)]


def middle_back_kernel(S, F, dgu_hbm, wgu_hbm, wout_hbm, mid_hbm, ct_hbm, g_ref, gm_ref, dattn_ref, gg_ref, dmix_ref, dgu, wgu, wout, mid, ct, acc, send_buf, recv_buf, send, recv, load):
    s = lax.axis_index("sp")
    T, width = mid.shape
    depth = wgu.shape[2]
    greet(S)
    if S == 4:
        x, y, d = mates(s)
        order = [d, x, y, s]
    else:
        order = [lax.rem(s + k, S) for k in range(1, S)] + [s]

    def chunk_load(n):
        rows = pl.ds(pl.multiple_of(order[n] * T, T), T)
        return pltpu.make_async_copy(dgu_hbm.at[:, rows], dgu.at[n], load.at[n])

    def weight_load(c):
        return pltpu.make_async_copy(wgu_hbm.at[c], wgu.at[c], load.at[S + c])

    others = [
        pltpu.make_async_copy(mid_hbm, mid, load.at[S + F]),
        pltpu.make_async_copy(ct_hbm, ct, load.at[S + F + 1]),
        pltpu.make_async_copy(wout_hbm, wout, load.at[S + F + 2]),
    ]
    chunk_load(0).start()
    for c in range(F):
        weight_load(c).start()
    for n in range(1, S):
        chunk_load(n).start()
    for copy in others:
        copy.start()
    calls = []

    def compute(chunk, out):
        n = len(calls)
        calls.append(n)
        chunk_load(n).wait()
        for c in range(F):
            if n == 0:
                weight_load(c).wait()
            part = dot_nt(dgu[n, 0], wgu[c, 0]) + dot_nt(dgu[n, 1], wgu[c, 1])
            out[:, c * depth : (c + 1) * depth] = part.astype(out.dtype)

    copies = sum_over_sp(S, compute, acc, send_buf, recv_buf, send, recv)
    for copy in others:
        copy.wait()
    v, e = mid[...], acc[...]
    r = lax.rsqrt(jnp.mean(v * v, axis=-1, keepdims=True) + EPS)
    gg_ref[...] = jnp.sum(e * v * r, axis=0, keepdims=True)
    ge = gain_row(g_ref, 1) * e
    gm = ct[...].astype(f32) + r * ge - v * (r * r * r * jnp.mean(ge * v, axis=-1, keepdims=True))
    gm_ref[...] = gm
    d_attn = gm.astype(bf16)
    dattn_ref[...] = d_attn

    for j in range(S):
        dmix_ref[j] = dot_nt(d_attn, wout[j]).astype(bf16)
    for copy in copies:
        copy.wait_send()


def middle_back(S, dgu, w_gu, wout_all, mid, gain, ct, collective):
    T, width = mid.shape
    F = w_gu.shape[0]
    FFs = dgu.shape[2]
    qw = wout_all.shape[1]
    n = max(6, S - 1)
    return pl.pallas_call(
        functools.partial(middle_back_kernel, S, F),
        in_specs=[ANY] * 5 + [VMEM],
        out_specs=[VMEM] * 4,
        out_shape=[shape((T, width), f32), shape((T, width)), shape((1, width), f32), shape((S, T, qw))],
        scratch_shapes=[
            pltpu.VMEM((S, 2, T, FFs), bf16),
            pltpu.VMEM(w_gu.shape, bf16),
            pltpu.VMEM(wout_all.shape, bf16),
            pltpu.VMEM((T, width), f32),
            pltpu.VMEM((T, width), bf16),
            pltpu.VMEM((T, width), f32),
            pltpu.VMEM((S - 1, T, width), bf16),
            pltpu.VMEM((S - 1, T, width), bf16),
            DMA((n,)),
            DMA((n,)),
            DMA((S + F + 3,)),
        ],
        compiler_params=params(collective),
        cost_estimate=cost(1),
    )(dgu, w_gu, wout_all, mid, ct, gain)


def attn_back_kernel(S, F, heads, rot_ref, raw_ref, lse_ref, pos_ref, cos_ref, sin_ref, gq_ref, gk_ref, g_ref, ggf_ref, mix_t_ref, x_hbm, gm_hbm, normed_hbm, wqkv0_hbm, wqkv1_hbm, dattn_hbm, dmix_hbm, packed_ref, gin_ref, k_buf, v_buf, dk_acc, dv_acc, gg, dproj, dattn_all, got, x, gm, normed_t, wqkv, dmix_all, send, recv, load, mix_send, mix_recv, *sems):
    i = pl.program_id(0)
    s = lax.axis_index("sp")
    qw = heads * HD
    hw = qw + 2 * HD
    half = HD // 2
    length = rot_ref.shape[1]
    T, width = gin_ref.shape
    move = Gather(S, dattn_hbm, dattn_all, sems)
    loads = [
        pltpu.make_async_copy(a, b, load.at[n])
        for n, (a, b) in enumerate(
            [
                (normed_hbm, normed_t),
                (wqkv0_hbm, wqkv.at[:, pl.ds(0, width // 2)]),
                (wqkv1_hbm, wqkv.at[:, pl.ds(width // 2, width // 2)]),
                (x_hbm, x),
                (gm_hbm, gm),
            ]
        )
    ]

    def mix_copy(k, slot):
        return to_peer(dmix_hbm.at[lax.rem(s + k, S)], dmix_all.at[slot], mix_send.at[k - 1], mix_recv.at[k - 1], k, S)

    mix_own = pltpu.make_async_copy(dmix_hbm.at[s], dmix_all.at[s], load.at[5])

    @pl.when(i == 0)
    def _():
        greet(S)
        for k in range(1, S):
            mix_copy(k, s).start()
        mix_own.start()
        move.start()
        for copy in loads:
            copy.start()
        k_buf[...] = rot_ref[qw : qw + HD, :].astype(f32).T.astype(bf16)
        v_buf[...] = rot_ref[qw + HD :, :].astype(f32).T.astype(bf16)
        dk_acc[...] = jnp.zeros_like(dk_acc)
        dv_acc[...] = jnp.zeros_like(dv_acc)
        gg[...] = jnp.zeros_like(gg)
        mix_own.wait()
        for k in range(1, S):
            mix_copy(k, lax.rem(s + S - k, S)).wait_recv()

    def unprep(e, u, gain, cosine, sine):
        front, back = e[:half], e[half:]
        e = jnp.concatenate([front * cosine + back * sine, back * cosine - front * sine], axis=0)
        r = lax.rsqrt(jnp.mean(u * u, axis=0, keepdims=True) + EPS)
        ge = gain * e
        du = r * ge - u * (r * r * r * jnp.mean(ge * u, axis=0, keepdims=True))
        return du, jnp.sum(e * u * r, axis=1, keepdims=True)

    for step in range(length // BLOCK):

        @pl.when(i == step)
        def _():
            n = (step + 1) * BLOCK
            here = slice(step * BLOCK, n)
            col = lax.broadcasted_iota(jnp.int32, (n, BLOCK), 0)
            row = step * BLOCK + lax.broadcasted_iota(jnp.int32, (n, BLOCK), 1)
            bias = jnp.where((col <= row) & (row - col <= pos_ref[:, here]), 0.0, -1e30)
            keys, values = k_buf[:n, :], v_buf[:n, :]
            kt = rot_ref[qw : qw + HD, :n]
            per = BLOCK // T
            dmix = dmix_all[step] if per == 1 else jnp.concatenate([dmix_all[step * per + j] for j in range(per)], axis=0)
            dmix_t = dmix.astype(f32).T.astype(bf16)
            qt = rot_ref[:qw, here]
            q = qt.astype(f32).T.astype(bf16)
            cosine, sine = cos_ref[:, here], sin_ref[:, here]
            dqs, gain_sum = [], jnp.zeros((HD, 1), f32)
            dk, dv = jnp.zeros((n, HD), f32), jnp.zeros((n, HD), f32)
            for h in range(heads):
                part = slice(h * HD, (h + 1) * HD)
                p = jnp.exp(dot(keys, qt[part] * 0.125) + bias - lse_ref[h : h + 1, here])
                dv += dot(p.astype(bf16), dmix[:, part])
                dp = dot(values, dmix_t[part])
                inner = jnp.sum(dp * p, axis=0, keepdims=True)
                ds = (p * (dp - inner)).astype(bf16)
                dk += dot(ds, q[:, part])
                dq = (dot(kt, ds) * 0.125).astype(bf16).astype(f32)
                du, dg = unprep(dq, raw_ref[part, here], gq_ref[...], cosine, sine)
                dqs.append(du)
                gain_sum += dg
            dk_acc[:n, :] += dk
            dv_acc[:n, :] += dv
            gg[:, :1] += gain_sum
            dproj[here, :qw] = jnp.concatenate(dqs, axis=0).T.astype(bf16)

    def exchange(k, slot):
        rows = pl.ds(pl.multiple_of(lax.rem(s + k, S) * T, T), T)
        return to_peer(dproj.at[rows], got.at[slot], send.at[k - 1], recv.at[k - 1], k, S)

    @pl.when(i == pl.num_programs(0) - 1)
    def _():
        dk = (dk_acc[...] * 0.125).astype(bf16).astype(f32).T
        du, dg = unprep(dk, raw_ref[qw : qw + HD, :], gk_ref[...], cos_ref[...], sin_ref[...])
        gg[:, 1:2] += dg
        dproj[:, qw:] = jnp.concatenate([du.T, dv_acc[...].astype(bf16).astype(f32)], axis=1).astype(bf16)
        for k in range(1, S):
            exchange(k, s).start()
        move.relay()
        W = 128
        rows_d, rows_o = width // (S * F), qw // F
        blocks = hw // W
        n_q, n_o = S * rows_d * blocks, rows_o * width // W
        tile = 512
        for copy in loads:
            copy.wait()
        d_all = dproj[...]
        for c in range(0, width, tile):
            part = dot(normed_t[c : c + tile, :], d_all).astype(bf16)
            for b in range(tile // rows_d):
                j, m = divmod(c // rows_d + b, F)
                for cb in range(blocks):
                    at = (j * blocks + cb) * rows_d
                    packed_ref[m, at : at + rows_d] = part[b * rows_d : (b + 1) * rows_d, cb * W : (cb + 1) * W]
        e = dot_nt(dproj[pl.ds(pl.multiple_of(s * T, T), T), :], wqkv[s])
        for k in range(1, S):
            slot = lax.rem(s + S - k, S)
            exchange(k, slot).wait_recv()
            e += dot_nt(got[slot], wqkv[slot])
        v = x[...].astype(f32)
        r = lax.rsqrt(jnp.mean(v * v, axis=-1, keepdims=True) + EPS)
        ga = jnp.sum(e * v * r, axis=0, keepdims=True)
        ge = gain_row(g_ref, 0) * e
        gin_ref[...] = gm[...] + r * ge - v * (r * r * r * jnp.mean(ge * v, axis=-1, keepdims=True))
        heads_t = gg[...].T
        second = jnp.concatenate([heads_t[0:1], heads_t[1:2]], axis=1)
        gf = ggf_ref[...]
        for j in range(S):
            for m in range(F):
                cut = slice((j * F + m) * rows_d, (j * F + m + 1) * rows_d)
                first = [ga[:, cut], gf[:, cut]]
                if 2 * rows_d < W:
                    first.append(jnp.zeros((1, W - 2 * rows_d), f32))
                rows = jnp.concatenate([jnp.concatenate(first, axis=1), second, jnp.zeros((14, W), f32)], axis=0)
                packed_ref[m, n_q + n_o + 16 * j : n_q + n_o + 16 * (j + 1)] = rows.astype(bf16)
        move.finish(True)
        mix_t = mix_t_ref[...]
        for c in range(0, width, tile):
            part = jnp.zeros((qw, tile), f32)
            for j in range(S):
                part += dot(mix_t[:, j * T : (j + 1) * T], dattn_all[j, :, c : c + tile])
            for m in range(F):
                cuts = [part[m * rows_o : (m + 1) * rows_o, cb * W : (cb + 1) * W] for cb in range(tile // W)]
                at = n_q + c // W * rows_o
                packed_ref[m, at : at + rows_o * tile // W] = jnp.concatenate(cuts, axis=0).astype(bf16)
        for k in range(1, S):
            exchange(k, s).wait_send()
            mix_copy(k, s).wait_send()


def attention_back(S, F, dmix, rot, raw, lse, pos, cosine, sine, gain_q, gain_k, gain, grad_gf, mix_t, x, gm, normed_t, wqkv0, wqkv1, d_attn, heads, collective):
    length = rot.shape[1]
    hw = rot.shape[0]
    T, width = x.shape
    rows_d, rows_o = width // (S * F), heads * HD // F
    total = S * rows_d * hw // 128 + rows_o * width // 128 + 16 * S
    whole = lambda a: pl.BlockSpec(a.shape, lambda i: (0,) * a.ndim)
    return pl.pallas_call(
        functools.partial(attn_back_kernel, S, F, heads),
        grid=(length // BLOCK,),
        in_specs=[whole(a) for a in (rot, raw, lse, pos, cosine, sine, gain_q, gain_k, gain, grad_gf, mix_t)] + [ANY] * 7,
        out_specs=[pl.BlockSpec((F, total, 128), lambda i: (0, 0, 0)), pl.BlockSpec((T, width), lambda i: (0, 0))],
        out_shape=[shape((F, total, 128)), shape((T, width), f32)],
        scratch_shapes=[
            pltpu.VMEM((length, HD), bf16),
            pltpu.VMEM((length, HD), bf16),
            pltpu.VMEM((length, HD), f32),
            pltpu.VMEM((length, HD), f32),
            pltpu.VMEM((HD, 128), f32),
            pltpu.VMEM((length, hw), bf16),
            pltpu.VMEM((S, T, width), bf16),
            pltpu.VMEM((S, T, hw), bf16),
            pltpu.VMEM((T, width), bf16),
            pltpu.VMEM((T, width), f32),
            pltpu.VMEM(normed_t.shape, bf16),
            pltpu.VMEM((S, width, hw), bf16),
            pltpu.VMEM(dmix.shape, bf16),
            DMA((S - 1,)),
            DMA((S - 1,)),
            DMA((6,)),
            DMA((S - 1,)),
            DMA((S - 1,)),
        ]
        + Gather.sems(S, d_attn),
        compiler_params=params(collective, 1),
        cost_estimate=cost(1),
    )(rot, raw, lse, pos, cosine, sine, gain_q, gain_k, gain, grad_gf, mix_t, x, gm, normed_t, wqkv0, wqkv1, d_attn, dmix)


def sum_kernel(S, F, heads, early, hid_ref, wd_ref, mid_ref, gu_hbm, down_hbm, packed_hbm, *refs):
    across = refs[0] if early else None
    refs = refs[early:]
    (
        out_ref, qkv_ref, gout_ref, tiny_ref, down_out, got_hbm, got, gu_send, gu_recv, gu_own, acc, send_buf, recv_buf, packed, twin, pairs, from_z, mine, mine_all,
        send, recv, far, load, twin_send, twin_recv, z_send, z_recv, end_sems,
    ) = refs
    s, f = lax.axis_index("sp"), lax.axis_index("fsdp")
    T, width = mid_ref.shape
    W = 128
    chips = F // 2
    core = lax.rem(f, 2)
    tile = 512

    def exchange(k, slot):
        return to_peer(gu_hbm.at[lax.rem(s + k, S)], got.at[slot], gu_send.at[k - 1], gu_recv.at[k - 1], k, S)

    def twins(n):
        there = 2 * n + 1 - core
        return push(packed_hbm.at[there], twin.at[n], twin_send.at[n], twin_recv.at[n], sibling())

    def over_z(k):
        target = lax.rem(f + 2 * k, F)
        return push(pairs.at[target // 2], from_z.at[k - 1], z_send.at[k - 1], z_recv.at[k - 1], {"fsdp": target})

    fill = pltpu.make_async_copy(packed_hbm, packed, load)
    fill.start()
    own = pltpu.make_async_copy(gu_hbm.at[s], got.at[s], gu_own.at[0])
    own.start()
    back = pltpu.make_async_copy(got, got_hbm, gu_own.at[1])
    owner = hidden_owner(S, s, f)
    far_send = push(down_hbm, down_out, far.at[0], far.at[1], {"sp": owner})
    far_keep = pltpu.make_async_copy(down_hbm, down_out, far.at[0])
    greet(S, F, True)

    @pl.when(owner == s)
    def _():
        far_keep.start()

    for n in range(chips):
        twins(n).start()
    fill.wait()
    for n in range(chips):
        twins(n).wait_recv()
        pairs[n] = (packed[2 * n + core].astype(f32) + twin[n].astype(f32)).astype(bf16)
    for k in range(1, chips):
        over_z(k).start()

    def compute(chunk, out):
        rows = hid_ref[pl.ds(pl.multiple_of(chunk * T, T), T), :]
        for c in range(0, width, tile):
            out[:, c : c + tile] = dot(rows, wd_ref[:, c : c + tile]).astype(out.dtype)
    rows_d = qkv_ref.shape[0]
    rows_o = gout_ref.shape[0]
    qw = heads * HD
    QW, KW = QUERY_HEADS * HD, KV_HEADS * HD
    blocks = (qw + 2 * HD) // W
    n_s = blocks * rows_d
    n_q, n_o = S * n_s, rows_o * width // W

    def rows_of(j):
        return pl.ds(pl.multiple_of(j * n_s, n_s), n_s), pl.ds(pl.multiple_of(n_q + n_o + 16 * j, 16), 16)

    def end(k, slot, part):
        to = (slice(0, n_s), slice(n_s, n_s + 16))[part]
        n = 2 * (k - 1) + part
        src = mine.at[rows_of(lax.rem(s + k, S))[part]]
        return to_peer(src, mine_all.at[slot, to], end_sems.at[0, n], end_sems.at[1, n], k, S)

    def reduce_z():
        total = pairs[f // 2].astype(f32)
        for k in range(1, chips):
            over_z(k).wait_recv()
            total += from_z[k - 1].astype(f32)
        mine[...] = total.astype(bf16)
        for k in range(1, S):
            for part in range(2):
                end(k, s, part).start()
        for k in range(1, S):
            exchange(k, s).start()

        @pl.when(owner != s)
        def _():
            far_send.start()

    copies = sum_over_sp(S, compute, acc, send_buf, recv_buf, send, recv, reduce_z, across)
    out_ref[...] = (mid_ref[...] + acc[...]).astype(bf16)
    main, small = rows_of(s)
    mine_all[s, :n_s] = mine[main, :]
    mine_all[s, n_s:] = mine[small, :]
    for c in range(0, width // W, 2):
        rows = mine[n_q + c * rows_o : n_q + (c + 2) * rows_o, :].astype(f32)
        gout_ref[:, c * W : (c + 1) * W] = rows[:rows_o]
        gout_ref[:, (c + 1) * W : (c + 2) * W] = rows[rows_o:]
    for k in range(1, S):
        for part in range(2):
            end(k, lax.rem(s + S - k, S), part).wait_recv()
    shared = max(1, S // KV_HEADS)
    tiny = jnp.zeros((16, W), f32)
    kvs = []
    for j in range(S):
        for cb in range(blocks - 1):
            at = j * qw + cb * W
            qkv_ref[:, at : at + W] = mine_all[j, cb * rows_d : (cb + 1) * rows_d].astype(f32)
        kv = mine_all[j, (blocks - 1) * rows_d : blocks * rows_d].astype(f32)
        if j % shared:
            kvs[-1] = kvs[-1] + kv
        else:
            kvs.append(kv)
        tiny += mine_all[j, n_s : n_s + 16].astype(f32)
    for h in range(0, KV_HEADS, 2):
        at = QW + h * HD
        qkv_ref[:, at : at + W] = jnp.concatenate([kvs[h][:, :HD], kvs[h + 1][:, :HD]], axis=1)
        qkv_ref[:, at + KW : at + KW + W] = jnp.concatenate([kvs[h][:, HD:], kvs[h + 1][:, HD:]], axis=1)
    tiny_ref[...] = tiny
    own.wait()
    for k in range(1, S):
        exchange(k, lax.rem(s + S - k, S)).wait_recv()
    back.start()
    for k in range(1, S):
        exchange(k, s).wait_send()
    back.wait()
    for copy in copies:
        copy.wait_send()
    for n in range(chips):
        twins(n).wait_send()
    for k in range(1, chips):
        over_z(k).wait_send()
    for k in range(1, S):
        for part in range(2):
            end(k, s, part).wait_send()

    @pl.when(owner == s)
    def _():
        far_keep.wait()

    @pl.when(owner != s)
    def _():
        far_send.wait_send()
        far_send.wait_recv()


def sum_rows(S, F, hidden, w_dn, mid, grad_gu, down, packed, across, rows_d, rows_o, heads, collective):
    T, width = mid.shape
    n = max(6, S - 1)
    chips = F // 2
    part = packed.shape[1:]
    n_s = rows_d * (heads + 2) * HD // 128
    return pl.pallas_call(
        functools.partial(sum_kernel, S, F, heads, len(across)),
        in_specs=[VMEM] * 3 + [ANY] * 3 + [VMEM] * len(across),
        out_specs=[VMEM] * 4 + [ANY] * 2,
        out_shape=[
            shape((T, width)),
            shape((rows_d, (QUERY_HEADS + 2 * KV_HEADS) * HD), f32),
            shape((rows_o, width), f32),
            shape((16, 128), f32),
            shape(down.shape),
            shape(grad_gu.shape),
        ],
        scratch_shapes=[
            pltpu.VMEM(grad_gu.shape, bf16),
            DMA((S - 1,)),
            DMA((S - 1,)),
            DMA((2,)),
            pltpu.VMEM((T, width), f32),
            pltpu.VMEM((S - 1, T, width), bf16),
            pltpu.VMEM((S - 1, T, width), bf16),
            pltpu.VMEM(packed.shape, bf16),
            pltpu.VMEM((chips,) + part, bf16),
            pltpu.VMEM((chips,) + part, bf16),
            pltpu.VMEM((chips - 1,) + part, bf16),
            pltpu.VMEM(part, bf16),
            pltpu.VMEM((S, n_s + 16, 128), bf16),
            DMA((n,)),
            DMA((n,)),
            DMA((2,)),
            DMA,
            DMA((chips,)),
            DMA((chips,)),
            DMA((chips - 1,)),
            DMA((chips - 1,)),
            DMA((2, 2 * (S - 1))),
        ],
        compiler_params=params(collective),
        cost_estimate=cost(40),
    )(hidden, w_dn, mid, grad_gu, down, packed, *across)


def write_kernel(S, F, kept, *refs):
    ins, refs = refs[: kept + 2], refs[kept + 2 :]
    outs, refs = refs[: kept + 3], refs[kept + 3 :]
    stages, wide, sem_in, sem_out = refs[: kept + 2], refs[kept + 2 : kept + 5], refs[-2], refs[-1]
    loads = [pltpu.make_async_copy(ins[n], stages[n], sem_in.at[n]) for n in range(kept + 2)]
    for copy in loads[::-1]:
        copy.start()
    stores = []

    def store(n, src):
        stores.append(pltpu.make_async_copy(src, outs[n], sem_out.at[n]))
        stores[-1].start()

    loads[kept + 1].wait()
    got = stages[kept + 1]
    piece = got.shape[3] // F
    for n in range(2):
        for j in range(S):
            for m in range(F):
                at = (m * S + hidden_block(S, j, m // 2)) * piece
                wide[1 + n][:, at : at + piece] = got[j, n, :, m * piece : (m + 1) * piece].astype(f32)
        store(kept + 1 + n, wide[1 + n])
    loads[kept].wait()
    wide[0][...] = stages[kept][...].astype(f32)
    store(kept, wide[0])
    for n in range(kept):
        loads[n].wait()
        store(n, stages[n])
    for copy in stores:
        copy.wait()


def write_outputs(S, F, kept, down, got):
    _, _, rows_d, FFs = got.shape
    wide = [shape(down.shape, f32)] + [shape((rows_d, FFs * S), f32)] * 2
    if FFs // F % 128:
        parts = got.reshape(S, 2, rows_d, F, FFs // F)
        parts = [parts[(t - m // 2) % S, :, :, m] for m in range(F) for t in range(S)]
        grad = jnp.concatenate(parts, axis=2).astype(f32)
        return list(kept) + [down.astype(f32), grad[0], grad[1]]
    outs = [shape(a.shape, a.dtype) for a in kept] + wide
    ins = list(kept) + [down, got]
    return pl.pallas_call(
        functools.partial(write_kernel, S, F, len(kept)),
        in_specs=[ANY] * len(ins),
        out_specs=[ANY] * len(outs),
        out_shape=outs,
        scratch_shapes=[pltpu.VMEM(a.shape, a.dtype) for a in ins]
        + [pltpu.VMEM(a.shape, f32) for a in wide]
        + [DMA((len(ins),)), DMA((len(outs),))],
        compiler_params=params(),
        cost_estimate=cost(5),
    )(*ins)


def ordered(value, *after):
    return lax.optimization_barrier((value,) + after)[0]


def local(x_own, positions, ct_own, w_qkv, w_out, w_gate, w_up, w_down, gain_attn, gain_ffn, gain_query, gain_key):
    S, F = lax.axis_size("sp"), lax.axis_size("fsdp")
    assert F == 2 * S
    s, f = lax.axis_index("sp"), lax.axis_index("fsdp")
    _, T, D = x_own.shape
    L = positions.shape[1]
    heads = QUERY_HEADS // S
    qw = heads * HD
    hw = qw + 2 * HD
    FFs = w_gate.shape[1] // S
    rows_d = D // (S * F)
    rows_o = qw // F
    x_own = x_own[0]
    ct_own = ct_own[0]

    def gather_z(w):
        return lax.all_gather(w, "fsdp", axis=0, tiled=True)

    def reduce_z(w):
        return lax.psum_scatter(w, "fsdp", scatter_dimension=0, tiled=True)

    gu_part = own_columns(S, F, s, w_gate, w_up)
    w_gu = gather_z(gu_part).reshape(F, 2, D // F, FFs)
    rows_w = w_down.shape[0] // S

    x_all, wqkv_s, gains, cosine, sine = first_gathers(
        S, F, x_own, ordered(w_qkv, gu_part), gain_attn[None], gain_ffn[None], positions, heads, 0
    )
    w_down, gain_query, gain_key, _ = lax.optimization_barrier((w_down, gain_query, gain_key, x_all))
    w_dn = gather_z(lax.dynamic_slice_in_dim(w_down, hidden_block(S, s, f // 2) * rows_w, rows_w, 0))
    x_all = x_all.reshape(L, D)
    wqkv_s = wqkv_s.reshape(D, hw)
    gain_q = gain_query.astype(f32)[:, None]
    gain_k = gain_key.astype(f32)[:, None]
    normed_t, raw, rot, lse, mix_t, mix_all, wout_all, ct0 = forward_attention(
        S, F, x_all, gains, wqkv_s, positions, cosine, sine, gain_q, gain_k, w_out, ct_own, heads, 1
    )
    wout_all = wout_all.reshape(S, qw, D)
    ct0 = ct0.reshape(L, D // 2)
    mid, ffn_in, ffn_t, ct1 = middle_rows(S, x_all, mix_all, wout_all, gains, ct_own, 2)
    ct1 = ct1.reshape(L, D // 2)
    gate, up, hidden, part_down, wqkv0 = ffn_forward(S, ffn_in, ct0, ct1, w_gu, wqkv_s, 3)
    grad_down = reduce_z(part_down.reshape(FFs, D))
    dgu, part_gu, wqkv1, *across = ffn_backward(S, F, ct0, ct1, w_dn, gate, up, ffn_t, wqkv_s, hidden, 4)
    grad_gu = reduce_z(part_gu.reshape(2 * D, FFs))
    gm, d_attn, grad_gf, d_mix = middle_back(S, dgu, w_gu, wout_all, mid, gains, ct_own, 5)
    packed, grad_input = attention_back(
        S, F, ordered(d_mix, grad_down), rot, raw, lse, positions, cosine, sine, gain_q, gain_k,
        gains, grad_gf, mix_t, x_own, gm, normed_t, wqkv0, wqkv1, d_attn, heads, 6,
    )
    out, grad_qkv, grad_out, tiny, grad_down, got = sum_rows(
        S, F, hidden, w_dn, mid, grad_gu.reshape(S, 2, rows_d, FFs), grad_down, packed, across, rows_d, rows_o, heads, 7
    )
    grad_input, out, grad_qkv, grad_out, grad_down, grad_gate, grad_up = write_outputs(
        S, F, (grad_input, out, grad_qkv, grad_out), grad_down, got
    )
    return (
        out[None],
        grad_input[None],
        grad_qkv,
        grad_out,
        grad_gate,
        grad_up,
        grad_down,
        tiny[0, :rows_d],
        tiny[0, rows_d : 2 * rows_d],
        tiny[1, :HD],
        tiny[1, HD:],
    )


def solution(mesh):
    row = P("fsdp", "sp", None)
    shard = P("fsdp", None)
    grad = P(("sp", "fsdp"), None)
    return jax.shard_map(
        local,
        mesh=mesh,
        in_specs=(row, shard, row, shard, shard, shard, shard, shard, P("fsdp"), P("fsdp"), P(), P()),
        out_specs=(row, row, grad, grad, grad, grad, grad, P(("sp", "fsdp")), P(("sp", "fsdp")), P(), P()),
        check_vma=False,
    )
```

```python
import functools

import jax
import jax.numpy as jnp
import numpy as np
from jax import lax
from jax.experimental import pallas as pl
from jax.experimental.pallas import tpu as pltpu
from jax.sharding import PartitionSpec as P

QUERY_HEADS = 16
KV_HEADS = 4
HD = 64
EPS = 1e-06
BLOCK = 256
VMEM_LIMIT = 60 << 20
MESH = pl.DeviceIdType.MESH
f32 = jnp.float32
bf16 = jnp.bfloat16


def params(collective=None, grid=0):
    return pltpu.CompilerParams(
        dimension_semantics=("arbitrary",) * grid if grid else None,
        vmem_limit_bytes=VMEM_LIMIT,
        collective_id=collective,
        has_side_effects=collective is not None,
    )


def cost(micros):
    return pl.CostEstimate(flops=0, bytes_accessed=int(micros * 3_600_000), transcendentals=0)


ANY = pl.BlockSpec(memory_space=pl.ANY)
VMEM = pl.BlockSpec(memory_space=pltpu.VMEM)
DMA = pltpu.SemaphoreType.DMA


def shape(dims, dtype=bf16):
    return jax.ShapeDtypeStruct(dims, dtype)


def dot(a, b):
    return jnp.dot(a, b, preferred_element_type=f32)


def dot_nt(a, b):
    return lax.dot_general(a, b, (((1,), (1,)), ((), ())), preferred_element_type=f32)


def sibling():
    f = lax.axis_index("fsdp")
    return {"fsdp": f + 1 - 2 * lax.rem(f, 2)}


def greet(S, F=0, with_sibling=False):
    s, f = lax.axis_index("sp"), lax.axis_index("fsdp")
    where = [{"sp": lax.rem(s + k, S)} for k in range(1, S)]
    where += [{"fsdp": lax.rem(f + 2 * k, F)} for k in range(1, F // 2)]
    if with_sibling:
        where.append(sibling())
    barrier = pltpu.get_barrier_semaphore()
    for target in where:
        pl.semaphore_signal(barrier, inc=1, device_id=target, device_id_type=MESH)
    pl.semaphore_wait(barrier, len(where))


def gain_row(g_ref, n):
    return jnp.concatenate([g_ref[j].astype(f32)[n : n + 1] for j in range(g_ref.shape[0])], axis=1)


def to_peer(src, dst, send, recv, k, S):
    s = lax.axis_index("sp")
    return pltpu.make_async_remote_copy(
        src_ref=src, dst_ref=dst, send_sem=send, recv_sem=recv, device_id={"sp": lax.rem(s + k, S)}, device_id_type=MESH
    )


def mates(s):
    return s + 1 - 2 * lax.rem(s, 2), lax.rem(s + 2, 4), 3 - s


def xor(a, b):
    return (a + b) % 2 + 2 * ((a // 2 + b // 2) % 2)


def hidden_block(S, s, q):
    if S != 4:
        return (s + q) % S
    x = xor(s, q)
    return (x % 3 + 1) * ((x + 3) // 4)


def hidden_owner(S, s, f):
    i = f % S
    if S != 4:
        return (i - s + S) % S
    return xor(s, ((i + 1) % 3 + 1) * ((i + 3) // 4))


def push(src, dst, send, recv, where):
    return pltpu.make_async_remote_copy(
        src_ref=src, dst_ref=dst, send_sem=send, recv_sem=recv, device_id=where, device_id_type=MESH
    )


class Gather:
    def __init__(self, S, src, dst, sems, halves=False, inner=False, staged=True):
        self.S, self.src, self.halves = S, src, halves
        self.slot = (lambda j: dst.at[:, j]) if inner else (lambda j: dst.at[j])
        self.stage = sems[-1] if staged else None
        self.send, self.recv, self.own = sems[:3]
        self.swap_send, self.swap_recv = sems[3:5] if halves else (None, None)
        self.s, self.f = lax.axis_index("sp"), lax.axis_index("fsdp")
        self.rows = src.shape[0] // (2 if halves else 1)
        self.size = self.rows // 2 if S == 4 else self.rows

    @staticmethod
    def sems(S, chunk, halves=False):
        count = 6 if S == 4 else S - 1
        base = [DMA((count,)), DMA((count,)), DMA((2,))]
        base += [DMA((S - 1,)), DMA((S - 1,))] if halves else []
        return base if chunk is None else base + [pltpu.VMEM(chunk.shape, chunk.dtype)]

    def base(self, mine=True):
        if not self.halves:
            return 0
        core = lax.rem(self.f, 2)
        return (core if mine else 1 - core) * self.rows

    def piece(self, ref, n):
        return ref.at[pl.ds(self.base() + n * self.size, self.size)]

    def share(self, slot, mine):
        if not self.halves:
            return self.slot(slot)
        return self.slot(slot).at[pl.ds(self.base(mine), self.rows)]

    def steps(self):
        s, S = self.s, self.S
        if S != 4:
            return [(self.src, s, lax.rem(s + S - k, S), 0, lax.rem(s + k, S)) for k in range(1, S)]
        x, y, d = mates(s)
        return [
            (self.src, s, x, 0, x),
            (self.src, s, y, 1, y),
            (self.src, s, x, 1, x),
            (self.src, s, y, 0, y),
            (self.slot(x), x, d, 0, y),
            (self.slot(y), y, d, 1, x),
        ]

    def copy(self, n, here):
        src, there, lands, piece, target = self.steps()[n]
        slot = lands if here else there
        return push(
            self.piece(src, piece), self.piece(self.slot(slot), piece), self.send.at[n], self.recv.at[n], {"sp": target}
        )

    def passing(self, n, mine):
        slots = mates(self.s) if self.S == 4 else [lax.rem(self.s + self.S - k, self.S) for k in range(1, self.S)]
        return push(
            self.share(slots[n], True), self.share(slots[n], mine), self.swap_send.at[n], self.swap_recv.at[n], sibling()
        )

    def local(self, out):
        if self.stage is None:
            return pltpu.make_async_copy(self.src, self.slot(self.s), self.own.at[0])
        if out:
            return pltpu.make_async_copy(self.stage, self.slot(self.s), self.own.at[1])
        return pltpu.make_async_copy(self.src, self.stage, self.own.at[0])

    def start(self):
        for n in range(4 if self.S == 4 else self.S - 1):
            self.copy(n, False).start()
        self.local(False).start()

    def relay(self):
        if self.stage is not None:
            self.local(False).wait()
            self.local(True).start()
        if self.S == 4:
            for n in range(2):
                self.copy(n, True).wait_recv()
                self.copy(4 + n, False).start()

    def spread(self):
        if self.S == 4:
            for n in range(2):
                self.copy(2 + n, True).wait_recv()
                if self.halves:
                    self.passing(n, True).start()

    def finish(self, relayed=False, spread=False):
        if not relayed:
            self.relay()
        if not spread:
            self.spread()
        ready = {5: 2} if self.S == 4 else {n: n for n in range(self.S - 1)}
        for n in range(4 if self.S == 4 else 0, len(self.steps())):
            self.copy(n, True).wait_recv()
            if self.halves and n in ready:
                self.passing(ready[n], True).start()
        self.local(True).wait()
        for n in range(len(self.steps())):
            self.copy(n, False).wait_send()
        if self.halves:
            for n in range(self.S - 1):
                self.passing(n, True).wait_send()
                self.passing(n, False).wait_recv()


class GatherZ:
    def __init__(self, F, src, dst, sems):
        self.F, self.src, self.dst = F, src, dst
        self.send, self.recv, self.pass_send, self.pass_recv, self.own = sems
        self.f = lax.axis_index("fsdp")

    @staticmethod
    def sems(F):
        return [DMA((F // 2 - 1,)), DMA((F // 2 - 1,)), DMA((F // 2,)), DMA((F // 2,)), DMA]

    def sending(self, k):
        return push(
            self.src, self.dst.at[self.f], self.send.at[k - 1], self.recv.at[k - 1], {"fsdp": lax.rem(self.f + 2 * k, self.F)}
        )

    def landing(self, k):
        slot = lax.rem(self.f + self.F - 2 * k, self.F)
        return push(
            self.src, self.dst.at[slot], self.send.at[k - 1], self.recv.at[k - 1], {"fsdp": lax.rem(self.f + 2 * k, self.F)}
        )

    def passing(self, k, mine):
        f, F = self.f, self.F
        slot = lax.rem(f + F - 2 * k, F)
        other = f + 1 - 2 * lax.rem(f, 2)
        there = slot if mine else lax.rem(other + F - 2 * k, F)
        src = self.src if k == 0 else self.dst.at[slot]
        return push(src, self.dst.at[there], self.pass_send.at[k], self.pass_recv.at[k], sibling())

    def local(self):
        return pltpu.make_async_copy(self.src, self.dst.at[self.f], self.own)

    def start(self):
        for k in range(1, self.F // 2):
            self.sending(k).start()
        self.passing(0, True).start()
        self.local().start()

    def finish(self):
        for k in range(1, self.F // 2):
            self.landing(k).wait_recv()
            self.passing(k, True).start()
        self.local().wait()
        for k in range(1, self.F // 2):
            self.sending(k).wait_send()
        for k in range(self.F // 2):
            self.passing(k, True).wait_send()
            self.passing(k, False).wait_recv()


def first_kernel(S, F, heads, x_ref, ct_ref, wqkv_ref, ga_ref, gf_ref, pos_ref, freq_ref, x_all, ct_all, wqkv_all, gains_all, cos_ref, sin_ref, part, gains, *sems):
    s = lax.axis_index("sp")
    qw = heads * HD
    QW, KW = QUERY_HEADS * HD, KV_HEADS * HD
    kv = s // max(1, S // KV_HEADS)
    pair = kv // 2
    high = lax.rem(kv, 2)

    def cut(start):
        block = wqkv_ref[:, pl.ds(pl.multiple_of(start + pair * 128, 128), 128)].astype(f32)
        return jnp.where(high == 1, block[:, HD:], block[:, :HD])

    part[:, :qw] = wqkv_ref[:, pl.ds(pl.multiple_of(s * qw, 128), qw)]
    part[:, qw:] = jnp.concatenate([cut(QW), cut(QW + KW)], axis=1).astype(bf16)
    pad = jnp.zeros((14, ga_ref.shape[1]), f32)
    gains[...] = jnp.concatenate([ga_ref[...].astype(f32), gf_ref[...].astype(f32), pad], axis=0).astype(bf16)
    n = len(Gather.sems(S, shape((1, 1))))
    m = len(GatherZ.sems(F))
    move_x = Gather(S, x_ref, x_all, sems[:n])
    move_ct = Gather(S, ct_ref.at[:, pl.ds(0, ct_all.shape[2])], ct_all, sems[n : 2 * n])
    moves_z = [
        GatherZ(F, part, wqkv_all, sems[2 * n : 2 * n + m]),
        GatherZ(F, gains, gains_all, sems[2 * n + m :]),
    ]
    greet(S, F, True)
    move_x.start()
    for move in moves_z:
        move.start()
    angles = freq_ref[...] * pos_ref[...].astype(f32)
    cos_ref[...] = jnp.cos(angles)
    sin_ref[...] = jnp.sin(angles)
    move_x.relay()
    move_ct.start()
    move_x.finish(True)
    move_ct.relay()
    for move in moves_z:
        move.finish()
    move_ct.finish(True)


def first_gathers(S, F, x, ct, w_qkv, gain_attn, gain_ffn, positions, heads, collective):
    T, width = x.shape
    depth = w_qkv.shape[0]
    hw = (heads + 2) * HD
    length = positions.shape[1]
    frequency = jnp.asarray(10000.0 ** (-2.0 * np.arange(HD // 2) / HD), f32)[:, None]
    table = shape((HD // 2, length), f32)
    return pl.pallas_call(
        functools.partial(first_kernel, S, F, heads),
        in_specs=[ANY] * 2 + [VMEM] * 5,
        out_specs=[ANY] * 4 + [VMEM] * 2,
        out_shape=[
            shape((S, T, width)),
            shape((S, T, width // 4)),
            shape((F, depth, hw)),
            shape((F, 16, depth)),
            table,
            table,
        ],
        scratch_shapes=[pltpu.VMEM((depth, hw), bf16), pltpu.VMEM((16, depth), bf16)]
        + Gather.sems(S, x)
        + Gather.sems(S, shape((T, width // 4)))
        + GatherZ.sems(F) * 2,
        compiler_params=params(collective),
        cost_estimate=cost(45),
    )(x, ct, w_qkv, gain_attn, gain_ffn, positions, frequency)


def columns_kernel(S, F, gate_hbm, up_hbm, out_hbm, buf, sem_in, sem_out):
    s = lax.axis_index("sp")
    piece = buf.shape[2] // F
    ins = []
    for n, ref in enumerate((gate_hbm, up_hbm)):
        for m in range(F):
            src = ref.at[:, pl.ds(pl.multiple_of((m * S + hidden_block(S, s, m // 2)) * piece, piece), piece)]
            ins.append(pltpu.make_async_copy(src, buf.at[n, :, pl.ds(m * piece, piece)], sem_in.at[n * F + m]))
    for copy in ins:
        copy.start()
    outs = []
    for n in range(2):
        for copy in ins[n * F : (n + 1) * F]:
            copy.wait()
        outs.append(pltpu.make_async_copy(buf.at[n], out_hbm.at[n], sem_out.at[n]))
        outs[-1].start()
    for copy in outs:
        copy.wait()


def own_columns(S, F, s, w_gate, w_up):
    depth, FF = w_gate.shape
    piece = FF // (S * F)
    if piece % 128:
        def pick(w):
            starts = [(m * S + hidden_block(S, s, m // 2)) * piece for m in range(F)]
            return jnp.concatenate([lax.dynamic_slice_in_dim(w, at, piece, 1) for at in starts], axis=1)

        return jnp.stack([pick(w_gate), pick(w_up)])
    return pl.pallas_call(
        functools.partial(columns_kernel, S, F),
        in_specs=[ANY, ANY],
        out_specs=ANY,
        out_shape=shape((2, depth, FF // S)),
        scratch_shapes=[pltpu.VMEM((2, depth, FF // S), bf16), DMA((2 * F,)), DMA((2,))],
        compiler_params=params(),
        cost_estimate=cost(3),
    )(w_gate, w_up)


def forward_kernel(S, F, heads, x_ref, g_ref, w_ref, pos_ref, cos_ref, sin_ref, gq_ref, gk_ref, wout_ref, ct_ref, normed_t_ref, raw_ref, rot_ref, lse_ref, mix_t_ref, mix_all, wout_all, ct_all, k_buf, vt_buf, mix_buf, mix_send, mix_recv, mix_own, wout_s, *sems):
    i = pl.program_id(0)
    s = lax.axis_index("sp")
    qw = heads * HD
    half = HD // 2
    blocks = pl.num_programs(0)
    n_z = len(GatherZ.sems(F))
    rows_o = wout_s.shape[1]
    own_out = wout_ref.at[pl.ds(pl.multiple_of(s * rows_o, rows_o), rows_o)]
    move_z = GatherZ(F, own_out, wout_s, sems[:n_z])
    n_w = n_z + len(Gather.sems(S, None, True))
    move = Gather(S, wout_s, wout_all, sems[n_z:n_w], halves=True, inner=True, staged=False)
    move_ct = Gather(S, ct_ref.at[:, pl.ds(ct_all.shape[2], ct_all.shape[2])], ct_all, sems[n_w:])

    @pl.when(i == 0)
    def _():
        greet(S, F, True)
        move_z.start()
        move_ct.start()

    @pl.when(i == blocks - 1)
    def _():
        move_ct.relay()

    x = x_ref[...].astype(f32)
    scale = lax.rsqrt(jnp.mean(x * x, axis=-1, keepdims=True) + EPS)
    scaled = x * scale * gain_row(g_ref, 0)
    normed = scaled.astype(bf16)
    normed_t_ref[...] = scaled.T.astype(bf16)
    raw = dot(normed, w_ref[...]).T
    raw_ref[...] = raw
    cosine, sine = cos_ref[...], sin_ref[...]

    def prep(u, gain):
        n = u * lax.rsqrt(jnp.mean(u * u, axis=0, keepdims=True) + EPS) * gain
        front, back = n[:half], n[half:]
        return jnp.concatenate([front * cosine - back * sine, back * cosine + front * sine], axis=0)

    q = [prep(raw[h * HD : (h + 1) * HD], gq_ref[...]).astype(bf16) for h in range(heads)]
    kt = prep(raw[qw : qw + HD], gk_ref[...])
    vt = raw[qw + HD :].astype(bf16)
    rot_ref[...] = jnp.concatenate(q + [kt.astype(bf16), vt], axis=0)
    steps = mix_buf.shape[0]

    x_mate, y_mate, d_mate = mates(s)

    def mix_copy(block, k, here):
        rows = pl.ds(block * BLOCK, BLOCK)
        n = block * (S - 1) + k - 1
        if S != 4:
            slot = lax.rem(s + S - k, S) if here else s
            return push(mix_buf.at[block], mix_all.at[slot, rows], mix_send.at[n], mix_recv.at[n], {"sp": lax.rem(s + k, S)})
        if k < 3:
            mate = x_mate if k == 1 else y_mate
            slot = mate if here else s
            return push(mix_buf.at[block], mix_all.at[slot, rows], mix_send.at[n], mix_recv.at[n], {"sp": mate})
        source, mate = (x_mate, y_mate) if block < steps // 2 else (y_mate, x_mate)
        slot = d_mate if here else source
        return push(mix_all.at[source, rows], mix_all.at[slot, rows], mix_send.at[n], mix_recv.at[n], {"sp": mate})

    def mix_local(block):
        return pltpu.make_async_copy(mix_buf.at[block], mix_all.at[s, pl.ds(block * BLOCK, BLOCK)], mix_own.at[block])

    for step in range(steps):

        @pl.when(i == step)
        def _():
            n = (step + 1) * BLOCK
            k_buf[step * BLOCK : n, :] = kt.T.astype(bf16)
            vt_buf[:, step * BLOCK : n] = vt
            col = lax.broadcasted_iota(jnp.int32, (n, BLOCK), 0)
            row = step * BLOCK + lax.broadcasted_iota(jnp.int32, (n, BLOCK), 1)
            bias = jnp.where((col <= row) & (row - col <= pos_ref[...]), 0.0, -1e30)
            keys, values = k_buf[:n, :], vt_buf[:, :n]
            mixes, lses = [], []
            for h in range(heads):
                e = jnp.exp(dot(keys, q[h] * 0.125) + bias)
                total = jnp.sum(e, axis=0, keepdims=True)
                p = (e * (1.0 / total)).astype(bf16)
                mixes.append(dot(values, p))
                lses.append(jnp.log(total))
            mix = jnp.concatenate(mixes, axis=0)
            mix_t_ref[...] = mix.astype(bf16)
            lse_ref[...] = jnp.concatenate(lses + [jnp.zeros((8 - heads, BLOCK), f32)], axis=0)
            mix_buf[step] = mix.T.astype(bf16)
            for k in range(1, 3 if S == 4 else S):
                mix_copy(step, k, False).start()
            mix_local(step).start()

    @pl.when(i == blocks - 1)
    def _():
        move_z.finish()
        move.start()
        for block in range(steps):
            for k in range(1, 3 if S == 4 else S):
                mix_copy(block, k, True).wait_recv()
                if S == 4 and k == (1 if block < steps // 2 else 2):
                    mix_copy(block, 3, False).start()
        move.relay()
        for block in range(steps):
            if S == 4:
                mix_copy(block, 3, True).wait_recv()
            for k in range(1, S):
                mix_copy(block, k, False).wait_send()
            mix_local(block).wait()
        move.finish(True)
        move_ct.finish(True)


def forward_attention(S, F, x, gain, w, pos, cosine, sine, gain_q, gain_k, wout, ct, heads, collective):
    length, width = x.shape
    hw = w.shape[1]
    qw = heads * HD
    steps = length // BLOCK
    full = lambda i: (0, 0)
    rows = lambda i: (i, 0)
    cols = lambda i: (0, i)
    return pl.pallas_call(
        functools.partial(forward_kernel, S, F, heads),
        grid=(steps,),
        in_specs=[
            pl.BlockSpec((BLOCK, width), rows),
            pl.BlockSpec(gain.shape, lambda i: (0, 0, 0)),
            pl.BlockSpec((width, hw), full),
            pl.BlockSpec((1, BLOCK), cols),
            pl.BlockSpec((HD // 2, BLOCK), cols),
            pl.BlockSpec((HD // 2, BLOCK), cols),
            pl.BlockSpec((HD, 1), full),
            pl.BlockSpec((HD, 1), full),
            pl.BlockSpec(wout.shape, full),
            ANY,
        ],
        out_specs=[
            pl.BlockSpec((width, BLOCK), cols),
            pl.BlockSpec((hw, BLOCK), cols),
            pl.BlockSpec((hw, BLOCK), cols),
            pl.BlockSpec((8, BLOCK), cols),
            pl.BlockSpec((qw, BLOCK), cols),
            ANY,
            ANY,
            ANY,
        ],
        out_shape=[
            shape((width, length)),
            shape((hw, length), f32),
            shape((hw, length)),
            shape((8, length), f32),
            shape((qw, length)),
            shape((S, length, qw)),
            shape((F, S, wout.shape[0] // S, width)),
            shape((S,) + ct.shape[:1] + (width // 4,)),
        ],
        scratch_shapes=[
            pltpu.VMEM((length, HD), bf16),
            pltpu.VMEM((HD, length), bf16),
            pltpu.VMEM((steps, BLOCK, qw), bf16),
            DMA((steps * (S - 1),)),
            DMA((steps * (S - 1),)),
            DMA((steps,)),
            pltpu.VMEM((F, wout.shape[0] // S, width), bf16),
        ]
        + GatherZ.sems(F)
        + Gather.sems(S, None, True)
        + Gather.sems(S, shape((ct.shape[0], width // 4))),
        compiler_params=params(collective, 1),
        cost_estimate=cost(45),
    )(x, gain, w, pos, cosine, sine, gain_q, gain_k, wout, ct)


def middle_kernel(S, T, x_ref, mix_ref, wout_ref, g_ref, ct_ref, mid_ref, ffn_ref, ffn_t_ref, ct_all, *sems):
    i = pl.program_id(0)
    s = lax.axis_index("sp")
    move = Gather(S, ct_ref.at[:, pl.ds(ct_all.shape[2], ct_all.shape[2])], ct_all, sems)

    @pl.when(i == 0)
    def _():
        greet(S)
        move.start()

    @pl.when(i == pl.num_programs(0) - 2)
    def _():
        move.relay()

    middle = x_ref[...].astype(f32)
    total = dot(mix_ref[0], wout_ref[0])
    for j in range(1, S):
        total += dot(mix_ref[j], wout_ref[j])
    middle = middle + total

    @pl.when(i == s)
    def _():
        mid_ref[...] = middle

    scaled = middle * lax.rsqrt(jnp.mean(middle * middle, axis=-1, keepdims=True) + EPS) * gain_row(g_ref, 1)
    ffn_ref[...] = scaled.astype(bf16)
    ffn_t_ref[...] = scaled.T.astype(bf16)

    @pl.when(i == pl.num_programs(0) - 1)
    def _():
        move.finish(True)


def middle_rows(S, x, mix_all, wout_all, gain, ct, collective):
    length, width = x.shape
    T = length // S
    qw = mix_all.shape[2]
    return pl.pallas_call(
        functools.partial(middle_kernel, S, T),
        grid=(S,),
        in_specs=[
            pl.BlockSpec((T, width), lambda i: (i, 0)),
            pl.BlockSpec((S, T, qw), lambda i: (0, i, 0)),
            pl.BlockSpec((S, qw, width), lambda i: (0, 0, 0)),
            pl.BlockSpec(gain.shape, lambda i: (0, 0, 0)),
            ANY,
        ],
        out_specs=[
            pl.BlockSpec((T, width), lambda i: (0, 0)),
            pl.BlockSpec((T, width), lambda i: (i, 0)),
            pl.BlockSpec((width, T), lambda i: (0, i)),
            ANY,
        ],
        out_shape=[shape((T, width), f32), shape((length, width)), shape((width, length)), shape((S, T, width // 2))],
        scratch_shapes=Gather.sems(S, shape((T, width // 2))),
        compiler_params=params(collective, 1),
        cost_estimate=cost(45),
    )(x, mix_all, wout_all, gain, ct)


def ffn_kernel(S, F, ffn_ref, cta_ref, ctb_ref, ctc_ref, wg_ref, wu_ref, wqkv_hbm, gate_ref, up_ref, hid_ref, down_ref, wqkv_all, *sems):
    i = pl.program_id(0)
    last = pl.num_programs(0) - 1
    s = lax.axis_index("sp")
    move = Gather(S, wqkv_hbm.at[pl.ds(0, wqkv_all.shape[1])], wqkv_all, sems, halves=True)

    @pl.when(i == 0)
    def _():
        greet(S, 0, True)
        move.start()

    @pl.when(i == last - 1)
    def _():
        move.relay()

    @pl.when(i == last)
    def _():
        move.spread()

    length, width = ffn_ref.shape
    rows = ffn_ref[...]
    gate, up = dot(rows, wg_ref[...].reshape(width, BLOCK)), dot(rows, wu_ref[...].reshape(width, BLOCK))
    gate_ref[...] = gate
    up_ref[...] = up
    hidden = gate / (1.0 + jnp.exp(-gate)) * up
    hid_ref[...] = hidden.astype(bf16)
    flipped = hidden.T.astype(bf16)
    piece = down_ref.shape[1]
    at = 0
    for ref in (cta_ref, ctb_ref, ctc_ref):
        cut = slice(at, at + ref.shape[1])
        at += ref.shape[1]
        part = dot(flipped, ref[...]).astype(bf16)
        for m in range(BLOCK // piece):
            block = i * (BLOCK // piece) + m
            owner = lax.rem(block, 2) * S + hidden_block(S, s, block // 2)
            down_ref[owner, :, cut] = part[m * piece : (m + 1) * piece]

    @pl.when(i == last)
    def _():
        move.finish(True, True)


def ffn_forward(S, ffn_in, cts, w_gu, wqkv_s, collective):
    length, width = ffn_in.shape
    F, _, depth, FFs = w_gu.shape
    whole = lambda i: (0, 0)
    col = pl.BlockSpec((length, BLOCK), lambda i: (0, i))
    return pl.pallas_call(
        functools.partial(ffn_kernel, S, F),
        grid=(FFs // BLOCK,),
        in_specs=[
            pl.BlockSpec((length, width), whole),
            *[pl.BlockSpec(ct.shape, whole) for ct in cts],
            pl.BlockSpec((F, 1, depth, BLOCK), lambda i: (0, 0, 0, i)),
            pl.BlockSpec((F, 1, depth, BLOCK), lambda i: (0, 1, 0, i)),
            ANY,
        ],
        out_specs=[col, col, col, pl.BlockSpec((F, FFs // F, width), lambda i: (0, 0, 0)), ANY],
        out_shape=[
            shape((length, FFs), f32),
            shape((length, FFs), f32),
            shape((length, FFs)),
            shape((F, FFs // F, width)),
            shape((S, width // 2, wqkv_s.shape[1])),
        ],
        scratch_shapes=Gather.sems(S, shape((width // 2, wqkv_s.shape[1])), True),
        compiler_params=params(collective, 1),
        cost_estimate=cost(20),
    )(ffn_in, *cts, w_gu, w_gu, wqkv_s)


def ffn_back_kernel(S, F, cta_ref, ctb_ref, ctc_ref, wd_ref, gate_ref, up_ref, ffn_t_ref, wqkv_ref, hid_hbm, wd_hbm, dgu_ref, pgu_ref, wqkv_all, *refs):
    i = pl.program_id(0)
    last = pl.num_programs(0) - 1
    s = lax.axis_index("sp")
    split = S == 4
    if split:
        across, hid, wd, send_buf, send, recv, load = refs[:7]
        x_mate, y_mate, d_mate = mates(s)
        T = send_buf.shape[0]
        loads = [
            pltpu.make_async_copy(hid_hbm.at[pl.ds(pl.multiple_of(d_mate * T, T), T)], hid, load.at[0]),
            pltpu.make_async_copy(wd_hbm, wd, load.at[1]),
        ]
        low, high = pl.ds(0, T // 2), pl.ds(T // 2, T // 2)
        ahead = [
            push(send_buf.at[low], across.at[low], send.at[0], recv.at[0], {"sp": y_mate}),
            push(send_buf.at[high], across.at[high], send.at[1], recv.at[1], {"sp": x_mate}),
        ]
    depth = wqkv_all.shape[1]
    move = Gather(S, wqkv_ref.at[pl.ds(depth, depth)], wqkv_all, refs[7 if split else 0 :], halves=True)

    @pl.when(i == 0)
    def _():
        greet(S, 0, True)
        move.start()
        if split:
            for copy in loads:
                copy.start()

    @pl.when(i == last - 1)
    def _():
        move.relay()

    @pl.when(i == last)
    def _():
        move.spread()

    cot = jnp.concatenate([cta_ref[...], ctb_ref[...], ctc_ref[...]], axis=1)
    gh = dot_nt(cot, wd_ref[...])
    gate, up = gate_ref[...], up_ref[...]
    sig = 1.0 / (1.0 + jnp.exp(-gate))
    d_gate = (gh * up * sig * (1.0 + gate * (1.0 - sig))).astype(bf16)
    d_up = (gh * (gate * sig)).astype(bf16)
    dgu_ref[0] = d_gate
    dgu_ref[1] = d_up
    ffn_t = ffn_t_ref[...]
    rows = pgu_ref.shape[3]
    for n, d in enumerate((d_gate, d_up)):
        part = dot(ffn_t, d).astype(bf16)
        for j in range(S):
            for m in range(F):
                pgu_ref[m, j, n] = part[(j * F + m) * rows : (j * F + m + 1) * rows]

    if split:

        @pl.when(i == 0)
        def _():
            for copy in loads:
                copy.wait()
            for c in range(0, wd.shape[1], 512):
                send_buf[:, c : c + 512] = dot(hid[...], wd[:, c : c + 512]).astype(bf16)
            for copy in ahead:
                copy.start()

    @pl.when(i == last)
    def _():
        move.finish(True, True)
        if split:
            for copy in ahead:
                copy.wait_recv()
                copy.wait_send()


def ffn_backward(S, F, cts, w_dn, gate, up, ffn_t, wqkv_s, hidden, collective):
    length, FFs = gate.shape
    width = w_dn.shape[1]
    tiles = FFs // BLOCK
    rows = width // (S * F)
    whole = lambda i: (0, 0)
    col = lambda i: (0, i)
    T = length // S
    if S == 4:
        extra = [shape((T, width))]
        scratch = [pltpu.VMEM((T, FFs), bf16), pltpu.VMEM((FFs, width), bf16), pltpu.VMEM((T, width), bf16)]
        scratch += [DMA((2,)), DMA((2,)), DMA((2,))]
    else:
        extra, scratch = [], []
    return pl.pallas_call(
        functools.partial(ffn_back_kernel, S, F),
        grid=(tiles,),
        in_specs=[
            *[pl.BlockSpec(ct.shape, whole) for ct in cts],
            pl.BlockSpec((BLOCK, width), lambda i: (i, 0)),
            pl.BlockSpec((length, BLOCK), col),
            pl.BlockSpec((length, BLOCK), col),
            pl.BlockSpec((width, length), whole),
            ANY,
            ANY,
            ANY,
        ],
        out_specs=[
            pl.BlockSpec((2, length, BLOCK), lambda i: (0, 0, i)),
            pl.BlockSpec((F, S, 2, rows, BLOCK), lambda i: (0, 0, 0, 0, i)),
            ANY,
        ]
        + [ANY] * len(extra),
        out_shape=[shape((2, length, FFs)), shape((F, S, 2, rows, FFs)), shape((S, width // 2, wqkv_s.shape[1]))] + extra,
        scratch_shapes=scratch + Gather.sems(S, shape((width // 2, wqkv_s.shape[1])), True),
        compiler_params=params(collective, 1),
        cost_estimate=cost(1),
    )(*cts, w_dn, gate, up, ffn_t, wqkv_s, hidden, w_dn)


def sum_over_sp(S, compute, acc, send_buf, recv_buf, send, recv, between=None, across=None):
    s = lax.axis_index("sp")
    if S != 4:

        def copy(k):
            return push(
                send_buf.at[k - 1], recv_buf.at[k - 1], send.at[k - 1], recv.at[k - 1], {"sp": lax.rem(s + k, S)}
            )

        for k in range(1, S):
            compute(lax.rem(s + k, S), send_buf.at[k - 1])
            copy(k).start()
        compute(s, acc)
        if between is not None:
            between()
        for k in range(1, S):
            copy(k).wait_recv()
            acc[...] += recv_buf[k - 1].astype(f32)
        return [copy(k) for k in range(1, S)]

    x, y, d = mates(s)
    half = acc.shape[0] // 2
    low, high = pl.ds(0, half), pl.ds(half, half)
    if across is not None:

        def whole(n):
            return push(send_buf.at[n], recv_buf.at[n], send.at[n], recv.at[n], {"sp": x if n == 0 else y})

        compute(x, acc)
        send_buf[0, half:] = acc[half:].astype(bf16)
        send_buf[0, :half] = (acc[:half] + across[:half].astype(f32)).astype(bf16)
        whole(0).start()
        compute(y, acc)
        send_buf[1, :half] = acc[:half].astype(bf16)
        send_buf[1, half:] = (acc[half:] + across[half:].astype(f32)).astype(bf16)
        whole(1).start()
        compute(s, acc)
        if between is not None:
            between()
        for n in range(2):
            whole(n).wait_recv()
        acc[...] += recv_buf[0].astype(f32) + recv_buf[1].astype(f32)
        return [whole(n) for n in range(2)]

    def copy(n):
        buf, rows, target = [(0, low, y), (0, high, x), (1, high, x), (2, low, y), (1, low, x), (2, high, y)][n]
        return push(send_buf.at[buf, rows], recv_buf.at[buf, rows], send.at[n], recv.at[n], {"sp": target})

    compute(d, send_buf.at[0])
    copy(0).start()
    copy(1).start()
    compute(x, send_buf.at[1])
    copy(2).start()
    compute(y, send_buf.at[2])
    copy(3).start()
    copy(0).wait_recv()
    send_buf[1, :half] = (send_buf[1, :half].astype(f32) + recv_buf[0, :half].astype(f32)).astype(bf16)
    copy(4).start()
    copy(1).wait_recv()
    send_buf[2, half:] = (send_buf[2, half:].astype(f32) + recv_buf[0, half:].astype(f32)).astype(bf16)
    copy(5).start()
    compute(s, acc)
    if between is not None:
        between()
    for n in range(2, 6):
        copy(n).wait_recv()
    acc[...] += recv_buf[1].astype(f32) + recv_buf[2].astype(f32)
    return [copy(n) for n in range(6)]


def middle_back_kernel(S, F, dgu_hbm, wgu_hbm, wout_hbm, mid_hbm, ct_hbm, g_ref, gm_ref, dattn_ref, gg_ref, dmix_ref, dgu, wgu, wout, mid, ct, acc, send_buf, recv_buf, send, recv, load):
    s = lax.axis_index("sp")
    T, width = mid.shape
    depth = wgu.shape[2]
    greet(S)
    if S == 4:
        x, y, d = mates(s)
        order = [d, x, y, s]
    else:
        order = [lax.rem(s + k, S) for k in range(1, S)] + [s]

    def chunk_load(n):
        rows = pl.ds(pl.multiple_of(order[n] * T, T), T)
        return pltpu.make_async_copy(dgu_hbm.at[:, rows], dgu.at[n], load.at[n])

    def weight_load(c):
        return pltpu.make_async_copy(wgu_hbm.at[c], wgu.at[c], load.at[S + c])

    others = [
        pltpu.make_async_copy(mid_hbm, mid, load.at[S + F]),
        pltpu.make_async_copy(ct_hbm, ct, load.at[S + F + 1]),
        pltpu.make_async_copy(wout_hbm, wout, load.at[S + F + 2]),
    ]
    chunk_load(0).start()
    for c in range(F):
        weight_load(c).start()
    for n in range(1, S):
        chunk_load(n).start()
    for copy in others:
        copy.start()
    calls = []

    def compute(chunk, out):
        n = len(calls)
        calls.append(n)
        chunk_load(n).wait()
        for c in range(F):
            if n == 0:
                weight_load(c).wait()
            part = dot_nt(dgu[n, 0], wgu[c, 0]) + dot_nt(dgu[n, 1], wgu[c, 1])
            out[:, c * depth : (c + 1) * depth] = part.astype(out.dtype)

    copies = sum_over_sp(S, compute, acc, send_buf, recv_buf, send, recv)
    for copy in others:
        copy.wait()
    v, e = mid[...], acc[...]
    r = lax.rsqrt(jnp.mean(v * v, axis=-1, keepdims=True) + EPS)
    gg_ref[...] = jnp.sum(e * v * r, axis=0, keepdims=True)
    ge = gain_row(g_ref, 1) * e
    gm = ct[...].astype(f32) + r * ge - v * (r * r * r * jnp.mean(ge * v, axis=-1, keepdims=True))
    gm_ref[...] = gm
    d_attn = gm.astype(bf16)
    dattn_ref[...] = d_attn

    for j in range(S):
        dmix_ref[j] = dot_nt(d_attn, wout[j]).astype(bf16)
    for copy in copies:
        copy.wait_send()


def middle_back(S, dgu, w_gu, wout_all, mid, gain, ct, collective):
    T, width = mid.shape
    F = w_gu.shape[0]
    FFs = dgu.shape[2]
    qw = wout_all.shape[1]
    n = max(6, S - 1)
    return pl.pallas_call(
        functools.partial(middle_back_kernel, S, F),
        in_specs=[ANY] * 5 + [VMEM],
        out_specs=[VMEM] * 4,
        out_shape=[shape((T, width), f32), shape((T, width)), shape((1, width), f32), shape((S, T, qw))],
        scratch_shapes=[
            pltpu.VMEM((S, 2, T, FFs), bf16),
            pltpu.VMEM(w_gu.shape, bf16),
            pltpu.VMEM(wout_all.shape, bf16),
            pltpu.VMEM((T, width), f32),
            pltpu.VMEM((T, width), bf16),
            pltpu.VMEM((T, width), f32),
            pltpu.VMEM((S - 1, T, width), bf16),
            pltpu.VMEM((S - 1, T, width), bf16),
            DMA((n,)),
            DMA((n,)),
            DMA((S + F + 3,)),
        ],
        compiler_params=params(collective),
        cost_estimate=cost(1),
    )(dgu, w_gu, wout_all, mid, ct, gain)


def attn_back_kernel(S, F, heads, rot_ref, raw_ref, lse_ref, pos_ref, cos_ref, sin_ref, gq_ref, gk_ref, g_ref, ggf_ref, mix_t_ref, x_hbm, gm_hbm, normed_hbm, wqkv0_hbm, wqkv1_hbm, dattn_hbm, dmix_hbm, packed_ref, gin_ref, k_buf, v_buf, dk_acc, dv_acc, gg, dproj, dattn_all, got, x, gm, normed_t, wqkv, dmix_all, send, recv, load, mix_send, mix_recv, *sems):
    i = pl.program_id(0)
    s = lax.axis_index("sp")
    qw = heads * HD
    hw = qw + 2 * HD
    half = HD // 2
    length = rot_ref.shape[1]
    T, width = gin_ref.shape
    move = Gather(S, dattn_hbm, dattn_all, sems)
    loads = [
        pltpu.make_async_copy(a, b, load.at[n])
        for n, (a, b) in enumerate(
            [
                (normed_hbm, normed_t),
                (wqkv0_hbm, wqkv.at[:, pl.ds(0, width // 2)]),
                (wqkv1_hbm, wqkv.at[:, pl.ds(width // 2, width // 2)]),
                (x_hbm, x),
                (gm_hbm, gm),
            ]
        )
    ]

    def mix_copy(k, slot):
        return to_peer(dmix_hbm.at[lax.rem(s + k, S)], dmix_all.at[slot], mix_send.at[k - 1], mix_recv.at[k - 1], k, S)

    mix_own = pltpu.make_async_copy(dmix_hbm.at[s], dmix_all.at[s], load.at[5])

    @pl.when(i == 0)
    def _():
        greet(S)
        for k in range(1, S):
            mix_copy(k, s).start()
        mix_own.start()
        move.start()
        for copy in loads:
            copy.start()
        k_buf[...] = rot_ref[qw : qw + HD, :].astype(f32).T.astype(bf16)
        v_buf[...] = rot_ref[qw + HD :, :].astype(f32).T.astype(bf16)
        dk_acc[...] = jnp.zeros_like(dk_acc)
        dv_acc[...] = jnp.zeros_like(dv_acc)
        gg[...] = jnp.zeros_like(gg)
        mix_own.wait()
        for k in range(1, S):
            mix_copy(k, lax.rem(s + S - k, S)).wait_recv()

    @pl.when(i == pl.num_programs(0) - 1)
    def _():
        move.relay()

    def unprep(e, u, gain, cosine, sine):
        front, back = e[:half], e[half:]
        e = jnp.concatenate([front * cosine + back * sine, back * cosine - front * sine], axis=0)
        r = lax.rsqrt(jnp.mean(u * u, axis=0, keepdims=True) + EPS)
        ge = gain * e
        du = r * ge - u * (r * r * r * jnp.mean(ge * u, axis=0, keepdims=True))
        return du, jnp.sum(e * u * r, axis=1, keepdims=True)

    for step in range(length // BLOCK):

        @pl.when(i == step)
        def _():
            n = (step + 1) * BLOCK
            here = slice(step * BLOCK, n)
            col = lax.broadcasted_iota(jnp.int32, (n, BLOCK), 0)
            row = step * BLOCK + lax.broadcasted_iota(jnp.int32, (n, BLOCK), 1)
            bias = jnp.where((col <= row) & (row - col <= pos_ref[:, here]), 0.0, -1e30)
            keys, values = k_buf[:n, :], v_buf[:n, :]
            kt = rot_ref[qw : qw + HD, :n]
            per = BLOCK // T
            dmix = dmix_all[step] if per == 1 else jnp.concatenate([dmix_all[step * per + j] for j in range(per)], axis=0)
            dmix_t = dmix.astype(f32).T.astype(bf16)
            qt = rot_ref[:qw, here]
            q = qt.astype(f32).T.astype(bf16)
            cosine, sine = cos_ref[:, here], sin_ref[:, here]
            dqs, gain_sum = [], jnp.zeros((HD, 1), f32)
            dk, dv = jnp.zeros((n, HD), f32), jnp.zeros((n, HD), f32)
            for h in range(heads):
                part = slice(h * HD, (h + 1) * HD)
                p = jnp.exp(dot(keys, qt[part] * 0.125) + bias - lse_ref[h : h + 1, here])
                dv += dot(p.astype(bf16), dmix[:, part])
                dp = dot(values, dmix_t[part])
                inner = jnp.sum(dp * p, axis=0, keepdims=True)
                ds = (p * (dp - inner)).astype(bf16)
                dk += dot(ds, q[:, part])
                dq = (dot(kt, ds) * 0.125).astype(bf16).astype(f32)
                du, dg = unprep(dq, raw_ref[part, here], gq_ref[...], cosine, sine)
                dqs.append(du)
                gain_sum += dg
            dk_acc[:n, :] += dk
            dv_acc[:n, :] += dv
            gg[:, :1] += gain_sum
            dproj[here, :qw] = jnp.concatenate(dqs, axis=0).T.astype(bf16)

    def exchange(k, slot):
        rows = pl.ds(pl.multiple_of(lax.rem(s + k, S) * T, T), T)
        return to_peer(dproj.at[rows], got.at[slot], send.at[k - 1], recv.at[k - 1], k, S)

    @pl.when(i == pl.num_programs(0) - 1)
    def _():
        dk = (dk_acc[...] * 0.125).astype(bf16).astype(f32).T
        du, dg = unprep(dk, raw_ref[qw : qw + HD, :], gk_ref[...], cos_ref[...], sin_ref[...])
        gg[:, 1:2] += dg
        dproj[:, qw:] = jnp.concatenate([du.T, dv_acc[...].astype(bf16).astype(f32)], axis=1).astype(bf16)
        for k in range(1, S):
            exchange(k, s).start()
        W = 128
        rows_d, rows_o = width // (S * F), qw // F
        blocks = hw // W
        n_q, n_o = S * rows_d * blocks, rows_o * width // W
        tile = 512
        for copy in loads:
            copy.wait()
        d_all = dproj[...]
        for c in range(0, width, tile):
            part = dot(normed_t[c : c + tile, :], d_all).astype(bf16)
            for b in range(tile // rows_d):
                j, m = divmod(c // rows_d + b, F)
                for cb in range(blocks):
                    at = (j * blocks + cb) * rows_d
                    packed_ref[m, at : at + rows_d] = part[b * rows_d : (b + 1) * rows_d, cb * W : (cb + 1) * W]
        e = dot_nt(dproj[pl.ds(pl.multiple_of(s * T, T), T), :], wqkv[s])
        for k in range(1, S):
            slot = lax.rem(s + S - k, S)
            exchange(k, slot).wait_recv()
            e += dot_nt(got[slot], wqkv[slot])
        v = x[...].astype(f32)
        r = lax.rsqrt(jnp.mean(v * v, axis=-1, keepdims=True) + EPS)
        ga = jnp.sum(e * v * r, axis=0, keepdims=True)
        ge = gain_row(g_ref, 0) * e
        gin_ref[...] = gm[...] + r * ge - v * (r * r * r * jnp.mean(ge * v, axis=-1, keepdims=True))
        heads_t = gg[...].T
        second = jnp.concatenate([heads_t[0:1], heads_t[1:2]], axis=1)
        gf = ggf_ref[...]
        for j in range(S):
            for m in range(F):
                cut = slice((j * F + m) * rows_d, (j * F + m + 1) * rows_d)
                first = [ga[:, cut], gf[:, cut]]
                if 2 * rows_d < W:
                    first.append(jnp.zeros((1, W - 2 * rows_d), f32))
                rows = jnp.concatenate([jnp.concatenate(first, axis=1), second, jnp.zeros((14, W), f32)], axis=0)
                packed_ref[m, n_q + n_o + 16 * j : n_q + n_o + 16 * (j + 1)] = rows.astype(bf16)
        move.finish(True)
        mix_t = mix_t_ref[...]
        for c in range(0, width, tile):
            part = jnp.zeros((qw, tile), f32)
            for j in range(S):
                part += dot(mix_t[:, j * T : (j + 1) * T], dattn_all[j, :, c : c + tile])
            for m in range(F):
                cuts = [part[m * rows_o : (m + 1) * rows_o, cb * W : (cb + 1) * W] for cb in range(tile // W)]
                at = n_q + c // W * rows_o
                packed_ref[m, at : at + rows_o * tile // W] = jnp.concatenate(cuts, axis=0).astype(bf16)
        for k in range(1, S):
            exchange(k, s).wait_send()
            mix_copy(k, s).wait_send()


def attention_back(S, F, dmix, rot, raw, lse, pos, cosine, sine, gain_q, gain_k, gain, grad_gf, mix_t, x, gm, normed_t, wqkv0, wqkv1, d_attn, heads, collective):
    length = rot.shape[1]
    hw = rot.shape[0]
    T, width = x.shape
    rows_d, rows_o = width // (S * F), heads * HD // F
    total = S * rows_d * hw // 128 + rows_o * width // 128 + 16 * S
    whole = lambda a: pl.BlockSpec(a.shape, lambda i: (0,) * a.ndim)
    return pl.pallas_call(
        functools.partial(attn_back_kernel, S, F, heads),
        grid=(length // BLOCK,),
        in_specs=[whole(a) for a in (rot, raw, lse, pos, cosine, sine, gain_q, gain_k, gain, grad_gf, mix_t)] + [ANY] * 7,
        out_specs=[pl.BlockSpec((F, total, 128), lambda i: (0, 0, 0)), pl.BlockSpec((T, width), lambda i: (0, 0))],
        out_shape=[shape((F, total, 128)), shape((T, width), f32)],
        scratch_shapes=[
            pltpu.VMEM((length, HD), bf16),
            pltpu.VMEM((length, HD), bf16),
            pltpu.VMEM((length, HD), f32),
            pltpu.VMEM((length, HD), f32),
            pltpu.VMEM((HD, 128), f32),
            pltpu.VMEM((length, hw), bf16),
            pltpu.VMEM((S, T, width), bf16),
            pltpu.VMEM((S, T, hw), bf16),
            pltpu.VMEM((T, width), bf16),
            pltpu.VMEM((T, width), f32),
            pltpu.VMEM(normed_t.shape, bf16),
            pltpu.VMEM((S, width, hw), bf16),
            pltpu.VMEM(dmix.shape, bf16),
            DMA((S - 1,)),
            DMA((S - 1,)),
            DMA((6,)),
            DMA((S - 1,)),
            DMA((S - 1,)),
        ]
        + Gather.sems(S, d_attn),
        compiler_params=params(collective, 1),
        cost_estimate=cost(1),
    )(rot, raw, lse, pos, cosine, sine, gain_q, gain_k, gain, grad_gf, mix_t, x, gm, normed_t, wqkv0, wqkv1, d_attn, dmix)


def sum_kernel(S, F, heads, early, hid_ref, wd_ref, mid_ref, gu_hbm, down_hbm, packed_hbm, *refs):
    across = refs[0] if early else None
    refs = refs[early:]
    (
        out_ref, qkv_ref, gout_ref, tiny_ref, down_out, got_hbm, got, gu_send, gu_recv, gu_own, acc, send_buf, recv_buf, packed, twin, pairs, from_z, mine, mine_all,
        send, recv, far, load, twin_send, twin_recv, z_send, z_recv, end_sems,
    ) = refs
    s, f = lax.axis_index("sp"), lax.axis_index("fsdp")
    T, width = mid_ref.shape
    W = 128
    chips = F // 2
    core = lax.rem(f, 2)
    tile = 512

    def exchange(k, slot):
        return to_peer(gu_hbm.at[lax.rem(s + k, S)], got.at[slot], gu_send.at[k - 1], gu_recv.at[k - 1], k, S)

    def twins(n):
        there = 2 * n + 1 - core
        return push(packed_hbm.at[there], twin.at[n], twin_send.at[n], twin_recv.at[n], sibling())

    def over_z(k):
        target = lax.rem(f + 2 * k, F)
        return push(pairs.at[target // 2], from_z.at[k - 1], z_send.at[k - 1], z_recv.at[k - 1], {"fsdp": target})

    fill = pltpu.make_async_copy(packed_hbm, packed, load)
    fill.start()
    own = pltpu.make_async_copy(gu_hbm.at[s], got.at[s], gu_own.at[0])
    own.start()
    back = pltpu.make_async_copy(got, got_hbm, gu_own.at[1])
    owner = hidden_owner(S, s, f)
    far_send = push(down_hbm, down_out, far.at[0], far.at[1], {"sp": owner})
    far_keep = pltpu.make_async_copy(down_hbm, down_out, far.at[0])
    greet(S, F, True)

    @pl.when(owner == s)
    def _():
        far_keep.start()

    for n in range(chips):
        twins(n).start()
    fill.wait()
    for n in range(chips):
        twins(n).wait_recv()
        pairs[n] = (packed[2 * n + core].astype(f32) + twin[n].astype(f32)).astype(bf16)
    for k in range(1, chips):
        over_z(k).start()

    def compute(chunk, out):
        rows = hid_ref[pl.ds(pl.multiple_of(chunk * T, T), T), :]
        for c in range(0, width, tile):
            out[:, c : c + tile] = dot(rows, wd_ref[:, c : c + tile]).astype(out.dtype)
    rows_d = qkv_ref.shape[0]
    rows_o = gout_ref.shape[0]
    qw = heads * HD
    QW, KW = QUERY_HEADS * HD, KV_HEADS * HD
    blocks = (qw + 2 * HD) // W
    n_s = blocks * rows_d
    n_q, n_o = S * n_s, rows_o * width // W

    def rows_of(j):
        return pl.ds(pl.multiple_of(j * n_s, n_s), n_s), pl.ds(pl.multiple_of(n_q + n_o + 16 * j, 16), 16)

    def end(k, slot, part):
        to = (slice(0, n_s), slice(n_s, n_s + 16))[part]
        n = 2 * (k - 1) + part
        src = mine.at[rows_of(lax.rem(s + k, S))[part]]
        return to_peer(src, mine_all.at[slot, to], end_sems.at[0, n], end_sems.at[1, n], k, S)

    def reduce_z():
        for k in range(1, S):
            exchange(k, s).start()

        @pl.when(owner != s)
        def _():
            far_send.start()

        total = pairs[f // 2].astype(f32)
        for k in range(1, chips):
            over_z(k).wait_recv()
            total += from_z[k - 1].astype(f32)
        mine[...] = total.astype(bf16)
        for k in range(1, S):
            for part in range(2):
                end(k, s, part).start()

    copies = sum_over_sp(S, compute, acc, send_buf, recv_buf, send, recv, reduce_z, across)
    out_ref[...] = (mid_ref[...] + acc[...]).astype(bf16)
    main, small = rows_of(s)
    mine_all[s, :n_s] = mine[main, :]
    mine_all[s, n_s:] = mine[small, :]
    for c in range(0, width // W, 2):
        rows = mine[n_q + c * rows_o : n_q + (c + 2) * rows_o, :].astype(f32)
        gout_ref[:, c * W : (c + 1) * W] = rows[:rows_o]
        gout_ref[:, (c + 1) * W : (c + 2) * W] = rows[rows_o:]
    for k in range(1, S):
        for part in range(2):
            end(k, lax.rem(s + S - k, S), part).wait_recv()
    shared = max(1, S // KV_HEADS)
    tiny = jnp.zeros((16, W), f32)
    kvs = []
    for j in range(S):
        for cb in range(blocks - 1):
            at = j * qw + cb * W
            qkv_ref[:, at : at + W] = mine_all[j, cb * rows_d : (cb + 1) * rows_d].astype(f32)
        kv = mine_all[j, (blocks - 1) * rows_d : blocks * rows_d].astype(f32)
        if j % shared:
            kvs[-1] = kvs[-1] + kv
        else:
            kvs.append(kv)
        tiny += mine_all[j, n_s : n_s + 16].astype(f32)
    for h in range(0, KV_HEADS, 2):
        at = QW + h * HD
        qkv_ref[:, at : at + W] = jnp.concatenate([kvs[h][:, :HD], kvs[h + 1][:, :HD]], axis=1)
        qkv_ref[:, at + KW : at + KW + W] = jnp.concatenate([kvs[h][:, HD:], kvs[h + 1][:, HD:]], axis=1)
    tiny_ref[...] = tiny
    own.wait()
    for k in range(1, S):
        exchange(k, lax.rem(s + S - k, S)).wait_recv()
    back.start()
    for k in range(1, S):
        exchange(k, s).wait_send()
    back.wait()
    for copy in copies:
        copy.wait_send()
    for n in range(chips):
        twins(n).wait_send()
    for k in range(1, chips):
        over_z(k).wait_send()
    for k in range(1, S):
        for part in range(2):
            end(k, s, part).wait_send()

    @pl.when(owner == s)
    def _():
        far_keep.wait()

    @pl.when(owner != s)
    def _():
        far_send.wait_send()
        far_send.wait_recv()


def sum_rows(S, F, hidden, w_dn, mid, grad_gu, down, packed, across, rows_d, rows_o, heads, collective):
    T, width = mid.shape
    n = max(6, S - 1)
    chips = F // 2
    part = packed.shape[1:]
    n_s = rows_d * (heads + 2) * HD // 128
    return pl.pallas_call(
        functools.partial(sum_kernel, S, F, heads, len(across)),
        in_specs=[VMEM] * 3 + [ANY] * 3 + [VMEM] * len(across),
        out_specs=[VMEM] * 4 + [ANY] * 2,
        out_shape=[
            shape((T, width)),
            shape((rows_d, (QUERY_HEADS + 2 * KV_HEADS) * HD), f32),
            shape((rows_o, width), f32),
            shape((16, 128), f32),
            shape(down.shape),
            shape(grad_gu.shape),
        ],
        scratch_shapes=[
            pltpu.VMEM(grad_gu.shape, bf16),
            DMA((S - 1,)),
            DMA((S - 1,)),
            DMA((2,)),
            pltpu.VMEM((T, width), f32),
            pltpu.VMEM((S - 1, T, width), bf16),
            pltpu.VMEM((S - 1, T, width), bf16),
            pltpu.VMEM(packed.shape, bf16),
            pltpu.VMEM((chips,) + part, bf16),
            pltpu.VMEM((chips,) + part, bf16),
            pltpu.VMEM((chips - 1,) + part, bf16),
            pltpu.VMEM(part, bf16),
            pltpu.VMEM((S, n_s + 16, 128), bf16),
            DMA((n,)),
            DMA((n,)),
            DMA((2,)),
            DMA,
            DMA((chips,)),
            DMA((chips,)),
            DMA((chips - 1,)),
            DMA((chips - 1,)),
            DMA((2, 2 * (S - 1))),
        ],
        compiler_params=params(collective),
        cost_estimate=cost(40),
    )(hidden, w_dn, mid, grad_gu, down, packed, *across)


def write_kernel(S, F, kept, *refs):
    ins, refs = refs[: kept + 2], refs[kept + 2 :]
    outs, refs = refs[: kept + 3], refs[kept + 3 :]
    stages, wide, sem_in, sem_out = refs[: kept + 2], refs[kept + 2 : kept + 5], refs[-2], refs[-1]
    loads = [pltpu.make_async_copy(ins[n], stages[n], sem_in.at[n]) for n in range(kept + 2)]
    for copy in loads[::-1]:
        copy.start()
    stores = []

    def store(n, src):
        stores.append(pltpu.make_async_copy(src, outs[n], sem_out.at[n]))
        stores[-1].start()

    loads[kept + 1].wait()
    got = stages[kept + 1]
    piece = got.shape[3] // F
    for n in range(2):
        for j in range(S):
            for m in range(F):
                at = (m * S + hidden_block(S, j, m // 2)) * piece
                wide[1 + n][:, at : at + piece] = got[j, n, :, m * piece : (m + 1) * piece].astype(f32)
        store(kept + 1 + n, wide[1 + n])
    loads[kept].wait()
    wide[0][...] = stages[kept][...].astype(f32)
    store(kept, wide[0])
    for n in range(kept):
        loads[n].wait()
        store(n, stages[n])
    for copy in stores:
        copy.wait()


def write_outputs(S, F, kept, down, got):
    _, _, rows_d, FFs = got.shape
    wide = [shape(down.shape, f32)] + [shape((rows_d, FFs * S), f32)] * 2
    if FFs // F % 128:
        parts = got.reshape(S, 2, rows_d, F, FFs // F)
        parts = [parts[(t - m // 2) % S, :, :, m] for m in range(F) for t in range(S)]
        grad = jnp.concatenate(parts, axis=2).astype(f32)
        return list(kept) + [down.astype(f32), grad[0], grad[1]]
    outs = [shape(a.shape, a.dtype) for a in kept] + wide
    ins = list(kept) + [down, got]
    return pl.pallas_call(
        functools.partial(write_kernel, S, F, len(kept)),
        in_specs=[ANY] * len(ins),
        out_specs=[ANY] * len(outs),
        out_shape=outs,
        scratch_shapes=[pltpu.VMEM(a.shape, a.dtype) for a in ins]
        + [pltpu.VMEM(a.shape, f32) for a in wide]
        + [DMA((len(ins),)), DMA((len(outs),))],
        compiler_params=params(),
        cost_estimate=cost(5),
    )(*ins)


def ordered(value, *after):
    return lax.optimization_barrier((value,) + after)[0]


def local(x_own, positions, ct_own, w_qkv, w_out, w_gate, w_up, w_down, gain_attn, gain_ffn, gain_query, gain_key):
    S, F = lax.axis_size("sp"), lax.axis_size("fsdp")
    assert F == 2 * S
    s, f = lax.axis_index("sp"), lax.axis_index("fsdp")
    _, T, D = x_own.shape
    L = positions.shape[1]
    heads = QUERY_HEADS // S
    qw = heads * HD
    hw = qw + 2 * HD
    FFs = w_gate.shape[1] // S
    rows_d = D // (S * F)
    rows_o = qw // F
    x_own = x_own[0]
    ct_own = ct_own[0]

    def gather_z(w):
        return lax.all_gather(w, "fsdp", axis=0, tiled=True)

    def reduce_z(w):
        return lax.psum_scatter(w, "fsdp", scatter_dimension=0, tiled=True)

    gu_part = own_columns(S, F, s, w_gate, w_up)
    w_gu = gather_z(gu_part).reshape(F, 2, D // F, FFs)
    rows_w = w_down.shape[0] // S

    x_all, ct_a, wqkv_s, gains, cosine, sine = first_gathers(
        S, F, x_own, ct_own, ordered(w_qkv, gu_part), gain_attn[None], gain_ffn[None], positions, heads, 0
    )
    w_down, gain_query, gain_key, _ = lax.optimization_barrier((w_down, gain_query, gain_key, x_all))
    w_dn = gather_z(lax.dynamic_slice_in_dim(w_down, hidden_block(S, s, f // 2) * rows_w, rows_w, 0))
    x_all = x_all.reshape(L, D)
    wqkv_s = wqkv_s.reshape(D, hw)
    gain_q = gain_query.astype(f32)[:, None]
    gain_k = gain_key.astype(f32)[:, None]
    normed_t, raw, rot, lse, mix_t, mix_all, wout_all, ct0 = forward_attention(
        S, F, x_all, gains, wqkv_s, positions, cosine, sine, gain_q, gain_k, w_out, ct_own, heads, 1
    )
    wout_all = wout_all.reshape(S, qw, D)
    cts = [ct_a.reshape(L, D // 4), ct0.reshape(L, D // 4)]
    mid, ffn_in, ffn_t, ct1 = middle_rows(S, x_all, mix_all, wout_all, gains, ct_own, 2)
    cts.append(ct1.reshape(L, D // 2))
    gate, up, hidden, part_down, wqkv0 = ffn_forward(S, ffn_in, cts, w_gu, wqkv_s, 3)
    grad_down = reduce_z(part_down.reshape(FFs, D))
    dgu, part_gu, wqkv1, *across = ffn_backward(S, F, cts, w_dn, gate, up, ffn_t, wqkv_s, hidden, 4)
    grad_gu = reduce_z(part_gu.reshape(2 * D, FFs))
    gm, d_attn, grad_gf, d_mix = middle_back(S, dgu, w_gu, wout_all, mid, gains, ct_own, 5)
    packed, grad_input = attention_back(
        S, F, ordered(d_mix, grad_down), rot, raw, lse, positions, cosine, sine, gain_q, gain_k,
        gains, grad_gf, mix_t, x_own, gm, normed_t, wqkv0, wqkv1, d_attn, heads, 6,
    )
    out, grad_qkv, grad_out, tiny, grad_down, got = sum_rows(
        S, F, hidden, w_dn, mid, grad_gu.reshape(S, 2, rows_d, FFs), grad_down, packed, across, rows_d, rows_o, heads, 7
    )
    grad_input, out, grad_qkv, grad_out, grad_down, grad_gate, grad_up = write_outputs(
        S, F, (grad_input, out, grad_qkv, grad_out), grad_down, got
    )
    return (
        out[None],
        grad_input[None],
        grad_qkv,
        grad_out,
        grad_gate,
        grad_up,
        grad_down,
        tiny[0, :rows_d],
        tiny[0, rows_d : 2 * rows_d],
        tiny[1, :HD],
        tiny[1, HD:],
    )


def solution(mesh):
    row = P("fsdp", "sp", None)
    shard = P("fsdp", None)
    grad = P(("sp", "fsdp"), None)
    return jax.shard_map(
        local,
        mesh=mesh,
        in_specs=(row, shard, row, shard, shard, shard, shard, shard, P("fsdp"), P("fsdp"), P(), P()),
        out_specs=(row, row, grad, grad, grad, grad, grad, P(("sp", "fsdp")), P(("sp", "fsdp")), P(), P()),
        check_vma=False,
    )
```

```python
import functools

import jax
import jax.numpy as jnp
import numpy as np
from jax import lax
from jax.experimental import pallas as pl
from jax.experimental.pallas import tpu as pltpu
from jax.sharding import PartitionSpec as P

QUERY_HEADS = 16
KV_HEADS = 4
HD = 64
EPS = 1e-06
BLOCK = 256
VMEM_LIMIT = 60 << 20
MESH = pl.DeviceIdType.MESH
f32 = jnp.float32
bf16 = jnp.bfloat16


def params(collective=None, grid=0):
    return pltpu.CompilerParams(
        dimension_semantics=("arbitrary",) * grid if grid else None,
        vmem_limit_bytes=VMEM_LIMIT,
        collective_id=collective,
        has_side_effects=collective is not None,
    )


def cost(micros):
    return pl.CostEstimate(flops=0, bytes_accessed=int(micros * 3_600_000), transcendentals=0)


ANY = pl.BlockSpec(memory_space=pl.ANY)
VMEM = pl.BlockSpec(memory_space=pltpu.VMEM)
DMA = pltpu.SemaphoreType.DMA


def shape(dims, dtype=bf16):
    return jax.ShapeDtypeStruct(dims, dtype)


def dot(a, b):
    return jnp.dot(a, b, preferred_element_type=f32)


def dot_nt(a, b):
    return lax.dot_general(a, b, (((1,), (1,)), ((), ())), preferred_element_type=f32)


def sibling():
    f = lax.axis_index("fsdp")
    return {"fsdp": f + 1 - 2 * lax.rem(f, 2)}


def greet(S, F=0, with_sibling=False):
    s, f = lax.axis_index("sp"), lax.axis_index("fsdp")
    where = [{"sp": lax.rem(s + k, S)} for k in range(1, S)]
    where += [{"fsdp": lax.rem(f + 2 * k, F)} for k in range(1, F // 2)]
    if with_sibling:
        where.append(sibling())
    barrier = pltpu.get_barrier_semaphore()
    for target in where:
        pl.semaphore_signal(barrier, inc=1, device_id=target, device_id_type=MESH)
    pl.semaphore_wait(barrier, len(where))


def gain_row(g_ref, n):
    return jnp.concatenate([g_ref[j].astype(f32)[n : n + 1] for j in range(g_ref.shape[0])], axis=1)


def to_peer(src, dst, send, recv, k, S):
    s = lax.axis_index("sp")
    return pltpu.make_async_remote_copy(
        src_ref=src, dst_ref=dst, send_sem=send, recv_sem=recv, device_id={"sp": lax.rem(s + k, S)}, device_id_type=MESH
    )


def mates(s):
    return s + 1 - 2 * lax.rem(s, 2), lax.rem(s + 2, 4), 3 - s


def xor(a, b):
    return (a + b) % 2 + 2 * ((a // 2 + b // 2) % 2)


def hidden_block(S, s, q):
    if S != 4:
        return (s + q) % S
    x = xor(s, q)
    return (x % 3 + 1) * ((x + 3) // 4)


def hidden_owner(S, s, f):
    i = f % S
    if S != 4:
        return (i - s + S) % S
    return xor(s, ((i + 1) % 3 + 1) * ((i + 3) // 4))


def push(src, dst, send, recv, where):
    return pltpu.make_async_remote_copy(
        src_ref=src, dst_ref=dst, send_sem=send, recv_sem=recv, device_id=where, device_id_type=MESH
    )


class Gather:
    def __init__(self, S, src, dst, sems, halves=False, inner=False, staged=True):
        self.S, self.src, self.halves = S, src, halves
        self.slot = (lambda j: dst.at[:, j]) if inner else (lambda j: dst.at[j])
        self.stage = sems[-1] if staged else None
        self.send, self.recv, self.own = sems[:3]
        self.swap_send, self.swap_recv = sems[3:5] if halves else (None, None)
        self.s, self.f = lax.axis_index("sp"), lax.axis_index("fsdp")
        self.rows = src.shape[0] // (2 if halves else 1)
        self.size = self.rows // 2 if S == 4 else self.rows

    @staticmethod
    def sems(S, chunk, halves=False):
        count = 6 if S == 4 else S - 1
        base = [DMA((count,)), DMA((count,)), DMA((2,))]
        base += [DMA((S - 1,)), DMA((S - 1,))] if halves else []
        return base if chunk is None else base + [pltpu.VMEM(chunk.shape, chunk.dtype)]

    def base(self, mine=True):
        if not self.halves:
            return 0
        core = lax.rem(self.f, 2)
        return (core if mine else 1 - core) * self.rows

    def piece(self, ref, n):
        return ref.at[pl.ds(self.base() + n * self.size, self.size)]

    def share(self, slot, mine):
        if not self.halves:
            return self.slot(slot)
        return self.slot(slot).at[pl.ds(self.base(mine), self.rows)]

    def steps(self):
        s, S = self.s, self.S
        if S != 4:
            return [(self.src, s, lax.rem(s + S - k, S), 0, lax.rem(s + k, S)) for k in range(1, S)]
        x, y, d = mates(s)
        return [
            (self.src, s, x, 0, x),
            (self.src, s, y, 1, y),
            (self.src, s, x, 1, x),
            (self.src, s, y, 0, y),
            (self.slot(x), x, d, 0, y),
            (self.slot(y), y, d, 1, x),
        ]

    def copy(self, n, here):
        src, there, lands, piece, target = self.steps()[n]
        slot = lands if here else there
        return push(
            self.piece(src, piece), self.piece(self.slot(slot), piece), self.send.at[n], self.recv.at[n], {"sp": target}
        )

    def passing(self, n, mine):
        slots = mates(self.s) if self.S == 4 else [lax.rem(self.s + self.S - k, self.S) for k in range(1, self.S)]
        return push(
            self.share(slots[n], True), self.share(slots[n], mine), self.swap_send.at[n], self.swap_recv.at[n], sibling()
        )

    def local(self, out):
        if self.stage is None:
            return pltpu.make_async_copy(self.src, self.slot(self.s), self.own.at[0])
        if out:
            return pltpu.make_async_copy(self.stage, self.slot(self.s), self.own.at[1])
        return pltpu.make_async_copy(self.src, self.stage, self.own.at[0])

    def start(self):
        for n in range(4 if self.S == 4 else self.S - 1):
            self.copy(n, False).start()
        self.local(False).start()

    def relay(self):
        if self.stage is not None:
            self.local(False).wait()
            self.local(True).start()
        if self.S == 4:
            for n in range(2):
                self.copy(n, True).wait_recv()
                self.copy(4 + n, False).start()

    def spread(self):
        if self.S == 4:
            for n in range(2):
                self.copy(2 + n, True).wait_recv()
                if self.halves:
                    self.passing(n, True).start()

    def finish(self, relayed=False, spread=False):
        if not relayed:
            self.relay()
        if not spread:
            self.spread()
        ready = {5: 2} if self.S == 4 else {n: n for n in range(self.S - 1)}
        for n in range(4 if self.S == 4 else 0, len(self.steps())):
            self.copy(n, True).wait_recv()
            if self.halves and n in ready:
                self.passing(ready[n], True).start()
        self.local(True).wait()
        for n in range(len(self.steps())):
            self.copy(n, False).wait_send()
        if self.halves:
            for n in range(self.S - 1):
                self.passing(n, True).wait_send()
                self.passing(n, False).wait_recv()


class GatherZ:
    def __init__(self, F, src, dst, sems):
        self.F, self.src, self.dst = F, src, dst
        self.send, self.recv, self.pass_send, self.pass_recv, self.own = sems
        self.f = lax.axis_index("fsdp")

    @staticmethod
    def sems(F):
        return [DMA((F // 2 - 1,)), DMA((F // 2 - 1,)), DMA((F // 2,)), DMA((F // 2,)), DMA]

    def sending(self, k):
        return push(
            self.src, self.dst.at[self.f], self.send.at[k - 1], self.recv.at[k - 1], {"fsdp": lax.rem(self.f + 2 * k, self.F)}
        )

    def landing(self, k):
        slot = lax.rem(self.f + self.F - 2 * k, self.F)
        return push(
            self.src, self.dst.at[slot], self.send.at[k - 1], self.recv.at[k - 1], {"fsdp": lax.rem(self.f + 2 * k, self.F)}
        )

    def passing(self, k, mine):
        f, F = self.f, self.F
        slot = lax.rem(f + F - 2 * k, F)
        other = f + 1 - 2 * lax.rem(f, 2)
        there = slot if mine else lax.rem(other + F - 2 * k, F)
        src = self.src if k == 0 else self.dst.at[slot]
        return push(src, self.dst.at[there], self.pass_send.at[k], self.pass_recv.at[k], sibling())

    def local(self):
        return pltpu.make_async_copy(self.src, self.dst.at[self.f], self.own)

    def start(self):
        for k in range(1, self.F // 2):
            self.sending(k).start()
        self.passing(0, True).start()
        self.local().start()

    def finish(self):
        for k in range(1, self.F // 2):
            self.landing(k).wait_recv()
            self.passing(k, True).start()
        self.local().wait()
        for k in range(1, self.F // 2):
            self.sending(k).wait_send()
        for k in range(self.F // 2):
            self.passing(k, True).wait_send()
            self.passing(k, False).wait_recv()


def first_kernel(S, F, heads, x_ref, ct_ref, wqkv_ref, ga_ref, gf_ref, pos_ref, freq_ref, x_all, ct_all, wqkv_all, gains_all, cos_ref, sin_ref, part, gains, *sems):
    s = lax.axis_index("sp")
    qw = heads * HD
    QW, KW = QUERY_HEADS * HD, KV_HEADS * HD
    kv = s // max(1, S // KV_HEADS)
    pair = kv // 2
    high = lax.rem(kv, 2)

    def cut(start):
        block = wqkv_ref[:, pl.ds(pl.multiple_of(start + pair * 128, 128), 128)].astype(f32)
        return jnp.where(high == 1, block[:, HD:], block[:, :HD])

    part[:, :qw] = wqkv_ref[:, pl.ds(pl.multiple_of(s * qw, 128), qw)]
    part[:, qw:] = jnp.concatenate([cut(QW), cut(QW + KW)], axis=1).astype(bf16)
    pad = jnp.zeros((14, ga_ref.shape[1]), f32)
    gains[...] = jnp.concatenate([ga_ref[...].astype(f32), gf_ref[...].astype(f32), pad], axis=0).astype(bf16)
    n = len(Gather.sems(S, shape((1, 1))))
    m = len(GatherZ.sems(F))
    move_x = Gather(S, x_ref, x_all, sems[:n])
    move_ct = Gather(S, ct_ref.at[:, pl.ds(0, ct_all.shape[2])], ct_all, sems[n : 2 * n])
    moves_z = [
        GatherZ(F, part, wqkv_all, sems[2 * n : 2 * n + m]),
        GatherZ(F, gains, gains_all, sems[2 * n + m :]),
    ]
    greet(S, F, True)
    move_x.start()
    for move in moves_z:
        move.start()
    angles = freq_ref[...] * pos_ref[...].astype(f32)
    cos_ref[...] = jnp.cos(angles)
    sin_ref[...] = jnp.sin(angles)
    move_x.relay()
    move_ct.start()
    move_x.finish(True)
    move_ct.relay()
    for move in moves_z:
        move.finish()
    move_ct.finish(True)


def first_gathers(S, F, x, ct, w_qkv, gain_attn, gain_ffn, positions, heads, collective):
    T, width = x.shape
    depth = w_qkv.shape[0]
    hw = (heads + 2) * HD
    length = positions.shape[1]
    frequency = jnp.asarray(10000.0 ** (-2.0 * np.arange(HD // 2) / HD), f32)[:, None]
    table = shape((HD // 2, length), f32)
    return pl.pallas_call(
        functools.partial(first_kernel, S, F, heads),
        in_specs=[ANY] * 2 + [VMEM] * 5,
        out_specs=[ANY] * 4 + [VMEM] * 2,
        out_shape=[
            shape((S, T, width)),
            shape((S, T, width // 4)),
            shape((F, depth, hw)),
            shape((F, 16, depth)),
            table,
            table,
        ],
        scratch_shapes=[pltpu.VMEM((depth, hw), bf16), pltpu.VMEM((16, depth), bf16)]
        + Gather.sems(S, x)
        + Gather.sems(S, shape((T, width // 4)))
        + GatherZ.sems(F) * 2,
        compiler_params=params(collective),
        cost_estimate=cost(45),
    )(x, ct, w_qkv, gain_attn, gain_ffn, positions, frequency)


def columns_kernel(S, F, gate_hbm, up_hbm, out_hbm, buf, sem_in, sem_out):
    s = lax.axis_index("sp")
    piece = buf.shape[2] // F
    ins = []
    for n, ref in enumerate((gate_hbm, up_hbm)):
        for m in range(F):
            src = ref.at[:, pl.ds(pl.multiple_of((m * S + hidden_block(S, s, m // 2)) * piece, piece), piece)]
            ins.append(pltpu.make_async_copy(src, buf.at[n, :, pl.ds(m * piece, piece)], sem_in.at[n * F + m]))
    for copy in ins:
        copy.start()
    outs = []
    for n in range(2):
        for copy in ins[n * F : (n + 1) * F]:
            copy.wait()
        outs.append(pltpu.make_async_copy(buf.at[n], out_hbm.at[n], sem_out.at[n]))
        outs[-1].start()
    for copy in outs:
        copy.wait()


def own_columns(S, F, s, w_gate, w_up):
    depth, FF = w_gate.shape
    piece = FF // (S * F)
    if piece % 128:
        def pick(w):
            starts = [(m * S + hidden_block(S, s, m // 2)) * piece for m in range(F)]
            return jnp.concatenate([lax.dynamic_slice_in_dim(w, at, piece, 1) for at in starts], axis=1)

        return jnp.stack([pick(w_gate), pick(w_up)])
    return pl.pallas_call(
        functools.partial(columns_kernel, S, F),
        in_specs=[ANY, ANY],
        out_specs=ANY,
        out_shape=shape((2, depth, FF // S)),
        scratch_shapes=[pltpu.VMEM((2, depth, FF // S), bf16), DMA((2 * F,)), DMA((2,))],
        compiler_params=params(),
        cost_estimate=cost(3),
    )(w_gate, w_up)


def forward_kernel(S, F, heads, x_ref, g_ref, w_ref, pos_ref, cos_ref, sin_ref, gq_ref, gk_ref, wout_ref, ct_ref, normed_t_ref, raw_ref, rot_ref, lse_ref, mix_t_ref, mix_all, wout_all, ct_all, k_buf, vt_buf, mix_buf, mix_send, mix_recv, mix_own, wout_s, *sems):
    i = pl.program_id(0)
    s = lax.axis_index("sp")
    qw = heads * HD
    half = HD // 2
    blocks = pl.num_programs(0)
    n_z = len(GatherZ.sems(F))
    rows_o = wout_s.shape[1]
    own_out = wout_ref.at[pl.ds(pl.multiple_of(s * rows_o, rows_o), rows_o)]
    move_z = GatherZ(F, own_out, wout_s, sems[:n_z])
    n_w = n_z + len(Gather.sems(S, None, True))
    move = Gather(S, wout_s, wout_all, sems[n_z:n_w], halves=True, inner=True, staged=False)
    move_ct = Gather(S, ct_ref.at[:, pl.ds(ct_all.shape[2], ct_all.shape[2])], ct_all, sems[n_w:])

    @pl.when(i == 0)
    def _():
        greet(S, F, True)
        move_z.start()
        move_ct.start()

    @pl.when(i == blocks - 1)
    def _():
        move_ct.relay()

    x = x_ref[...].astype(f32)
    scale = lax.rsqrt(jnp.mean(x * x, axis=-1, keepdims=True) + EPS)
    scaled = x * scale * gain_row(g_ref, 0)
    normed = scaled.astype(bf16)
    normed_t_ref[...] = scaled.T.astype(bf16)
    raw = dot(normed, w_ref[...]).T
    raw_ref[...] = raw
    cosine, sine = cos_ref[...], sin_ref[...]

    def prep(u, gain):
        n = u * lax.rsqrt(jnp.mean(u * u, axis=0, keepdims=True) + EPS) * gain
        front, back = n[:half], n[half:]
        return jnp.concatenate([front * cosine - back * sine, back * cosine + front * sine], axis=0)

    q = [prep(raw[h * HD : (h + 1) * HD], gq_ref[...]).astype(bf16) for h in range(heads)]
    kt = prep(raw[qw : qw + HD], gk_ref[...])
    vt = raw[qw + HD :].astype(bf16)
    rot_ref[...] = jnp.concatenate(q + [kt.astype(bf16), vt], axis=0)
    steps = mix_buf.shape[0]

    x_mate, y_mate, d_mate = mates(s)

    def mix_copy(block, k, here):
        rows = pl.ds(block * BLOCK, BLOCK)
        n = block * (S - 1) + k - 1
        if S != 4:
            slot = lax.rem(s + S - k, S) if here else s
            return push(mix_buf.at[block], mix_all.at[slot, rows], mix_send.at[n], mix_recv.at[n], {"sp": lax.rem(s + k, S)})
        if k < 3:
            mate = x_mate if k == 1 else y_mate
            slot = mate if here else s
            return push(mix_buf.at[block], mix_all.at[slot, rows], mix_send.at[n], mix_recv.at[n], {"sp": mate})
        source, mate = (x_mate, y_mate) if block < steps // 2 else (y_mate, x_mate)
        slot = d_mate if here else source
        return push(mix_all.at[source, rows], mix_all.at[slot, rows], mix_send.at[n], mix_recv.at[n], {"sp": mate})

    def mix_local(block):
        return pltpu.make_async_copy(mix_buf.at[block], mix_all.at[s, pl.ds(block * BLOCK, BLOCK)], mix_own.at[block])

    for step in range(steps):

        @pl.when(i == step)
        def _():
            n = (step + 1) * BLOCK
            k_buf[step * BLOCK : n, :] = kt.T.astype(bf16)
            vt_buf[:, step * BLOCK : n] = vt
            col = lax.broadcasted_iota(jnp.int32, (n, BLOCK), 0)
            row = step * BLOCK + lax.broadcasted_iota(jnp.int32, (n, BLOCK), 1)
            bias = jnp.where((col <= row) & (row - col <= pos_ref[...]), 0.0, -1e30)
            keys, values = k_buf[:n, :], vt_buf[:, :n]
            mixes, lses = [], []
            for h in range(heads):
                e = jnp.exp(dot(keys, q[h] * 0.125) + bias)
                total = jnp.sum(e, axis=0, keepdims=True)
                p = (e * (1.0 / total)).astype(bf16)
                mixes.append(dot(values, p))
                lses.append(jnp.log(total))
            mix = jnp.concatenate(mixes, axis=0)
            mix_t_ref[...] = mix.astype(bf16)
            lse_ref[...] = jnp.concatenate(lses + [jnp.zeros((8 - heads, BLOCK), f32)], axis=0)
            mix_buf[step] = mix.T.astype(bf16)
            for k in range(1, 3 if S == 4 else S):
                mix_copy(step, k, False).start()
            mix_local(step).start()

    @pl.when(i == blocks - 1)
    def _():
        move_z.finish()
        move.start()
        for block in range(steps):
            for k in range(1, 3 if S == 4 else S):
                mix_copy(block, k, True).wait_recv()
                if S == 4 and k == (1 if block < steps // 2 else 2):
                    mix_copy(block, 3, False).start()
        move.relay()
        for block in range(steps):
            if S == 4:
                mix_copy(block, 3, True).wait_recv()
            for k in range(1, S):
                mix_copy(block, k, False).wait_send()
            mix_local(block).wait()
        move.finish(True)
        move_ct.finish(True)


def forward_attention(S, F, x, gain, w, pos, cosine, sine, gain_q, gain_k, wout, ct, heads, collective):
    length, width = x.shape
    hw = w.shape[1]
    qw = heads * HD
    steps = length // BLOCK
    full = lambda i: (0, 0)
    rows = lambda i: (i, 0)
    cols = lambda i: (0, i)
    return pl.pallas_call(
        functools.partial(forward_kernel, S, F, heads),
        grid=(steps,),
        in_specs=[
            pl.BlockSpec((BLOCK, width), rows),
            pl.BlockSpec(gain.shape, lambda i: (0, 0, 0)),
            pl.BlockSpec((width, hw), full),
            pl.BlockSpec((1, BLOCK), cols),
            pl.BlockSpec((HD // 2, BLOCK), cols),
            pl.BlockSpec((HD // 2, BLOCK), cols),
            pl.BlockSpec((HD, 1), full),
            pl.BlockSpec((HD, 1), full),
            pl.BlockSpec(wout.shape, full),
            ANY,
        ],
        out_specs=[
            pl.BlockSpec((width, BLOCK), cols),
            pl.BlockSpec((hw, BLOCK), cols),
            pl.BlockSpec((hw, BLOCK), cols),
            pl.BlockSpec((8, BLOCK), cols),
            pl.BlockSpec((qw, BLOCK), cols),
            ANY,
            ANY,
            ANY,
        ],
        out_shape=[
            shape((width, length)),
            shape((hw, length), f32),
            shape((hw, length)),
            shape((8, length), f32),
            shape((qw, length)),
            shape((S, length, qw)),
            shape((F, S, wout.shape[0] // S, width)),
            shape((S,) + ct.shape[:1] + (width // 4,)),
        ],
        scratch_shapes=[
            pltpu.VMEM((length, HD), bf16),
            pltpu.VMEM((HD, length), bf16),
            pltpu.VMEM((steps, BLOCK, qw), bf16),
            DMA((steps * (S - 1),)),
            DMA((steps * (S - 1),)),
            DMA((steps,)),
            pltpu.VMEM((F, wout.shape[0] // S, width), bf16),
        ]
        + GatherZ.sems(F)
        + Gather.sems(S, None, True)
        + Gather.sems(S, shape((ct.shape[0], width // 4))),
        compiler_params=params(collective, 1),
        cost_estimate=cost(45),
    )(x, gain, w, pos, cosine, sine, gain_q, gain_k, wout, ct)


def middle_kernel(S, T, x_ref, mix_ref, wout_ref, g_ref, ct_ref, mid_ref, ffn_ref, ffn_t_ref, ct_all, *sems):
    i = pl.program_id(0)
    s = lax.axis_index("sp")
    move = Gather(S, ct_ref.at[:, pl.ds(ct_all.shape[2], ct_all.shape[2])], ct_all, sems)

    @pl.when(i == 0)
    def _():
        greet(S)
        move.start()

    @pl.when(i == pl.num_programs(0) - 2)
    def _():
        move.relay()

    middle = x_ref[...].astype(f32)
    total = dot(mix_ref[0], wout_ref[0])
    for j in range(1, S):
        total += dot(mix_ref[j], wout_ref[j])
    middle = middle + total

    @pl.when(i == s)
    def _():
        mid_ref[...] = middle

    scaled = middle * lax.rsqrt(jnp.mean(middle * middle, axis=-1, keepdims=True) + EPS) * gain_row(g_ref, 1)
    ffn_ref[...] = scaled.astype(bf16)
    ffn_t_ref[...] = scaled.T.astype(bf16)

    @pl.when(i == pl.num_programs(0) - 1)
    def _():
        move.finish(True)


def middle_rows(S, x, mix_all, wout_all, gain, ct, collective):
    length, width = x.shape
    T = length // S
    qw = mix_all.shape[2]
    return pl.pallas_call(
        functools.partial(middle_kernel, S, T),
        grid=(S,),
        in_specs=[
            pl.BlockSpec((T, width), lambda i: (i, 0)),
            pl.BlockSpec((S, T, qw), lambda i: (0, i, 0)),
            pl.BlockSpec((S, qw, width), lambda i: (0, 0, 0)),
            pl.BlockSpec(gain.shape, lambda i: (0, 0, 0)),
            ANY,
        ],
        out_specs=[
            pl.BlockSpec((T, width), lambda i: (0, 0)),
            pl.BlockSpec((T, width), lambda i: (i, 0)),
            pl.BlockSpec((width, T), lambda i: (0, i)),
            ANY,
        ],
        out_shape=[shape((T, width), f32), shape((length, width)), shape((width, length)), shape((S, T, width // 2))],
        scratch_shapes=Gather.sems(S, shape((T, width // 2))),
        compiler_params=params(collective, 1),
        cost_estimate=cost(45),
    )(x, mix_all, wout_all, gain, ct)


def ffn_kernel(S, F, ffn_ref, cta_ref, ctb_ref, ctc_ref, wg_ref, wu_ref, wqkv_hbm, gate_ref, up_ref, hid_ref, down_ref, wqkv_all, *sems):
    i = pl.program_id(0)
    last = pl.num_programs(0) - 1
    s = lax.axis_index("sp")
    move = Gather(S, wqkv_hbm.at[pl.ds(0, wqkv_all.shape[1])], wqkv_all, sems, halves=True)

    @pl.when(i == 0)
    def _():
        greet(S, 0, True)
        move.start()

    @pl.when(i == last - 1)
    def _():
        move.relay()

    @pl.when(i == last)
    def _():
        move.spread()

    length, width = ffn_ref.shape
    rows = ffn_ref[...]
    gate, up = dot(rows, wg_ref[...].reshape(width, BLOCK)), dot(rows, wu_ref[...].reshape(width, BLOCK))
    gate_ref[...] = gate
    up_ref[...] = up
    hidden = gate / (1.0 + jnp.exp(-gate)) * up
    hid_ref[...] = hidden.astype(bf16)
    flipped = hidden.T.astype(bf16)
    piece = down_ref.shape[1]
    at = 0
    for ref in (cta_ref, ctb_ref, ctc_ref):
        cut = slice(at, at + ref.shape[1])
        at += ref.shape[1]
        part = dot(flipped, ref[...]).astype(bf16)
        for m in range(BLOCK // piece):
            block = i * (BLOCK // piece) + m
            owner = lax.rem(block, 2) * S + hidden_block(S, s, block // 2)
            down_ref[owner, :, cut] = part[m * piece : (m + 1) * piece]

    @pl.when(i == last)
    def _():
        move.finish(True, True)


def ffn_forward(S, ffn_in, cts, w_gu, wqkv_s, collective):
    length, width = ffn_in.shape
    F, _, depth, FFs = w_gu.shape
    whole = lambda i: (0, 0)
    col = pl.BlockSpec((length, BLOCK), lambda i: (0, i))
    return pl.pallas_call(
        functools.partial(ffn_kernel, S, F),
        grid=(FFs // BLOCK,),
        in_specs=[
            pl.BlockSpec((length, width), whole),
            *[pl.BlockSpec(ct.shape, whole) for ct in cts],
            pl.BlockSpec((F, 1, depth, BLOCK), lambda i: (0, 0, 0, i)),
            pl.BlockSpec((F, 1, depth, BLOCK), lambda i: (0, 1, 0, i)),
            ANY,
        ],
        out_specs=[col, col, col, pl.BlockSpec((F, FFs // F, width), lambda i: (0, 0, 0)), ANY],
        out_shape=[
            shape((length, FFs), f32),
            shape((length, FFs), f32),
            shape((length, FFs)),
            shape((F, FFs // F, width)),
            shape((S, width // 2, wqkv_s.shape[1])),
        ],
        scratch_shapes=Gather.sems(S, shape((width // 2, wqkv_s.shape[1])), True),
        compiler_params=params(collective, 1),
        cost_estimate=cost(20),
    )(ffn_in, *cts, w_gu, w_gu, wqkv_s)


def ffn_back_kernel(S, F, cta_ref, ctb_ref, ctc_ref, wd_ref, gate_ref, up_ref, ffn_t_ref, wqkv_ref, hid_hbm, wd_hbm, dgu_ref, pgu_ref, wqkv_all, *refs):
    i = pl.program_id(0)
    last = pl.num_programs(0) - 1
    s = lax.axis_index("sp")
    split = S == 4
    if split:
        across, hid, wd, send_buf, send, recv, load = refs[:7]
        x_mate, y_mate, d_mate = mates(s)
        T = send_buf.shape[0]
        loads = [
            pltpu.make_async_copy(hid_hbm.at[pl.ds(pl.multiple_of(d_mate * T, T), T)], hid, load.at[0]),
            pltpu.make_async_copy(wd_hbm, wd, load.at[1]),
        ]
        low, high = pl.ds(0, T // 2), pl.ds(T // 2, T // 2)
        ahead = [
            push(send_buf.at[low], across.at[low], send.at[0], recv.at[0], {"sp": y_mate}),
            push(send_buf.at[high], across.at[high], send.at[1], recv.at[1], {"sp": x_mate}),
        ]
    depth = wqkv_all.shape[1]
    move = Gather(S, wqkv_ref.at[pl.ds(depth, depth)], wqkv_all, refs[7 if split else 0 :], halves=True)

    @pl.when(i == 0)
    def _():
        greet(S, 0, True)
        move.start()
        if split:
            for copy in loads:
                copy.start()

    @pl.when(i == last - 1)
    def _():
        move.relay()

    @pl.when(i == last)
    def _():
        move.spread()

    cot = jnp.concatenate([cta_ref[...], ctb_ref[...], ctc_ref[...]], axis=1)
    gh = dot_nt(cot, wd_ref[...])
    gate, up = gate_ref[...], up_ref[...]
    sig = 1.0 / (1.0 + jnp.exp(-gate))
    d_gate = (gh * up * sig * (1.0 + gate * (1.0 - sig))).astype(bf16)
    d_up = (gh * (gate * sig)).astype(bf16)
    dgu_ref[0] = d_gate
    dgu_ref[1] = d_up
    ffn_t = ffn_t_ref[...]
    rows = pgu_ref.shape[3]
    for n, d in enumerate((d_gate, d_up)):
        part = dot(ffn_t, d).astype(bf16)
        for j in range(S):
            for m in range(F):
                pgu_ref[m, j, n] = part[(j * F + m) * rows : (j * F + m + 1) * rows]

    if split:

        @pl.when(i == 0)
        def _():
            for copy in loads:
                copy.wait()
            for c in range(0, wd.shape[1], 512):
                send_buf[:, c : c + 512] = dot(hid[...], wd[:, c : c + 512]).astype(bf16)
            for copy in ahead:
                copy.start()

    @pl.when(i == last)
    def _():
        move.finish(True, True)
        if split:
            for copy in ahead:
                copy.wait_recv()
                copy.wait_send()


def ffn_backward(S, F, cts, w_dn, gate, up, ffn_t, wqkv_s, hidden, collective):
    length, FFs = gate.shape
    width = w_dn.shape[1]
    tiles = FFs // BLOCK
    rows = width // (S * F)
    whole = lambda i: (0, 0)
    col = lambda i: (0, i)
    T = length // S
    if S == 4:
        extra = [shape((T, width))]
        scratch = [pltpu.VMEM((T, FFs), bf16), pltpu.VMEM((FFs, width), bf16), pltpu.VMEM((T, width), bf16)]
        scratch += [DMA((2,)), DMA((2,)), DMA((2,))]
    else:
        extra, scratch = [], []
    return pl.pallas_call(
        functools.partial(ffn_back_kernel, S, F),
        grid=(tiles,),
        in_specs=[
            *[pl.BlockSpec(ct.shape, whole) for ct in cts],
            pl.BlockSpec((BLOCK, width), lambda i: (i, 0)),
            pl.BlockSpec((length, BLOCK), col),
            pl.BlockSpec((length, BLOCK), col),
            pl.BlockSpec((width, length), whole),
            ANY,
            ANY,
            ANY,
        ],
        out_specs=[
            pl.BlockSpec((2, length, BLOCK), lambda i: (0, 0, i)),
            pl.BlockSpec((F, S, 2, rows, BLOCK), lambda i: (0, 0, 0, 0, i)),
            ANY,
        ]
        + [ANY] * len(extra),
        out_shape=[shape((2, length, FFs)), shape((F, S, 2, rows, FFs)), shape((S, width // 2, wqkv_s.shape[1]))] + extra,
        scratch_shapes=scratch + Gather.sems(S, shape((width // 2, wqkv_s.shape[1])), True),
        compiler_params=params(collective, 1),
        cost_estimate=cost(1),
    )(*cts, w_dn, gate, up, ffn_t, wqkv_s, hidden, w_dn)


def sum_over_sp(S, compute, acc, send_buf, recv_buf, send, recv, between=None, across=None):
    s = lax.axis_index("sp")
    if S != 4:

        def copy(k):
            return push(
                send_buf.at[k - 1], recv_buf.at[k - 1], send.at[k - 1], recv.at[k - 1], {"sp": lax.rem(s + k, S)}
            )

        for k in range(1, S):
            compute(lax.rem(s + k, S), send_buf.at[k - 1])
            copy(k).start()
        compute(s, acc)
        if between is not None:
            between()
        for k in range(1, S):
            copy(k).wait_recv()
            acc[...] += recv_buf[k - 1].astype(f32)
        return [copy(k) for k in range(1, S)]

    x, y, d = mates(s)
    half = acc.shape[0] // 2
    low, high = pl.ds(0, half), pl.ds(half, half)
    if across is not None:

        def whole(n):
            return push(send_buf.at[n], recv_buf.at[n], send.at[n], recv.at[n], {"sp": x if n == 0 else y})

        compute(x, acc)
        send_buf[0, half:] = acc[half:].astype(bf16)
        send_buf[0, :half] = (acc[:half] + across[:half].astype(f32)).astype(bf16)
        whole(0).start()
        compute(y, acc)
        send_buf[1, :half] = acc[:half].astype(bf16)
        send_buf[1, half:] = (acc[half:] + across[half:].astype(f32)).astype(bf16)
        whole(1).start()
        compute(s, acc)
        if between is not None:
            between()
        for n in range(2):
            whole(n).wait_recv()
        acc[...] += recv_buf[0].astype(f32) + recv_buf[1].astype(f32)
        return [whole(n) for n in range(2)]

    def copy(n):
        buf, rows, target = [(0, low, y), (0, high, x), (1, high, x), (2, low, y), (1, low, x), (2, high, y)][n]
        return push(send_buf.at[buf, rows], recv_buf.at[buf, rows], send.at[n], recv.at[n], {"sp": target})

    compute(d, send_buf.at[0])
    copy(0).start()
    copy(1).start()
    compute(x, send_buf.at[1])
    copy(2).start()
    compute(y, send_buf.at[2])
    copy(3).start()
    copy(0).wait_recv()
    send_buf[1, :half] = (send_buf[1, :half].astype(f32) + recv_buf[0, :half].astype(f32)).astype(bf16)
    copy(4).start()
    copy(1).wait_recv()
    send_buf[2, half:] = (send_buf[2, half:].astype(f32) + recv_buf[0, half:].astype(f32)).astype(bf16)
    copy(5).start()
    compute(s, acc)
    if between is not None:
        between()
    for n in range(2, 6):
        copy(n).wait_recv()
    acc[...] += recv_buf[1].astype(f32) + recv_buf[2].astype(f32)
    return [copy(n) for n in range(6)]


def middle_back_kernel(S, F, dgu_hbm, wgu_hbm, wout_hbm, mid_hbm, ct_hbm, g_ref, gm_ref, dattn_ref, gg_ref, dmix_ref, dgu, wgu, wout, mid, ct, acc, send_buf, recv_buf, send, recv, load):
    s = lax.axis_index("sp")
    T, width = mid.shape
    depth = wgu.shape[2]
    greet(S)
    if S == 4:
        x, y, d = mates(s)
        order = [d, x, y, s]
    else:
        order = [lax.rem(s + k, S) for k in range(1, S)] + [s]

    def chunk_load(n):
        rows = pl.ds(pl.multiple_of(order[n] * T, T), T)
        return pltpu.make_async_copy(dgu_hbm.at[:, rows], dgu.at[n], load.at[n])

    def weight_load(c):
        return pltpu.make_async_copy(wgu_hbm.at[c], wgu.at[c], load.at[S + c])

    others = [
        pltpu.make_async_copy(mid_hbm, mid, load.at[S + F]),
        pltpu.make_async_copy(ct_hbm, ct, load.at[S + F + 1]),
        pltpu.make_async_copy(wout_hbm, wout, load.at[S + F + 2]),
    ]
    chunk_load(0).start()
    for c in range(F):
        weight_load(c).start()
    for n in range(1, S):
        chunk_load(n).start()
    for copy in others:
        copy.start()
    calls = []

    def compute(chunk, out):
        n = len(calls)
        calls.append(n)
        chunk_load(n).wait()
        for c in range(F):
            if n == 0:
                weight_load(c).wait()
            part = dot_nt(dgu[n, 0], wgu[c, 0]) + dot_nt(dgu[n, 1], wgu[c, 1])
            out[:, c * depth : (c + 1) * depth] = part.astype(out.dtype)

    copies = sum_over_sp(S, compute, acc, send_buf, recv_buf, send, recv)
    for copy in others:
        copy.wait()
    v, e = mid[...], acc[...]
    r = lax.rsqrt(jnp.mean(v * v, axis=-1, keepdims=True) + EPS)
    gg_ref[...] = jnp.sum(e * v * r, axis=0, keepdims=True)
    ge = gain_row(g_ref, 1) * e
    gm = ct[...].astype(f32) + r * ge - v * (r * r * r * jnp.mean(ge * v, axis=-1, keepdims=True))
    gm_ref[...] = gm
    d_attn = gm.astype(bf16)
    dattn_ref[...] = d_attn

    for j in range(S):
        dmix_ref[j] = dot_nt(d_attn, wout[j]).astype(bf16)
    for copy in copies:
        copy.wait_send()


def middle_back(S, dgu, w_gu, wout_all, mid, gain, ct, collective):
    T, width = mid.shape
    F = w_gu.shape[0]
    FFs = dgu.shape[2]
    qw = wout_all.shape[1]
    n = max(6, S - 1)
    return pl.pallas_call(
        functools.partial(middle_back_kernel, S, F),
        in_specs=[ANY] * 5 + [VMEM],
        out_specs=[VMEM] * 4,
        out_shape=[shape((T, width), f32), shape((T, width)), shape((1, width), f32), shape((S, T, qw))],
        scratch_shapes=[
            pltpu.VMEM((S, 2, T, FFs), bf16),
            pltpu.VMEM(w_gu.shape, bf16),
            pltpu.VMEM(wout_all.shape, bf16),
            pltpu.VMEM((T, width), f32),
            pltpu.VMEM((T, width), bf16),
            pltpu.VMEM((T, width), f32),
            pltpu.VMEM((S - 1, T, width), bf16),
            pltpu.VMEM((S - 1, T, width), bf16),
            DMA((n,)),
            DMA((n,)),
            DMA((S + F + 3,)),
        ],
        compiler_params=params(collective),
        cost_estimate=cost(1),
    )(dgu, w_gu, wout_all, mid, ct, gain)


def attn_back_kernel(S, F, heads, rot_ref, raw_ref, lse_ref, pos_ref, cos_ref, sin_ref, gq_ref, gk_ref, g_ref, ggf_ref, mix_t_ref, x_hbm, gm_hbm, normed_hbm, wqkv0_hbm, wqkv1_hbm, dattn_hbm, dmix_hbm, packed_ref, gin_ref, k_buf, v_buf, dk_acc, dv_acc, gg, dproj, dattn_all, got, x, gm, normed_t, wqkv, dmix_all, send, recv, load, mix_send, mix_recv, *sems):
    i = pl.program_id(0)
    s = lax.axis_index("sp")
    qw = heads * HD
    hw = qw + 2 * HD
    half = HD // 2
    length = rot_ref.shape[1]
    T, width = gin_ref.shape
    move = Gather(S, dattn_hbm, dattn_all, sems)
    loads = [
        pltpu.make_async_copy(a, b, load.at[n])
        for n, (a, b) in enumerate(
            [
                (normed_hbm, normed_t),
                (wqkv0_hbm, wqkv.at[:, pl.ds(0, width // 2)]),
                (wqkv1_hbm, wqkv.at[:, pl.ds(width // 2, width // 2)]),
                (x_hbm, x),
                (gm_hbm, gm),
            ]
        )
    ]

    def mix_copy(k, slot):
        return to_peer(dmix_hbm.at[lax.rem(s + k, S)], dmix_all.at[slot], mix_send.at[k - 1], mix_recv.at[k - 1], k, S)

    mix_own = pltpu.make_async_copy(dmix_hbm.at[s], dmix_all.at[s], load.at[5])

    @pl.when(i == 0)
    def _():
        greet(S)
        for k in range(1, S):
            mix_copy(k, s).start()
        mix_own.start()
        move.start()
        for copy in loads:
            copy.start()
        k_buf[...] = rot_ref[qw : qw + HD, :].astype(f32).T.astype(bf16)
        v_buf[...] = rot_ref[qw + HD :, :].astype(f32).T.astype(bf16)
        dk_acc[...] = jnp.zeros_like(dk_acc)
        dv_acc[...] = jnp.zeros_like(dv_acc)
        gg[...] = jnp.zeros_like(gg)
        mix_own.wait()
        for k in range(1, S):
            mix_copy(k, lax.rem(s + S - k, S)).wait_recv()

    @pl.when(i == pl.num_programs(0) - 1)
    def _():
        move.relay()

    def unprep(e, u, gain, cosine, sine):
        front, back = e[:half], e[half:]
        e = jnp.concatenate([front * cosine + back * sine, back * cosine - front * sine], axis=0)
        r = lax.rsqrt(jnp.mean(u * u, axis=0, keepdims=True) + EPS)
        ge = gain * e
        du = r * ge - u * (r * r * r * jnp.mean(ge * u, axis=0, keepdims=True))
        return du, jnp.sum(e * u * r, axis=1, keepdims=True)

    for step in range(length // BLOCK):

        @pl.when(i == step)
        def _():
            n = (step + 1) * BLOCK
            here = slice(step * BLOCK, n)
            col = lax.broadcasted_iota(jnp.int32, (n, BLOCK), 0)
            row = step * BLOCK + lax.broadcasted_iota(jnp.int32, (n, BLOCK), 1)
            bias = jnp.where((col <= row) & (row - col <= pos_ref[:, here]), 0.0, -1e30)
            keys, values = k_buf[:n, :], v_buf[:n, :]
            kt = rot_ref[qw : qw + HD, :n]
            per = BLOCK // T
            dmix = dmix_all[step] if per == 1 else jnp.concatenate([dmix_all[step * per + j] for j in range(per)], axis=0)
            dmix_t = dmix.astype(f32).T.astype(bf16)
            qt = rot_ref[:qw, here]
            q = qt.astype(f32).T.astype(bf16)
            cosine, sine = cos_ref[:, here], sin_ref[:, here]
            dqs, gain_sum = [], jnp.zeros((HD, 1), f32)
            dk, dv = jnp.zeros((n, HD), f32), jnp.zeros((n, HD), f32)
            for h in range(heads):
                part = slice(h * HD, (h + 1) * HD)
                p = jnp.exp(dot(keys, qt[part] * 0.125) + bias - lse_ref[h : h + 1, here])
                dv += dot(p.astype(bf16), dmix[:, part])
                dp = dot(values, dmix_t[part])
                inner = jnp.sum(dp * p, axis=0, keepdims=True)
                ds = (p * (dp - inner)).astype(bf16)
                dk += dot(ds, q[:, part])
                dq = (dot(kt, ds) * 0.125).astype(bf16).astype(f32)
                du, dg = unprep(dq, raw_ref[part, here], gq_ref[...], cosine, sine)
                dqs.append(du)
                gain_sum += dg
            dk_acc[:n, :] += dk
            dv_acc[:n, :] += dv
            gg[:, :1] += gain_sum
            dproj[here, :qw] = jnp.concatenate(dqs, axis=0).T.astype(bf16)

    def exchange(k, slot):
        rows = pl.ds(pl.multiple_of(lax.rem(s + k, S) * T, T), T)
        return to_peer(dproj.at[rows], got.at[slot], send.at[k - 1], recv.at[k - 1], k, S)

    @pl.when(i == pl.num_programs(0) - 1)
    def _():
        dk = (dk_acc[...] * 0.125).astype(bf16).astype(f32).T
        du, dg = unprep(dk, raw_ref[qw : qw + HD, :], gk_ref[...], cos_ref[...], sin_ref[...])
        gg[:, 1:2] += dg
        dproj[:, qw:] = jnp.concatenate([du.T, dv_acc[...].astype(bf16).astype(f32)], axis=1).astype(bf16)
        for k in range(1, S):
            exchange(k, s).start()
        W = 128
        rows_d, rows_o = width // (S * F), qw // F
        blocks = hw // W
        n_q, n_o = S * rows_d * blocks, rows_o * width // W
        tile = 512
        for copy in loads:
            copy.wait()
        d_all = dproj[...]
        for c in range(0, width, tile):
            part = dot(normed_t[c : c + tile, :], d_all).astype(bf16)
            for b in range(tile // rows_d):
                j, m = divmod(c // rows_d + b, F)
                for cb in range(blocks):
                    at = (j * blocks + cb) * rows_d
                    packed_ref[m, at : at + rows_d] = part[b * rows_d : (b + 1) * rows_d, cb * W : (cb + 1) * W]
        e = dot_nt(dproj[pl.ds(pl.multiple_of(s * T, T), T), :], wqkv[s])
        for k in range(1, S):
            slot = lax.rem(s + S - k, S)
            exchange(k, slot).wait_recv()
            e += dot_nt(got[slot], wqkv[slot])
        v = x[...].astype(f32)
        r = lax.rsqrt(jnp.mean(v * v, axis=-1, keepdims=True) + EPS)
        ga = jnp.sum(e * v * r, axis=0, keepdims=True)
        ge = gain_row(g_ref, 0) * e
        gin_ref[...] = gm[...] + r * ge - v * (r * r * r * jnp.mean(ge * v, axis=-1, keepdims=True))
        heads_t = gg[...].T
        second = jnp.concatenate([heads_t[0:1], heads_t[1:2]], axis=1)
        gf = ggf_ref[...]
        for j in range(S):
            for m in range(F):
                cut = slice((j * F + m) * rows_d, (j * F + m + 1) * rows_d)
                first = [ga[:, cut], gf[:, cut]]
                if 2 * rows_d < W:
                    first.append(jnp.zeros((1, W - 2 * rows_d), f32))
                rows = jnp.concatenate([jnp.concatenate(first, axis=1), second, jnp.zeros((14, W), f32)], axis=0)
                packed_ref[m, n_q + n_o + 16 * j : n_q + n_o + 16 * (j + 1)] = rows.astype(bf16)
        move.finish(True)
        mix_t = mix_t_ref[...]
        for c in range(0, width, tile):
            part = jnp.zeros((qw, tile), f32)
            for j in range(S):
                part += dot(mix_t[:, j * T : (j + 1) * T], dattn_all[j, :, c : c + tile])
            for m in range(F):
                cuts = [part[m * rows_o : (m + 1) * rows_o, cb * W : (cb + 1) * W] for cb in range(tile // W)]
                at = n_q + c // W * rows_o
                packed_ref[m, at : at + rows_o * tile // W] = jnp.concatenate(cuts, axis=0).astype(bf16)
        for k in range(1, S):
            exchange(k, s).wait_send()
            mix_copy(k, s).wait_send()


def attention_back(S, F, dmix, rot, raw, lse, pos, cosine, sine, gain_q, gain_k, gain, grad_gf, mix_t, x, gm, normed_t, wqkv0, wqkv1, d_attn, heads, collective):
    length = rot.shape[1]
    hw = rot.shape[0]
    T, width = x.shape
    rows_d, rows_o = width // (S * F), heads * HD // F
    total = S * rows_d * hw // 128 + rows_o * width // 128 + 16 * S
    whole = lambda a: pl.BlockSpec(a.shape, lambda i: (0,) * a.ndim)
    return pl.pallas_call(
        functools.partial(attn_back_kernel, S, F, heads),
        grid=(length // BLOCK,),
        in_specs=[whole(a) for a in (rot, raw, lse, pos, cosine, sine, gain_q, gain_k, gain, grad_gf, mix_t)] + [ANY] * 7,
        out_specs=[pl.BlockSpec((F, total, 128), lambda i: (0, 0, 0)), pl.BlockSpec((T, width), lambda i: (0, 0))],
        out_shape=[shape((F, total, 128)), shape((T, width), f32)],
        scratch_shapes=[
            pltpu.VMEM((length, HD), bf16),
            pltpu.VMEM((length, HD), bf16),
            pltpu.VMEM((length, HD), f32),
            pltpu.VMEM((length, HD), f32),
            pltpu.VMEM((HD, 128), f32),
            pltpu.VMEM((length, hw), bf16),
            pltpu.VMEM((S, T, width), bf16),
            pltpu.VMEM((S, T, hw), bf16),
            pltpu.VMEM((T, width), bf16),
            pltpu.VMEM((T, width), f32),
            pltpu.VMEM(normed_t.shape, bf16),
            pltpu.VMEM((S, width, hw), bf16),
            pltpu.VMEM(dmix.shape, bf16),
            DMA((S - 1,)),
            DMA((S - 1,)),
            DMA((6,)),
            DMA((S - 1,)),
            DMA((S - 1,)),
        ]
        + Gather.sems(S, d_attn),
        compiler_params=params(collective, 1),
        cost_estimate=cost(1),
    )(rot, raw, lse, pos, cosine, sine, gain_q, gain_k, gain, grad_gf, mix_t, x, gm, normed_t, wqkv0, wqkv1, d_attn, dmix)


def sum_kernel(S, F, heads, early, hid_ref, wd_ref, mid_ref, gu_hbm, down_hbm, packed_hbm, *refs):
    across = refs[0] if early else None
    refs = refs[early:]
    (
        out_ref, qkv_ref, gout_ref, tiny_ref, down_out, got_hbm, got, gu_send, gu_recv, gu_own, acc, send_buf, recv_buf, packed, twin, pairs, from_z, mine, mine_all,
        send, recv, far, load, twin_send, twin_recv, z_send, z_recv, end_sems,
    ) = refs
    s, f = lax.axis_index("sp"), lax.axis_index("fsdp")
    T, width = mid_ref.shape
    W = 128
    chips = F // 2
    core = lax.rem(f, 2)
    tile = 512

    def exchange(k, slot):
        return to_peer(gu_hbm.at[lax.rem(s + k, S)], got.at[slot], gu_send.at[k - 1], gu_recv.at[k - 1], k, S)

    def twins(n):
        there = 2 * n + 1 - core
        return push(packed_hbm.at[there], twin.at[n], twin_send.at[n], twin_recv.at[n], sibling())

    def over_z(k):
        target = lax.rem(f + 2 * k, F)
        return push(pairs.at[target // 2], from_z.at[k - 1], z_send.at[k - 1], z_recv.at[k - 1], {"fsdp": target})

    fill = pltpu.make_async_copy(packed_hbm, packed, load)
    fill.start()
    own = pltpu.make_async_copy(gu_hbm.at[s], got.at[s], gu_own.at[0])
    own.start()
    back = pltpu.make_async_copy(got, got_hbm, gu_own.at[1])
    owner = hidden_owner(S, s, f)
    far_send = push(down_hbm, down_out, far.at[0], far.at[1], {"sp": owner})
    far_keep = pltpu.make_async_copy(down_hbm, down_out, far.at[0])
    greet(S, F, True)

    @pl.when(owner == s)
    def _():
        far_keep.start()

    for n in range(chips):
        twins(n).start()
    fill.wait()
    for n in range(chips):
        twins(n).wait_recv()
        pairs[n] = (packed[2 * n + core].astype(f32) + twin[n].astype(f32)).astype(bf16)
    for k in range(1, chips):
        over_z(k).start()

    def compute(chunk, out):
        rows = hid_ref[pl.ds(pl.multiple_of(chunk * T, T), T), :]
        for c in range(0, width, tile):
            out[:, c : c + tile] = dot(rows, wd_ref[:, c : c + tile]).astype(out.dtype)
    rows_d = qkv_ref.shape[0]
    rows_o = gout_ref.shape[0]
    qw = heads * HD
    QW, KW = QUERY_HEADS * HD, KV_HEADS * HD
    blocks = (qw + 2 * HD) // W
    n_s = blocks * rows_d
    n_q, n_o = S * n_s, rows_o * width // W

    def rows_of(j):
        return pl.ds(pl.multiple_of(j * n_s, n_s), n_s), pl.ds(pl.multiple_of(n_q + n_o + 16 * j, 16), 16)

    def end(k, slot, part):
        to = (slice(0, n_s), slice(n_s, n_s + 16))[part]
        n = 2 * (k - 1) + part
        src = mine.at[rows_of(lax.rem(s + k, S))[part]]
        return to_peer(src, mine_all.at[slot, to], end_sems.at[0, n], end_sems.at[1, n], k, S)

    def reduce_z():
        for k in range(1, S):
            exchange(k, s).start()

        @pl.when(owner != s)
        def _():
            far_send.start()

        total = pairs[f // 2].astype(f32)
        for k in range(1, chips):
            over_z(k).wait_recv()
            total += from_z[k - 1].astype(f32)
        mine[...] = total.astype(bf16)
        for k in range(1, S):
            for part in range(2):
                end(k, s, part).start()

    copies = sum_over_sp(S, compute, acc, send_buf, recv_buf, send, recv, reduce_z, across)
    out_ref[...] = (mid_ref[...] + acc[...]).astype(bf16)
    main, small = rows_of(s)
    mine_all[s, :n_s] = mine[main, :]
    mine_all[s, n_s:] = mine[small, :]
    for c in range(0, width // W, 2):
        rows = mine[n_q + c * rows_o : n_q + (c + 2) * rows_o, :].astype(f32)
        gout_ref[:, c * W : (c + 1) * W] = rows[:rows_o]
        gout_ref[:, (c + 1) * W : (c + 2) * W] = rows[rows_o:]
    for k in range(1, S):
        for part in range(2):
            end(k, lax.rem(s + S - k, S), part).wait_recv()
    shared = max(1, S // KV_HEADS)
    tiny = jnp.zeros((16, W), f32)
    kvs = []
    for j in range(S):
        for cb in range(blocks - 1):
            at = j * qw + cb * W
            qkv_ref[:, at : at + W] = mine_all[j, cb * rows_d : (cb + 1) * rows_d].astype(f32)
        kv = mine_all[j, (blocks - 1) * rows_d : blocks * rows_d].astype(f32)
        if j % shared:
            kvs[-1] = kvs[-1] + kv
        else:
            kvs.append(kv)
        tiny += mine_all[j, n_s : n_s + 16].astype(f32)
    for h in range(0, KV_HEADS, 2):
        at = QW + h * HD
        qkv_ref[:, at : at + W] = jnp.concatenate([kvs[h][:, :HD], kvs[h + 1][:, :HD]], axis=1)
        qkv_ref[:, at + KW : at + KW + W] = jnp.concatenate([kvs[h][:, HD:], kvs[h + 1][:, HD:]], axis=1)
    tiny_ref[...] = tiny
    own.wait()
    for k in range(1, S):
        exchange(k, lax.rem(s + S - k, S)).wait_recv()
    back.start()
    for k in range(1, S):
        exchange(k, s).wait_send()
    back.wait()
    for copy in copies:
        copy.wait_send()
    for n in range(chips):
        twins(n).wait_send()
    for k in range(1, chips):
        over_z(k).wait_send()
    for k in range(1, S):
        for part in range(2):
            end(k, s, part).wait_send()

    @pl.when(owner == s)
    def _():
        far_keep.wait()

    @pl.when(owner != s)
    def _():
        far_send.wait_send()
        far_send.wait_recv()


def sum_rows(S, F, hidden, w_dn, mid, grad_gu, down, packed, across, rows_d, rows_o, heads, collective):
    T, width = mid.shape
    n = max(6, S - 1)
    chips = F // 2
    part = packed.shape[1:]
    n_s = rows_d * (heads + 2) * HD // 128
    return pl.pallas_call(
        functools.partial(sum_kernel, S, F, heads, len(across)),
        in_specs=[VMEM] * 3 + [ANY] * 3 + [VMEM] * len(across),
        out_specs=[VMEM] * 4 + [ANY] * 2,
        out_shape=[
            shape((T, width)),
            shape((rows_d, (QUERY_HEADS + 2 * KV_HEADS) * HD), f32),
            shape((rows_o, width), f32),
            shape((16, 128), f32),
            shape(down.shape),
            shape(grad_gu.shape),
        ],
        scratch_shapes=[
            pltpu.VMEM(grad_gu.shape, bf16),
            DMA((S - 1,)),
            DMA((S - 1,)),
            DMA((2,)),
            pltpu.VMEM((T, width), f32),
            pltpu.VMEM((S - 1, T, width), bf16),
            pltpu.VMEM((S - 1, T, width), bf16),
            pltpu.VMEM(packed.shape, bf16),
            pltpu.VMEM((chips,) + part, bf16),
            pltpu.VMEM((chips,) + part, bf16),
            pltpu.VMEM((chips - 1,) + part, bf16),
            pltpu.VMEM(part, bf16),
            pltpu.VMEM((S, n_s + 16, 128), bf16),
            DMA((n,)),
            DMA((n,)),
            DMA((2,)),
            DMA,
            DMA((chips,)),
            DMA((chips,)),
            DMA((chips - 1,)),
            DMA((chips - 1,)),
            DMA((2, 2 * (S - 1))),
        ],
        compiler_params=params(collective),
        cost_estimate=cost(40),
    )(hidden, w_dn, mid, grad_gu, down, packed, *across)


def write_kernel(S, F, kept, *refs):
    ins, refs = refs[: kept + 2], refs[kept + 2 :]
    outs, refs = refs[: kept + 3], refs[kept + 3 :]
    stages, wide, sem_in, sem_out = refs[: kept + 2], refs[kept + 2 : kept + 5], refs[-2], refs[-1]
    loads = [pltpu.make_async_copy(ins[n], stages[n], sem_in.at[n]) for n in range(kept + 2)]
    for copy in loads:
        copy.start()
    stores = []

    def store(n, src):
        stores.append(pltpu.make_async_copy(src, outs[n], sem_out.at[n]))
        stores[-1].start()

    for n in range(kept):
        loads[n].wait()
        store(n, stages[n])
    loads[kept + 1].wait()
    got = stages[kept + 1]
    piece = got.shape[3] // F
    for n in range(2):
        for j in range(S):
            for m in range(F):
                at = (m * S + hidden_block(S, j, m // 2)) * piece
                wide[1 + n][:, at : at + piece] = got[j, n, :, m * piece : (m + 1) * piece].astype(f32)
        store(kept + 1 + n, wide[1 + n])
    loads[kept].wait()
    wide[0][...] = stages[kept][...].astype(f32)
    store(kept, wide[0])
    for copy in stores:
        copy.wait()


def write_outputs(S, F, kept, down, got):
    _, _, rows_d, FFs = got.shape
    wide = [shape(down.shape, f32)] + [shape((rows_d, FFs * S), f32)] * 2
    if FFs // F % 128:
        parts = got.reshape(S, 2, rows_d, F, FFs // F)
        parts = [parts[(t - m // 2) % S, :, :, m] for m in range(F) for t in range(S)]
        grad = jnp.concatenate(parts, axis=2).astype(f32)
        return list(kept) + [down.astype(f32), grad[0], grad[1]]
    outs = [shape(a.shape, a.dtype) for a in kept] + wide
    ins = list(kept) + [down, got]
    return pl.pallas_call(
        functools.partial(write_kernel, S, F, len(kept)),
        in_specs=[ANY] * len(ins),
        out_specs=[ANY] * len(outs),
        out_shape=outs,
        scratch_shapes=[pltpu.VMEM(a.shape, a.dtype) for a in ins]
        + [pltpu.VMEM(a.shape, f32) for a in wide]
        + [DMA((len(ins),)), DMA((len(outs),))],
        compiler_params=params(),
        cost_estimate=cost(5),
    )(*ins)


def ordered(value, *after):
    return lax.optimization_barrier((value,) + after)[0]


def local(x_own, positions, ct_own, w_qkv, w_out, w_gate, w_up, w_down, gain_attn, gain_ffn, gain_query, gain_key):
    S, F = lax.axis_size("sp"), lax.axis_size("fsdp")
    assert F == 2 * S
    s, f = lax.axis_index("sp"), lax.axis_index("fsdp")
    _, T, D = x_own.shape
    L = positions.shape[1]
    heads = QUERY_HEADS // S
    qw = heads * HD
    hw = qw + 2 * HD
    FFs = w_gate.shape[1] // S
    rows_d = D // (S * F)
    rows_o = qw // F
    x_own = x_own[0]
    ct_own = ct_own[0]

    def gather_z(w):
        return lax.all_gather(w, "fsdp", axis=0, tiled=True)

    def reduce_z(w):
        return lax.psum_scatter(w, "fsdp", scatter_dimension=0, tiled=True)

    gu_part = own_columns(S, F, s, w_gate, w_up)
    w_gu = gather_z(gu_part).reshape(F, 2, D // F, FFs)
    rows_w = w_down.shape[0] // S

    x_all, ct_a, wqkv_s, gains, cosine, sine = first_gathers(
        S, F, x_own, ct_own, ordered(w_qkv, gu_part), gain_attn[None], gain_ffn[None], positions, heads, 0
    )
    w_down, gain_query, gain_key, _ = lax.optimization_barrier((w_down, gain_query, gain_key, x_all))
    w_dn = gather_z(lax.dynamic_slice_in_dim(w_down, hidden_block(S, s, f // 2) * rows_w, rows_w, 0))
    x_all = x_all.reshape(L, D)
    wqkv_s = wqkv_s.reshape(D, hw)
    gain_q = gain_query.astype(f32)[:, None]
    gain_k = gain_key.astype(f32)[:, None]
    normed_t, raw, rot, lse, mix_t, mix_all, wout_all, ct0 = forward_attention(
        S, F, x_all, gains, wqkv_s, positions, cosine, sine, gain_q, gain_k, w_out, ct_own, heads, 1
    )
    wout_all = wout_all.reshape(S, qw, D)
    cts = [ct_a.reshape(L, D // 4), ct0.reshape(L, D // 4)]
    mid, ffn_in, ffn_t, ct1 = middle_rows(S, x_all, mix_all, wout_all, gains, ct_own, 2)
    cts.append(ct1.reshape(L, D // 2))
    gate, up, hidden, part_down, wqkv0 = ffn_forward(S, ffn_in, cts, w_gu, wqkv_s, 3)
    grad_down = reduce_z(part_down.reshape(FFs, D))
    dgu, part_gu, wqkv1, *across = ffn_backward(S, F, cts, w_dn, gate, up, ffn_t, wqkv_s, hidden, 4)
    grad_gu = reduce_z(part_gu.reshape(2 * D, FFs))
    gm, d_attn, grad_gf, d_mix = middle_back(S, dgu, w_gu, wout_all, mid, gains, ct_own, 5)
    packed, grad_input = attention_back(
        S, F, ordered(d_mix, grad_down), rot, raw, lse, positions, cosine, sine, gain_q, gain_k,
        gains, grad_gf, mix_t, x_own, gm, normed_t, wqkv0, wqkv1, d_attn, heads, 6,
    )
    out, grad_qkv, grad_out, tiny, grad_down, got = sum_rows(
        S, F, hidden, w_dn, mid, grad_gu.reshape(S, 2, rows_d, FFs), grad_down, packed, across, rows_d, rows_o, heads, 7
    )
    grad_input, out, grad_qkv, grad_out, grad_down, grad_gate, grad_up = write_outputs(
        S, F, (grad_input, out, grad_qkv, grad_out), grad_down, got
    )
    return (
        out[None],
        grad_input[None],
        grad_qkv,
        grad_out,
        grad_gate,
        grad_up,
        grad_down,
        tiny[0, :rows_d],
        tiny[0, rows_d : 2 * rows_d],
        tiny[1, :HD],
        tiny[1, HD:],
    )


def solution(mesh):
    row = P("fsdp", "sp", None)
    shard = P("fsdp", None)
    grad = P(("sp", "fsdp"), None)
    return jax.shard_map(
        local,
        mesh=mesh,
        in_specs=(row, shard, row, shard, shard, shard, shard, shard, P("fsdp"), P("fsdp"), P(), P()),
        out_specs=(row, row, grad, grad, grad, grad, grad, P(("sp", "fsdp")), P(("sp", "fsdp")), P(), P()),
        check_vma=False,
    )
```
